512 devices in a mesh: gx: 64 (over z, x_lo, core), gy: 8 (over y, x_hi).
Axes of the slice: x: 4 (x_hi: 2, x_lo: 2; x = x_hi * 2 + x_lo), y: 4, z: 16, core: 2. Of those that a mesh axis runs over, the one named last changes fastest.
Arguments:
- positions: float32 [3, 262144], P(None, ('gx', 'gy')), may hold values from 0 to 1
- velocities: float32 [3, 262144], P(None, ('gx', 'gy')), may hold values from -4 to 4
- forces: float32 [3, 262144], P(None, ('gx', 'gy')), may hold values from -6 to 6
- neighbours: int32 [1, 32, 262144], P(None, None, ('gx', 'gy')), may hold values from -1 to 1151, as said below
- ghost_x: int32 [1, 2, 65536], P(None, None, ('gx', 'gy')), may hold values from 0 to 511, as said below
- ghost_y: int32 [1, 2, 98304], P(None, None, ('gx', 'gy')), may hold values from 0 to 767, as said below
- migrate_x: int32 [1, 2, 4096], P(None, None, ('gx', 'gy')), may hold values from 0 to 511, as said below
- migrate_y: int32 [1, 2, 4096], P(None, None, ('gx', 'gy')), may hold values from 0 to 511, as said below
- w_basis: float32 [64, 8], replicated, may hold values from -2 to 2
- b_basis: float32 [64], replicated, may hold values from -3 to 3
- w_embed: float32 [32, 64], replicated, may hold values from -0.75 to 0.75
- w_pair: float32 [64, 64], replicated, may hold values from -0.75 to 0.75
- w_mix: float32 [64, 32], replicated, may hold values from -1 to 1
- b_pair: float32 [64], replicated, may hold values from -3 to 3
- w_out: float32 [64], replicated, may hold values from -0.75 to 0.75
Outputs:
- positions_out: float32 [3, 262144], P(None, ('gx', 'gy'))
- velocities_out: float32 [3, 262144], P(None, ('gx', 'gy'))
- forces_out: float32 [3, 262144], P(None, ('gx', 'gy'))
The draws below stay inside these ranges and needn't reach their ends.
Inputs may be any that keep to these rules, and one draw needn't show every extreme that they name: `neighbours`: entries index the step's extended columns of the bin (own slots, then 128 ghosts from the lower and 128 from the upper gx neighbour, then 192 from the lower and 192 from the upper gy neighbour); -1 marks an empty slot. In every bin the atoms with a non-empty list (live atoms) fill the first whole blocks of 128 slots, at least 3 blocks, and all 4 in some bin; other atoms have only -1 and no list names them. Every list names ghosts or live atoms only. `ghost_x`: for each step and each of the two rows, 128 distinct live slots of the bin. `ghost_y`: for each step and each of the two rows, 192 distinct columns of the bin's own live atoms and gx ghosts. `migrate_x`: for each step the 16 slots of a bin are distinct and live. `migrate_y`: for each step the 16 slots of a bin are distinct and live.
All inputs are finite; a program needn't handle non-finite values.
Results may differ from the reference program's by a relative error of at most 0.0003.
Values sent between devices are 32-bit elements; how exact they have to be, the bound alone decides.
No kernel may reach another device: no remote copies, remote signals or barrier semaphores. Data moves between devices by JAX's collectives and lax.ppermute only.
A program may use at most 64 MiB of HBM per device.

```python
import math
import jax
import jax.numpy as jnp
from jax import lax

H = 64
NB = 8
EMB = 32
NEI = 32
BLOCK = 128
BLK = 4
MIG = 8
STEPS = 1
ATOMS_DEV = 512
GX = 128
GY = 192
ATOMS = 262144
N_GX = 64
N_GY = 8


def live_blocks(key):
    devices = N_GX * N_GY
    counts = jax.random.randint(jax.random.fold_in(key, 101), (devices,), 3 * BLK // 4, BLK + 1)
    fullest = jax.random.randint(jax.random.fold_in(key, 102), (), 0, devices)
    return jnp.where(jnp.arange(devices) == fullest, BLK, counts).astype(jnp.int32)


def distinct_slots(key, allowed, pick_count):
    width_all = allowed.shape[1]
    column_index = jnp.arange(width_all)[None, :]
    scores = jax.random.randint(key, allowed.shape, 0, 1 << 15)
    ranked = (scores + jnp.where(allowed, 0, 1 << 15)) * width_all + column_index
    last_allowed = jnp.max(jnp.where(allowed, column_index, -1), axis=1)
    ranked = jnp.where(column_index == last_allowed[:, None], -1, ranked)
    return jnp.argsort(ranked, axis=1)[:, :pick_count].astype(jnp.int32)


def side_lists(key, allowed, pick_count, salt):
    devices = allowed.shape[0]
    row_list = []
    for moment in range(STEPS):
        for side_index in range(2):
            chosen = distinct_slots(jax.random.fold_in(key, salt + 2 * moment + side_index), allowed, pick_count)
            row_list.append(chosen.reshape(-1))
    return jnp.stack(row_list).reshape(STEPS, 2, devices * pick_count).astype(jnp.int32)


def draw_ghost_x(key, part):
    local_count = live_blocks(key) * BLOCK
    allowed = jnp.arange(ATOMS_DEV)[None, :] < local_count[:, None]
    return side_lists(key, allowed, GX, 200)


def draw_ghost_y(key, part):
    local_count = live_blocks(key) * BLOCK
    slot_index = jnp.arange(ATOMS_DEV + 2 * GX)[None, :]
    allowed = (slot_index < local_count[:, None]) | (slot_index >= ATOMS_DEV)
    return side_lists(key, allowed, GY, 300)


def migration_lists(key, salt):
    devices = N_GX * N_GY
    local_count = live_blocks(key) * BLOCK
    allowed = jnp.arange(ATOMS_DEV)[None, :] < local_count[:, None]
    row_list = []
    for moment in range(STEPS):
        chosen = distinct_slots(jax.random.fold_in(key, salt + moment), allowed, 2 * MIG)
        row_list.append(chosen[:, :MIG].reshape(-1))
        row_list.append(chosen[:, MIG:].reshape(-1))
    return jnp.stack(row_list).reshape(STEPS, 2, devices * MIG).astype(jnp.int32)


def draw_migrate_x(key, part):
    return migration_lists(key, 400)


def draw_migrate_y(key, part):
    return migration_lists(key, 500)


def draw_neighbours(key, part):
    devices = N_GX * N_GY
    local_count = live_blocks(key) * BLOCK
    span_size = local_count + 2 * GX + 2 * GY
    slot_index = jnp.arange(ATOMS_DEV)
    is_live = slot_index[None, None, :] < local_count[:, None, None]
    first_slot = (jnp.arange(NEI) == 0)[None, :, None]
    step_list = []
    for moment in range(STEPS):
        raw_draw = jax.random.randint(jax.random.fold_in(key, 600 + moment), (devices, NEI, ATOMS_DEV), 0, 1 << 24)
        drawn_slot = raw_draw % span_size[:, None, None]
        neighbour = jnp.where(drawn_slot < local_count[:, None, None], drawn_slot, drawn_slot - local_count[:, None, None] + ATOMS_DEV)
        kept = jax.random.randint(jax.random.fold_in(key, 700 + moment), (devices, NEI, ATOMS_DEV), 0, 8) < 7
        kept = kept | first_slot
        neighbour = jnp.where(kept & is_live, neighbour, -1)
        step_list.append(jnp.transpose(neighbour, (1, 0, 2)).reshape(NEI, devices * ATOMS_DEV))
    return jnp.stack(step_list).astype(jnp.int32)


def block_levels(key, extent, split, low, largest):
    level = 1.0
    for dim, shards_of in split:
        steps = jax.random.uniform(jax.random.fold_in(jax.random.fold_in(key, 6), dim), (shards_of,), jnp.float32, low / len(split), largest / len(split))
        level = level * jnp.repeat(jnp.exp(steps), extent[dim] // shards_of).reshape((-1,) + (1,) * (len(extent) - 1 - dim))
    return level


def centred(own_key, shape, spread, most, cuts=(), kind=jnp.bfloat16):
    array = jax.random.normal(own_key, shape, jnp.float32) * spread
    if len(cuts) > 0:
        array = block_levels(own_key, shape, cuts, -0.22, 0.18) * array
    return jnp.clip(array, min=-most, max=most).astype(kind)


def setup_inputs(seed: int = 0) -> dict:
    seeds = jax.random.split(jax.random.key(seed), 16)
    positions = jnp.clip(1.0 * jax.random.uniform(seeds[0], (3, ATOMS), jnp.float32) ** block_levels(seeds[0], (3, ATOMS), ((1, 512),), -0.2, 0.2), 0.0, 1.0)
    velocities = centred(seeds[1], (3, ATOMS), 1.0, 4.0, ((1, 512),), jnp.float32)
    forces = centred(seeds[2], (3, ATOMS), 1.0, 6.0, ((1, 512),), jnp.float32)
    neighbours = draw_neighbours(jax.random.fold_in(seeds[15], 71), 0)
    ghost_x = draw_ghost_x(jax.random.fold_in(seeds[15], 71), 0)
    ghost_y = draw_ghost_y(jax.random.fold_in(seeds[15], 71), 0)
    migrate_x = draw_migrate_x(jax.random.fold_in(seeds[15], 71), 0)
    migrate_y = draw_migrate_y(jax.random.fold_in(seeds[15], 71), 0)
    w_basis = centred(seeds[8], (H, NB), NB ** -0.5, 2.0, (), jnp.float32)
    b_basis = centred(seeds[9], (H,), 0.5, 3.0, (), jnp.float32)
    w_embed = centred(seeds[10], (EMB, H), H ** -0.5, 0.75, (), jnp.float32)
    w_pair = centred(seeds[11], (H, H), H ** -0.5, 0.75, (), jnp.float32)
    w_mix = centred(seeds[12], (H, EMB), EMB ** -0.5, 1.0, (), jnp.float32)
    b_pair = centred(seeds[13], (H,), 0.5, 3.0, (), jnp.float32)
    w_out = centred(seeds[14], (H,), H ** -0.5, 0.75, (), jnp.float32)
    return dict(positions=positions, velocities=velocities, forces=forces, neighbours=neighbours, ghost_x=ghost_x, ghost_y=ghost_y, migrate_x=migrate_x, migrate_y=migrate_y, w_basis=w_basis, b_basis=b_basis, w_embed=w_embed, w_pair=w_pair, w_mix=w_mix, b_pair=b_pair, w_out=w_out)


TIME_STEP = 0.05
CENTRE_SPAN = 3.0
HIGHEST = lax.Precision.HIGHEST

def matmul(left, right):
    return jnp.dot(left, right, precision=HIGHEST, preferred_element_type=jnp.float32)

def pair_latent(ext_pos, own_pos, nearby, w_basis, b_basis):
    present = nearby >= 0
    safe_index = jnp.where(present, nearby, 0)
    separation = ext_pos[:, safe_index] - own_pos[:, None, :]
    square = lax.optimization_barrier(jnp.sum(separation * separation, axis=0))
    weight = jnp.where(present, 1.0 / (1.0 + square), 0.0)
    centres = jnp.arange(NB, dtype=jnp.float32) * (CENTRE_SPAN / (NB - 1))
    radial = jnp.exp(-(square[None] - centres[:, None, None]) ** 2)
    latent = jax.nn.silu(matmul(w_basis, radial.reshape(NB, -1)) + b_basis[:, None])
    return (latent * weight.reshape(1, -1), weight, safe_index)

def pair_env(ext_pos, own_pos, nearby, w_basis, b_basis):
    latent, weight, safe_index = pair_latent(ext_pos, own_pos, nearby, w_basis, b_basis)
    summed = latent.reshape(latent.shape[0], nearby.shape[0], nearby.shape[1]).sum(axis=1)
    return summed * (1.0 / math.sqrt(NEI))

def pair_energy(ext_pos, own_pos, nearby, embed_ext, embed_own, weights):
    w_basis, b_basis, w_pair, w_mix, b_pair, w_out = weights
    latent, weight, safe_index = pair_latent(ext_pos, own_pos, nearby, w_basis, b_basis)
    partner = embed_ext[:, safe_index]
    product = (partner * embed_own[:, None, :]).reshape(embed_own.shape[0], -1)
    hidden = jax.nn.silu(matmul(w_pair, latent) + matmul(w_mix, product) + b_pair[:, None])
    return jnp.sum(matmul(w_out, hidden) * weight.reshape(-1))

def grid_roll(values, step_long, step_narrow):
    leading = values.shape[:-2]
    grid_view = values.reshape(leading + (N_GX, N_GY, values.shape[-1]))
    grid_view = jnp.roll(grid_view, step_long, axis=len(leading))
    grid_view = jnp.roll(grid_view, step_narrow, axis=len(leading) + 1)
    return grid_view.reshape(values.shape)

def take_columns(values, columns):
    return values[:, columns]

def pick_columns(values, columns):
    return jax.vmap(take_columns, in_axes=(1, 0), out_axes=1)(values, columns)

def put_columns(values, columns, update):
    return values.at[:, columns].set(update)

def place_columns(values, columns, update):
    return jax.vmap(put_columns, in_axes=(1, 0, 1), out_axes=1)(values, columns, update)

def unit_column(channels, component):
    return jnp.zeros((channels, 1, 1), jnp.float32).at[component, 0, 0].set(1.0)

def migrate(bundle, slot_lists, component, step_long, step_narrow):
    offset = unit_column(bundle.shape[0], component)
    upward = pick_columns(bundle, slot_lists[0]) - offset
    downward = pick_columns(bundle, slot_lists[1]) + offset
    bundle = place_columns(bundle, slot_lists[1], grid_roll(upward, step_long, step_narrow))
    return place_columns(bundle, slot_lists[0], grid_roll(downward, -step_long, -step_narrow))

def extend(values, list_long, list_narrow, offset_long, offset_narrow):
    upward = pick_columns(values, list_long[0]) - offset_long
    downward = pick_columns(values, list_long[1]) + offset_long
    partial_value = jnp.concatenate([values, grid_roll(upward, 1, 0), grid_roll(downward, -1, 0)], axis=2)
    upward = pick_columns(partial_value, list_narrow[0]) - offset_narrow
    downward = pick_columns(partial_value, list_narrow[1]) + offset_narrow
    return jnp.concatenate([partial_value, grid_roll(upward, 0, 1), grid_roll(downward, 0, -1)], axis=2)

def total_energy(position, nearby, list_long, list_narrow, weights):
    w_basis, b_basis, w_embed, w_pair, w_mix, b_pair, w_out = weights
    extended = extend(position, list_long, list_narrow, unit_column(3, 0), unit_column(3, 1))
    ext_device = jnp.moveaxis(extended, 1, 0)
    own_device = jnp.moveaxis(position, 1, 0)

    def env_item(device_items):
        return pair_env(device_items[0], device_items[1], device_items[2], w_basis, b_basis)
    environ = lax.map(jax.checkpoint(env_item), (ext_device, own_device, nearby))
    embed = jnp.einsum('eh,dha->eda', w_embed, environ, precision=HIGHEST)
    no_shift = jnp.zeros((embed.shape[0], 1, 1), jnp.float32)
    embed_ext = extend(embed, list_long, list_narrow, no_shift, no_shift)
    pair_weights = (w_basis, b_basis, w_pair, w_mix, b_pair, w_out)

    def energy_item(device_items):
        return pair_energy(device_items[0], device_items[1], device_items[2], device_items[3], device_items[4], pair_weights)
    energies = lax.map(jax.checkpoint(energy_item), (ext_device, own_device, nearby, jnp.moveaxis(embed_ext, 1, 0), jnp.moveaxis(embed, 1, 0)))
    return jnp.sum(energies)

def reference(positions, velocities, forces, neighbours, ghost_x, ghost_y, migrate_x, migrate_y, w_basis, b_basis, w_embed, w_pair, w_mix, b_pair, w_out):
    devices = N_GX * N_GY
    weights = (w_basis, b_basis, w_embed, w_pair, w_mix, b_pair, w_out)
    position = positions.reshape(3, devices, ATOMS_DEV)
    velocity = velocities.reshape(3, devices, ATOMS_DEV)
    forcing = forces.reshape(3, devices, ATOMS_DEV)
    energy_grad = jax.grad(total_energy)
    for moment in range(STEPS):
        velocity = velocity + 0.5 * TIME_STEP * forcing
        position = position + TIME_STEP * velocity
        bundle = jnp.concatenate([position, velocity], axis=0)
        bundle = migrate(bundle, migrate_x[moment].reshape(2, devices, MIG), 0, 1, 0)
        bundle = migrate(bundle, migrate_y[moment].reshape(2, devices, MIG), 1, 0, 1)
        position = bundle[:3]
        velocity = bundle[3:]
        nearby = jnp.transpose(neighbours[moment].reshape(NEI, devices, ATOMS_DEV), (1, 0, 2))
        list_long = ghost_x[moment].reshape(2, devices, GX)
        list_narrow = ghost_y[moment].reshape(2, devices, GY)
        forcing = -energy_grad(position, nearby, list_long, list_narrow, weights)
        velocity = velocity + 0.5 * TIME_STEP * forcing
    return (position.reshape(3, -1), velocity.reshape(3, -1), forcing.reshape(3, -1))
```

```python
import math

import jax
import jax.numpy as jnp
from jax import lax
from jax.experimental import pallas as pl
from jax.experimental.pallas import tpu as pltpu
from jax.sharding import PartitionSpec as P

F32 = jnp.float32
BF16 = jnp.bfloat16
I32 = jnp.int32

TIME_STEP = 0.05
CENTRE_SPAN = 3.0
HIGHEST = lax.Precision.HIGHEST

NB = 8
NEI = 32
H = 64
EMB = 32
OWN = 512
GX = 128
GY = 192
MIG = 8
LANES = 128
INNER = OWN + 2 * GX
EXT = INNER + 2 * GY
GROUPS = EXT // LANES
HALF = 256
LEVELS = -(-EXT // HALF)
BIG = 48 * 1024 * 1024


def half_split(value):
    high = value.astype(BF16)
    low = (value - high.astype(F32)).astype(BF16)
    return high, low


def third_split(value):
    high = value.astype(BF16)
    rest = value - high.astype(F32)
    middle = rest.astype(BF16)
    low = (rest - middle.astype(F32)).astype(BF16)
    return high, middle, low


def lane_take(table, index):
    return jnp.take_along_axis(table, index, axis=1, mode="promise_in_bounds")


def take_lanes(read, rows, groups, index_row):
    low = jnp.broadcast_to(index_row & (LANES - 1), (8, LANES))
    high = jnp.broadcast_to(index_row >> 7, (8, LANES))
    pieces = []
    for r in range(rows // 8):
        taken = jnp.zeros((8, LANES), F32)
        for g in range(groups):
            taken = jnp.where(high == g, lane_take(read(r, g), low), taken)
        pieces.append(taken)
    return jnp.concatenate(pieces, axis=0) if len(pieces) > 1 else pieces[0]


def tile_reader(ref):
    return lambda r, g: ref[8 * r : 8 * r + 8, LANES * g : LANES * (g + 1)]


def spread(values, lists, width):
    count = values.shape[1]
    hot = jnp.where(lax.broadcasted_iota(I32, (width, count), 0) == lists, 1.0, 0.0).astype(BF16)
    total = None
    for part in third_split(values):
        piece = lax.dot_general(part, hot, (((1,), (1,)), ((), ())), preferred_element_type=F32)
        total = piece if total is None else total + piece
    return total


def by_parity(parity, even, odd):
    return jnp.where(parity == 0, even, odd)


def unit_row(rows, row, amount):
    return jnp.where(lax.broadcasted_iota(I32, (rows, 1), 0) == row, amount, 0.0)


def place(bundle, slots, message):
    lane = lax.broadcasted_iota(I32, bundle.shape, 1)
    for k in range(MIG):
        bundle = jnp.where(lane == slots[:, k : k + 1], message[:, k : k + 1], bundle)
    return bundle


def take_migrants(scratch, lists, row, first, second):
    pair = []
    for chosen, shift in (first, second):
        pair.append(take_lanes(tile_reader(scratch), 8, OWN // LANES, chosen) + unit_row(8, row, shift))
    return pair


def prepare_kernel(
    par, basis_t, pair, mix_t, w_embed, b_basis, b_pair, w_out, basis, ahead, back, w_back, columns
):
    high, low = half_split(basis_t[...])
    high, low = high.astype(F32), low.astype(F32)
    parts = [part.astype(F32) for part in third_split(b_basis[...])]
    parts = jnp.concatenate(parts + [jnp.zeros((NB - 3, H), F32)], axis=0)
    basis[...] = jnp.concatenate([high, high, low, parts], axis=0).T.astype(BF16)
    rows = jnp.concatenate([b_pair[...], w_out[...], jnp.zeros((NB - 2, H), F32)], axis=0)
    columns[...] = rows.T
    w_back[...] = w_embed[...].T
    layer_t = jnp.concatenate([pair[...].T, mix_t[...]], axis=0)
    high, low = half_split(layer_t)
    high, low = high.astype(F32), low.astype(F32)
    nothing = jnp.zeros((H + EMB, H), F32)
    back[...] = jnp.concatenate(
        [jnp.concatenate([high, high], axis=1), jnp.concatenate([low, nothing], axis=1)], axis=0
    ).astype(BF16)
    ahead[0:H, :] = jnp.concatenate([high, high], axis=0).T.astype(BF16)
    ahead[H : 2 * H, :] = jnp.concatenate([low, nothing], axis=0).T.astype(BF16)


def start_kernel(par, pos, vel, frc, mx, bundle_out, one, two):
    speeds = vel[...] + (0.5 * TIME_STEP) * frc[...]
    coords = pos[...] + TIME_STEP * speeds
    bundle_out[0:3, :] = coords
    bundle_out[3:6, :] = speeds
    bundle_out[6:8, :] = jnp.zeros((2, OWN), F32)
    p = par[0]
    first = (by_parity(p, mx[0:1, :], mx[1:2, :]), by_parity(p, -1.0, 1.0))
    second = (by_parity(p, mx[1:2, :], mx[0:1, :]), by_parity(p, 1.0, -1.0))
    one[...], two[...] = take_migrants(bundle_out, mx, 0, first, second)


def arrive(bundle, par, p_index, lists, one, two):
    p = par[p_index]
    from_lower = by_parity(p, two[...], one[...])
    from_upper = by_parity(p, one[...], two[...])
    bundle = place(bundle, lists[1:2, :], from_lower)
    return place(bundle, lists[0:1, :], from_upper)


def cross_kernel(par, bundle, one_in, two_in, mx, my, bundle_out, one, two):
    bundle_out[...] = arrive(bundle[...], par, 0, mx, one_in, two_in)
    p = par[1]
    first = (by_parity(p, my[0:1, :], my[1:2, :]), by_parity(p, -1.0, 1.0))
    second = (by_parity(p, my[1:2, :], my[0:1, :]), by_parity(p, 1.0, -1.0))
    one[...], two[...] = take_migrants(bundle_out, my, 1, first, second)


def settle_kernel(par, bundle, one_in, two_in, my, gx, bundle_out, one, two):
    bundle_out[...] = arrive(bundle[...], par, 1, my, one_in, two_in)
    p = par[0]
    first = (by_parity(p, gx[0:1, :], gx[1:2, :]), by_parity(p, -1.0, 1.0))
    second = (by_parity(p, gx[1:2, :], gx[0:1, :]), by_parity(p, 1.0, -1.0))
    one[...], two[...] = take_migrants(bundle_out, gx, 0, first, second)


def narrow_messages(par, table, rows, gy, row, one, two):
    p = par[1]
    for out, chosen, shift in (
        (one, by_parity(p, gy[0:1, :], gy[1:2, :]), by_parity(p, -1.0, 1.0)),
        (two, by_parity(p, gy[1:2, :], gy[0:1, :]), by_parity(p, 1.0, -1.0)),
    ):
        for c in range(2):
            taken = take_lanes(tile_reader(table), rows, INNER // LANES, chosen[:, LANES * c : LANES * (c + 1)])
            if row is not None:
                taken = taken + unit_row(rows, row, shift)
            out[:, LANES * c : LANES * (c + 1)] = taken


def inner_table(par, own, one, two, table):
    p = par[0]
    table[:, 0:OWN] = own
    table[:, OWN : OWN + GX] = by_parity(p, two[...], one[...])
    table[:, OWN + GX : INNER] = by_parity(p, one[...], two[...])


def outer_table(par, one, two, table):
    p = par[1]
    table[:, INNER : INNER + GY] = by_parity(p, two[:, 0:GY], one[:, 0:GY])
    table[:, INNER + GY : EXT] = by_parity(p, one[:, 0:GY], two[:, 0:GY])


def ghost_kernel(shift_row, par, own, one_in, two_in, gy, one, two, table):
    inner_table(par, own[...], one_in, two_in, table)
    narrow_messages(par, table, own.shape[0], gy, shift_row, one, two)


def env_kernel(
    par, own, gx1, gx2, gy1, gy2, nbr, basis, w_embed, gx,
    embed, one, two, lat_high, lat_low, slope, geo, table, square,
):
    inner_table(par, own[...], gx1, gx2, table)
    outer_table(par, gy1, gy2, table)
    for b in range(OWN // LANES):
        lanes = slice(LANES * b, LANES * (b + 1))
        for q in range(NEI // 8):
            rows = slice(8 * q, 8 * q + 8)
            index = nbr[rows, lanes]
            low = index & (LANES - 1)
            high = index >> 7
            total = jnp.zeros((8, LANES), F32)
            for c in range(3):
                taken = jnp.zeros((8, LANES), F32)
                for g in range(GROUPS):
                    tile = jnp.broadcast_to(table[c : c + 1, LANES * g : LANES * (g + 1)], (8, LANES))
                    taken = jnp.where(high == g, lane_take(tile, low), taken)
                apart = taken - own[c : c + 1, lanes]
                geo[c, rows, lanes] = apart
                total = total + apart * apart
            square[rows, lanes] = total
            geo[3, rows, lanes] = jnp.where(index >= 0, 1.0 / (1.0 + total), 0.0)

    centre = lax.broadcasted_iota(I32, (NB, 1), 0).astype(F32) * (CENTRE_SPAN / (NB - 1))
    ones = jnp.ones((NB, HALF), F32)
    left = basis[...]
    for half in range(OWN // HALF):
        lanes = slice(HALF * half, HALF * (half + 1))

        def turn(n, gathered):
            offset = square[pl.ds(n, 1), lanes] - centre
            weight = geo[3, pl.ds(n, 1), lanes]
            radial = jnp.exp(-(offset * offset))
            falling = -2.0 * offset * radial
            radial_high = radial.astype(BF16).astype(F32)
            falling_high = falling.astype(BF16).astype(F32)
            right = jnp.concatenate(
                [
                    jnp.concatenate([radial_high, radial - radial_high, radial_high, ones], axis=0),
                    jnp.concatenate([falling_high, falling - falling_high, falling_high, 0.0 * ones], axis=0),
                ],
                axis=1,
            ).astype(BF16)
            both = lax.dot_general(left, right, (((1,), (0,)), ((), ())), preferred_element_type=F32)
            value = both[:, :HALF]
            rate = both[:, HALF:]
            gate = 0.5 * jnp.tanh(0.5 * value) + 0.5
            raw = value * gate
            latent = raw * weight
            slope[n, :, lanes] = weight * ((gate + raw * (1.0 - gate)) * rate - latent)
            high, low = half_split(latent)
            lat_high[n, :, lanes] = high
            lat_low[n, :, lanes] = low
            return gathered + latent

        gathered = lax.fori_loop(0, NEI, turn, jnp.zeros((H, HALF), F32))
        environ = gathered * (1.0 / math.sqrt(NEI))
        embed[:, lanes] = jnp.dot(w_embed[...], environ, precision=HIGHEST, preferred_element_type=F32)
    p = par[0]
    reader = tile_reader(embed)
    one[...] = take_lanes(reader, EMB, OWN // LANES, by_parity(p, gx[0:1, :], gx[1:2, :]))
    two[...] = take_lanes(reader, EMB, OWN // LANES, by_parity(p, gx[1:2, :], gx[0:1, :]))


def hot_rows(low_row, count):
    level = lax.broadcasted_iota(I32, (HALF, count), 0)
    return jnp.where(level == low_row, 1.0, 0.0).astype(BF16)


def level_rows(value, high_row):
    pieces = []
    for k in range(LEVELS):
        mask = jnp.where(high_row == k, 1.0, 0.0).astype(BF16)
        pieces.append(value * mask)
    return jnp.concatenate(pieces, axis=0)


def pair_kernel(
    par, own, gx1, gx2, gy1, gy2, nbr, lat_high, lat_low, slope, geo, ahead, back, columns,
    rise, inner, one, two, table, spread_sum, own_sum, joined,
):
    inner_table(par, own[...], gx1, gx2, table)
    outer_table(par, gy1, gy2, table)
    spread_sum[...] = jnp.zeros(spread_sum.shape, F32)
    own_sum[...] = jnp.zeros(own_sum.shape, F32)
    left = ahead[...]
    right_back = back[...]
    bias = columns[:, 0:1]
    readout = columns[:, 1:2]

    def turn(n, carry):
        for half in range(OWN // HALF):
            lanes = slice(HALF * half, HALF * (half + 1))
            index = nbr[pl.ds(n, 1), lanes]
            weight = geo[3, pl.ds(n, 1), lanes]
            partner = jnp.concatenate(
                [
                    take_lanes(tile_reader(table), EMB, GROUPS, index[:, LANES * c : LANES * (c + 1)])
                    for c in range(HALF // LANES)
                ],
                axis=1,
            )
            embed_own = own[:, lanes]
            product_high, product_low = half_split(partner * embed_own)
            right = jnp.concatenate(
                [lat_high[n, :, lanes], product_high, lat_low[n, :, lanes], product_low], axis=0
            )
            sums = lax.dot_general(left, right, (((1,), (0,)), ((), ())), preferred_element_type=F32)
            value = sums[:H] + sums[H:] + bias
            gate = 0.5 * jnp.tanh(0.5 * value) + 0.5
            hidden = value * gate
            dvalue = (gate + hidden * (1.0 - gate)) * (readout * weight)
            dhigh, dlow = half_split(dvalue)
            sums = lax.dot_general(
                right_back, jnp.concatenate([dhigh, dlow], axis=0), (((1,), (0,)), ((), ())),
                preferred_element_type=F32,
            )
            total = sums[: H + EMB] + sums[H + EMB :]
            dlatent = total[:H]
            dproduct = total[H:]
            dsum = dlatent * slope[n, :, lanes] - (weight * weight) * (hidden * readout)
            rise[pl.ds(n, 1), lanes] = jnp.sum(dsum, axis=0, keepdims=True)
            own_sum[:, lanes] = own_sum[:, lanes] + dproduct * partner
            high, low = half_split(dproduct * embed_own)
            joined[:, lanes] = jnp.concatenate([high, low], axis=0)
        index = nbr[pl.ds(n, 1), :]
        spread_sum[...] += lax.dot_general(
            level_rows(joined[...], index >> 8), hot_rows(index & (HALF - 1), OWN),
            (((1,), (1,)), ((), ())), preferred_element_type=F32,
        )
        return carry

    lax.fori_loop(0, NEI, turn, 0)
    for k in range(LEVELS):
        base = 2 * EMB * k
        width = min(HALF, EXT - HALF * k)
        table[:, HALF * k : HALF * k + width] = (
            spread_sum[base : base + EMB, :width] + spread_sum[base + EMB : base + 2 * EMB, :width]
        )
    inner[:, 0:OWN] = table[:, 0:OWN] + own_sum[...]
    inner[:, OWN:INNER] = table[:, OWN:INNER]
    outer_messages(par, table, one, two)


def outer_messages(par, table, one, two):
    p = par[1]
    down = table[:, INNER : INNER + GY]
    up = table[:, INNER + GY : EXT]
    one[...] = by_parity(p, up, down)
    two[...] = by_parity(p, down, up)


def fold_narrow(par, inner, one, two, gy):
    p = par[1]
    from_upper = by_parity(p, one[...], two[...])
    from_lower = by_parity(p, two[...], one[...])
    return (
        inner[...]
        + spread(from_upper, gy[0:1, 0:GY], INNER)
        + spread(from_lower, gy[1:2, 0:GY], INNER)
    )


def fold_long(par, own, one, two, gx):
    p = par[0]
    from_upper = by_parity(p, one[...], two[...])
    from_lower = by_parity(p, two[...], one[...])
    return own[...] + spread(from_upper, gx[0:1, :], OWN) + spread(from_lower, gx[1:2, :], OWN)


def fold_kernel(par, inner, one_in, two_in, gy, own, one, two):
    total = fold_narrow(par, inner, one_in, two_in, gy)
    own[...] = total[:, 0:OWN]
    down = total[:, OWN : OWN + GX]
    up = total[:, OWN + GX : INNER]
    p = par[0]
    one[...] = by_parity(p, up, down)
    two[...] = by_parity(p, down, up)


def force_kernel(
    par, own_in, gx1, gx2, gx, w_back, slope, rise, geo, nbr, inner, one, two, table, spread_sum, pushes, grown,
):
    grad = fold_long(par, own_in, gx1, gx2, gx)
    grown[...] = jnp.dot(w_back[...], grad, precision=HIGHEST, preferred_element_type=F32) * (1.0 / math.sqrt(NEI))
    spread_sum[...] = jnp.zeros(spread_sum.shape, F32)

    def turn(n, carry):
        rate = jnp.sum(slope[n] * grown[...], axis=0, keepdims=True) + rise[pl.ds(n, 1), :]
        twice = 2.0 * rate
        push = [geo[c, pl.ds(n, 1), :] * twice for c in range(3)]
        highs = [v.astype(BF16).astype(F32) for v in push]
        rows = highs + [v - h for v, h in zip(push, highs)]
        empty = jnp.zeros((2, OWN), F32)
        value = jnp.concatenate(rows + [empty], axis=0)
        pushes[...] += value
        index = nbr[pl.ds(n, 1), :]
        high_row = index >> 8
        lifted = jnp.concatenate(
            [jnp.where(high_row == k, value, 0.0) for k in range(LEVELS)], axis=0
        ).astype(BF16)
        spread_sum[...] += lax.dot_general(
            lifted, hot_rows(index & (HALF - 1), OWN), (((1,), (1,)), ((), ())), preferred_element_type=F32
        )
        return carry

    pushes[...] = jnp.zeros(pushes.shape, F32)
    lax.fori_loop(0, NEI, turn, 0)
    table[...] = jnp.zeros(table.shape, F32)
    for k in range(LEVELS):
        width = min(HALF, EXT - HALF * k)
        table[0:3, HALF * k : HALF * k + width] = (
            spread_sum[8 * k : 8 * k + 3, :width] + spread_sum[8 * k + 3 : 8 * k + 6, :width]
        )
    table[0:3, 0:OWN] = table[0:3, 0:OWN] - pushes[0:3, :] - pushes[3:6, :]
    inner[...] = table[:, 0:INNER]
    outer_messages(par, table, one, two)


def final_kernel(par, own, one, two, gx, bundle, pos_out, vel_out, frc_out):
    forces = -fold_long(par, own, one, two, gx)[0:3, :]
    pos_out[...] = bundle[0:3, :]
    vel_out[...] = bundle[3:6, :] + (0.5 * TIME_STEP) * forces
    frc_out[...] = forces


def call(kernel, name, shapes, scratch, par, *operands):
    return pl.pallas_call(
        kernel,
        name=name,
        out_shape=[jax.ShapeDtypeStruct(shape, kind) for shape, kind in shapes],
        in_specs=[pl.BlockSpec(memory_space=pltpu.SMEM)]
        + [pl.BlockSpec(memory_space=pltpu.VMEM)] * len(operands),
        out_specs=[pl.BlockSpec(memory_space=pltpu.VMEM)] * len(shapes),
        scratch_shapes=[pltpu.VMEM(shape, kind) for shape, kind in scratch],
        compiler_params=pltpu.CompilerParams(vmem_limit_bytes=BIG),
    )(par, *operands)


def swap(axis, first):
    count = lax.axis_size(axis)
    offset = 0 if first else 1
    route = []
    for i in range(count):
        route.append((i, (((i + offset) ^ 1) - offset) % count))
    return route


def exchange(axis, one, two):
    return (
        lax.ppermute(one, axis, swap(axis, True)),
        lax.ppermute(two, axis, swap(axis, False)),
    )


def on_device(
    positions, velocities, forces, neighbours, ghost_x, ghost_y, migrate_x, migrate_y,
    w_basis, b_basis, w_embed, w_pair, w_mix, b_pair, w_out,
):
    par = jnp.stack([lax.axis_index("gx") % 2, lax.axis_index("gy") % 2]).astype(I32)
    near = neighbours[0]
    gx = ghost_x[0]
    gy = jnp.pad(ghost_y[0], ((0, 0), (0, HALF - GY)))
    mx = jnp.pad(migrate_x[0], ((0, 0), (0, LANES - MIG)))
    my = jnp.pad(migrate_y[0], ((0, 0), (0, LANES - MIG)))

    basis, ahead, back, w_back, columns = call(
        prepare_kernel,
        "prepare",
        [
            ((H, 4 * NB), BF16), ((2 * H, 2 * (H + EMB)), BF16), ((2 * (H + EMB), 2 * H), BF16),
            ((H, EMB), F32), ((H, NB), F32),
        ],
        [],
        par, w_basis.T, w_pair, w_mix.T, w_embed,
        b_basis.reshape(1, H), b_pair.reshape(1, H), w_out.reshape(1, H),
    )

    tile = ((8, LANES), F32)
    wide = ((8, OWN), F32)
    bundle, one, two = call(start_kernel, "start", [wide, tile, tile], [], par, positions, velocities, forces, mx)
    one, two = exchange("gx", one, two)
    bundle, one, two = call(cross_kernel, "cross", [wide, tile, tile], [], par, bundle, one, two, mx, my)
    one, two = exchange("gy", one, two)
    bundle, one, two = call(settle_kernel, "settle", [wide, tile, tile], [], par, bundle, one, two, my, gx)
    px = exchange("gx", one, two)
    message = ((8, HALF), F32)
    one, two = call(
        lambda *refs: ghost_kernel(1, *refs), "ghost", [message, message], [((8, INNER), F32)], par, bundle, *px, gy
    )
    py = exchange("gy", one, two)

    embed, one, two, lat_high, lat_low, slope, geo = call(
        env_kernel,
        "env",
        [
            ((EMB, OWN), F32), ((EMB, GX), F32), ((EMB, GX), F32),
            ((NEI, H, OWN), BF16), ((NEI, H, OWN), BF16), ((NEI, H, OWN), F32), ((4, NEI, OWN), F32),
        ],
        [((8, EXT), F32), ((NEI, OWN), F32)],
        par, bundle, *px, *py, near, basis, w_embed, gx,
    )
    ex = exchange("gx", one, two)
    message = ((EMB, HALF), F32)
    one, two = call(
        lambda *refs: ghost_kernel(None, *refs), "ghost_embed", [message, message], [((EMB, INNER), F32)],
        par, embed, *ex, gy,
    )
    ey = exchange("gy", one, two)
    message = ((EMB, GY), F32)
    rise, inner, one, two = call(
        pair_kernel,
        "pair",
        [((NEI, OWN), F32), ((EMB, INNER), F32), message, message],
        [
            ((EMB, EXT), F32), ((LEVELS * 2 * EMB, HALF), F32), ((EMB, OWN), F32), ((2 * EMB, OWN), BF16),
        ],
        par, embed, *ex, *ey, near, lat_high, lat_low, slope, geo, ahead, back, columns,
    )
    one, two = exchange("gy", one, two)
    message = ((EMB, GX), F32)
    own, one, two = call(
        fold_kernel, "fold_embed", [((EMB, OWN), F32), message, message], [], par, inner, one, two, gy
    )
    one, two = exchange("gx", one, two)
    message = ((8, GY), F32)
    inner, one, two = call(
        force_kernel,
        "force",
        [((8, INNER), F32), message, message],
        [((8, EXT), F32), ((8 * LEVELS, HALF), F32), ((8, OWN), F32), ((H, OWN), F32)],
        par, own, one, two, gx, w_back, slope, rise, geo, near,
    )
    one, two = exchange("gy", one, two)
    own, one, two = call(fold_kernel, "fold_force", [wide, tile, tile], [], par, inner, one, two, gy)
    one, two = exchange("gx", one, two)
    flat = ((3, OWN), F32)
    return tuple(call(final_kernel, "final", [flat, flat, flat], [], par, own, one, two, gx, bundle))


def solution(mesh):
    both = ("gx", "gy")
    flat = P(None, both)
    stacked = P(None, None, both)
    return jax.shard_map(
        on_device,
        mesh=mesh,
        in_specs=(flat,) * 3 + (stacked,) * 5 + (P(),) * 7,
        out_specs=(flat,) * 3,
        check_vma=False,
    )
```

```python
import math

import jax
import jax.numpy as jnp
from jax import lax
from jax.experimental import pallas as pl
from jax.experimental.pallas import tpu as pltpu
from jax.sharding import PartitionSpec as P

F32 = jnp.float32
BF16 = jnp.bfloat16
I32 = jnp.int32

TIME_STEP = 0.05
CENTRE_SPAN = 3.0
HIGHEST = lax.Precision.HIGHEST

NB = 8
NEI = 32
H = 64
EMB = 32
OWN = 512
GX = 128
GY = 192
MIG = 8
LANES = 128
INNER = OWN + 2 * GX
EXT = INNER + 2 * GY
GROUPS = EXT // LANES
HALF = 256
LEVELS = -(-EXT // HALF)
BIG = 48 * 1024 * 1024
GROUP = 4
CHUNK = 512
UNROLL_ENV = 8
UNROLL_FORCE = 4


def half_split(value):
    high = value.astype(BF16)
    low = (value - high.astype(F32)).astype(BF16)
    return high, low


def third_split(value):
    high = value.astype(BF16)
    rest = value - high.astype(F32)
    middle = rest.astype(BF16)
    low = (rest - middle.astype(F32)).astype(BF16)
    return high, middle, low


def lane_take(table, index):
    return jnp.take_along_axis(table, index, axis=1, mode="promise_in_bounds")


def take_lanes(read, rows, groups, index_row):
    low = jnp.broadcast_to(index_row & (LANES - 1), (8, LANES))
    high = jnp.broadcast_to(index_row >> 7, (8, LANES))
    pieces = []
    for r in range(rows // 8):
        taken = jnp.zeros((8, LANES), F32)
        for g in range(groups):
            taken = jnp.where(high == g, lane_take(read(r, g), low), taken)
        pieces.append(taken)
    return jnp.concatenate(pieces, axis=0) if len(pieces) > 1 else pieces[0]


def tile_reader(ref):
    return lambda r, g: ref[8 * r : 8 * r + 8, LANES * g : LANES * (g + 1)]


def spread(values, lists, width):
    count = values.shape[1]
    hot = jnp.where(lax.broadcasted_iota(I32, (width, count), 0) == lists, 1.0, 0.0).astype(BF16)
    total = None
    for part in third_split(values):
        piece = lax.dot_general(part, hot, (((1,), (1,)), ((), ())), preferred_element_type=F32)
        total = piece if total is None else total + piece
    return total


def by_parity(parity, even, odd):
    return jnp.where(parity == 0, even, odd)


def unit_row(rows, row, amount):
    return jnp.where(lax.broadcasted_iota(I32, (rows, 1), 0) == row, amount, 0.0)


def place(record, slots, message, base):
    lane = lax.broadcasted_iota(I32, record.shape, 1)
    moved = record
    for k in range(base, base + MIG):
        moved = jnp.where(lane == slots[:, k : k + 1], message[:, k : k + 1], moved)
    return jnp.where(lax.broadcasted_iota(I32, record.shape, 0) < 6, moved, record)


def value_reader(value):
    return lambda r, g: value[8 * r : 8 * r + 8, LANES * g : LANES * (g + 1)]


def side_list(record, side):
    return record[6:7, 2 * GX + LANES * side : 2 * GX + LANES * (side + 1)].astype(I32)


def ghost_list(record, side):
    return record[6:7, GX * side : GX * (side + 1)].astype(I32)


def narrow_list(record, side):
    return record[7:8, HALF * side : HALF * (side + 1)].astype(I32)


def leavers(record, side, row):
    shift = -1.0 if side == 0 else 1.0
    return take_lanes(value_reader(record), 8, OWN // LANES, side_list(record, side)) + unit_row(8, row, shift)


def fetch(sources, targets, sems):
    copies = [pltpu.make_async_copy(src, dst, sems.at[k]) for k, (src, dst) in enumerate(zip(sources, targets))]
    for copy in copies:
        copy.start()
    for copy in copies:
        copy.wait()


def prepare_kernel(
    par, basis_t, pair, mix_t, w_embed, b_basis, b_pair, w_out, basis, ahead, back, w_back, columns, *scratch
):
    held = scratch[:-1]
    fetch((basis_t, pair, mix_t, w_embed, b_basis, b_pair, w_out), held, scratch[-1])
    basis_t, pair, mix_t, w_embed, b_basis, b_pair, w_out = held
    high, low = half_split(basis_t[...])
    high, low = high.astype(F32), low.astype(F32)
    parts = [part.astype(F32) for part in third_split(b_basis[...])]
    parts = jnp.concatenate(parts + [jnp.zeros((NB - 3, H), F32)], axis=0)
    basis[...] = jnp.concatenate([high, high, low, parts], axis=0).T.astype(BF16)
    rows = jnp.concatenate([b_pair[...], w_out[...], jnp.zeros((NB - 2, H), F32)], axis=0)
    columns[...] = rows.T
    w_back[...] = w_embed[...].T
    layer_t = jnp.concatenate([pair[...].T, mix_t[...]], axis=0)
    high, low = half_split(layer_t)
    high, low = high.astype(F32), low.astype(F32)
    nothing = jnp.zeros((H + EMB, H), F32)
    back[...] = jnp.concatenate(
        [jnp.concatenate([high, high], axis=1), jnp.concatenate([low, nothing], axis=1)], axis=0
    ).astype(BF16)
    ahead[0:H, :] = jnp.concatenate([high, high], axis=0).T.astype(BF16)
    ahead[H : 2 * H, :] = jnp.concatenate([low, nothing], axis=0).T.astype(BF16)


def start_kernel(par, pos, vel, frc, gx, gy, mx, my, record, message, gx_out, gy_out, *scratch):
    held = scratch[:-1]
    fetch((pos, vel, frc, gx, gy, mx, my), held, scratch[-1])
    pos, vel, frc, gx, gy, mx, my = held
    speeds = vel[...] + (0.5 * TIME_STEP) * frc[...]
    record[0:3, :] = pos[...] + TIME_STEP * speeds
    record[3:6, :] = speeds
    record[6:8, :] = jnp.zeros((2, OWN), F32)
    gy_out[...] = jnp.zeros((2, HALF), I32)
    gx_out[...] = gx[0]
    gy_out[:, 0:GY] = gy[0]
    for side in range(2):
        start = 2 * GX + LANES * side
        record[6:7, GX * side : GX * (side + 1)] = gx[0, side : side + 1, :].astype(F32)
        record[6:7, start : start + MIG] = mx[0, side : side + 1, :].astype(F32)
        record[6:7, start + MIG : start + 2 * MIG] = my[0, side : side + 1, :].astype(F32)
        record[7:8, HALF * side : HALF * side + GY] = gy[0, side : side + 1, :].astype(F32)
    whole = record[...]
    message[...] = by_parity(par[0], leavers(whole, 0, 0), leavers(whole, 1, 0))


def cross_kernel(par, record, message, joined, out):
    p = par[0]
    own = record[...]
    other = joined[:, 0:OWN]
    mine = message[...]
    theirs = joined[:, OWN : OWN + LANES]
    low = by_parity(p, other, own)
    high = by_parity(p, own, other)
    from_below = by_parity(p, theirs, mine)
    from_above = by_parity(p, mine, theirs)
    new_low = place(low, side_list(low, 1), from_below, 0)
    new_low = place(new_low, side_list(low, 0), leavers(high, 1, 0), 0)
    new_high = place(high, side_list(high, 1), leavers(low, 0, 0), 0)
    new_high = place(new_high, side_list(high, 0), from_above, 0)
    for b in range(out.shape[0]):
        out[b, 0:8, :] = new_low
        out[b, 8:16, :] = new_high


def settle(par, records, narrow_count, bundle, table, inner):
    p = par[0]

    def record_of(long_step, narrow_step):
        number = p + 1 + long_step
        column = lax.rem(par[2] + (narrow_step + narrow_count), narrow_count)
        return records[((number >> 1) * narrow_count + column) * 2 + (number & 1)]

    def settled(long_step, narrow_step):
        own = record_of(long_step, narrow_step)
        moved = place(own, side_list(own, 1), leavers(record_of(long_step, narrow_step - 1), 0, 1), MIG)
        return place(moved, side_list(own, 0), leavers(record_of(long_step, narrow_step + 1), 1, 1), MIG)

    for narrow_step in (-1, 1, 0):
        middle = settled(0, narrow_step)
        low = settled(-1, narrow_step)
        high = settled(1, narrow_step)
        inner[:, 0:OWN] = middle
        inner[:, OWN : OWN + GX] = (
            take_lanes(value_reader(low), 8, OWN // LANES, ghost_list(low, 0)) + unit_row(8, 0, -1.0)
        )
        inner[:, OWN + GX : INNER] = (
            take_lanes(value_reader(high), 8, OWN // LANES, ghost_list(high, 1)) + unit_row(8, 0, 1.0)
        )
        if narrow_step == 0:
            bundle[...] = middle
            table[:, 0:INNER] = inner[...]
            continue
        side = 0 if narrow_step < 0 else 1
        chosen = narrow_list(middle, side)
        taken = jnp.concatenate(
            [
                take_lanes(tile_reader(inner), 8, INNER // LANES, chosen[:, LANES * c : LANES * (c + 1)])
                for c in range(2)
            ],
            axis=1,
        )
        base = INNER + GY * side
        table[:, base : base + GY] = taken[:, 0:GY] + unit_row(8, 1, float(narrow_step))


def narrow_messages(par, table, rows, gy, one, two):
    p = par[1]
    for out, chosen in (
        (one, by_parity(p, gy[0:1, :], gy[1:2, :])),
        (two, by_parity(p, gy[1:2, :], gy[0:1, :])),
    ):
        for c in range(2):
            out[:, LANES * c : LANES * (c + 1)] = take_lanes(
                tile_reader(table), rows, INNER // LANES, chosen[:, LANES * c : LANES * (c + 1)]
            )


def inner_table(par, own, one, two, table):
    p = par[0]
    table[:, 0:OWN] = own
    table[:, OWN : OWN + GX] = by_parity(p, two[...], one[...])
    table[:, OWN + GX : INNER] = by_parity(p, one[...], two[...])


def outer_table(par, one, two, table):
    p = par[1]
    table[:, INNER : INNER + GY] = by_parity(p, two[:, 0:GY], one[:, 0:GY])
    table[:, INNER + GY : EXT] = by_parity(p, one[:, 0:GY], two[:, 0:GY])


def ghost_kernel(par, own, one_in, two_in, gy, one, two, table):
    inner_table(par, own[...], one_in, two_in, table)
    narrow_messages(par, table, own.shape[0], gy, one, two)


def env_kernel(
    narrow_count, par, records, neighbours, basis, w_embed, gx,
    own, embed, one, two, lat_high, lat_low, slope, geo, nbr, table, square, inner, sem,
):
    copy = pltpu.make_async_copy(neighbours.at[0], nbr, sem.at[0])
    copy.start()
    settle(par, records, narrow_count, own, table, inner)
    copy.wait()
    for b in range(OWN // LANES):
        lanes = slice(LANES * b, LANES * (b + 1))
        for q in range(NEI // 8):
            rows = slice(8 * q, 8 * q + 8)
            index = nbr[rows, lanes]
            low = index & (LANES - 1)
            high = index >> 7
            total = jnp.zeros((8, LANES), F32)
            for c in range(3):
                taken = jnp.zeros((8, LANES), F32)
                for g in range(GROUPS):
                    tile = jnp.broadcast_to(table[c : c + 1, LANES * g : LANES * (g + 1)], (8, LANES))
                    taken = jnp.where(high == g, lane_take(tile, low), taken)
                apart = taken - own[c : c + 1, lanes]
                geo[c, rows, lanes] = apart
                total = total + apart * apart
            square[rows, lanes] = total
            geo[3, rows, lanes] = jnp.where(index >= 0, 1.0 / (1.0 + total), 0.0)

    centre = lax.broadcasted_iota(I32, (NB, 1), 0).astype(F32) * (CENTRE_SPAN / (NB - 1))
    ones = jnp.ones((NB, HALF), F32)
    left = basis[...]
    for half in range(OWN // HALF):
        lanes = slice(HALF * half, HALF * (half + 1))

        def turn(n, gathered):
            offset = square[pl.ds(n, 1), lanes] - centre
            weight = geo[3, pl.ds(n, 1), lanes]
            radial = jnp.exp(-(offset * offset))
            falling = -2.0 * offset * radial
            radial_high = radial.astype(BF16).astype(F32)
            falling_high = falling.astype(BF16).astype(F32)
            right = jnp.concatenate(
                [
                    jnp.concatenate([radial_high, radial - radial_high, radial_high, ones], axis=0),
                    jnp.concatenate([falling_high, falling - falling_high, falling_high, 0.0 * ones], axis=0),
                ],
                axis=1,
            ).astype(BF16)
            both = lax.dot_general(left, right, (((1,), (0,)), ((), ())), preferred_element_type=F32)
            value = both[:, :HALF]
            rate = both[:, HALF:]
            gate = 0.5 * jnp.tanh(0.5 * value) + 0.5
            raw = value * gate
            latent = raw * weight
            slope[n, :, lanes] = weight * ((gate + raw * (1.0 - gate)) * rate - latent)
            high, low = half_split(latent)
            lat_high[n, :, lanes] = high
            lat_low[n, :, lanes] = low
            return gathered + latent

        gathered = lax.fori_loop(0, NEI, turn, jnp.zeros((H, HALF), F32), unroll=UNROLL_ENV)
        environ = gathered * (1.0 / math.sqrt(NEI))
        embed[:, lanes] = jnp.dot(w_embed[...], environ, precision=HIGHEST, preferred_element_type=F32)
    p = par[0]
    reader = tile_reader(embed)
    one[...] = take_lanes(reader, EMB, OWN // LANES, by_parity(p, gx[0:1, :], gx[1:2, :]))
    two[...] = take_lanes(reader, EMB, OWN // LANES, by_parity(p, gx[1:2, :], gx[0:1, :]))


def hot_rows(low_row, count):
    level = lax.broadcasted_iota(I32, (HALF, count), 0)
    return jnp.where(level == low_row, 1.0, 0.0).astype(BF16)


def level_rows(value, high_row):
    pieces = []
    for k in range(LEVELS):
        mask = jnp.where(high_row == k, 1.0, 0.0).astype(BF16)
        pieces.append(value * mask)
    return jnp.concatenate(pieces, axis=0)


def pair_kernel(
    par, own, gx1, gx2, gy1, gy2, nbr, lat_high, lat_low, slope, geo, ahead, back, columns,
    rise, inner, one, two, table, spread_sum, own_sum,
):
    inner_table(par, own[...], gx1, gx2, table)
    outer_table(par, gy1, gy2, table)
    spread_sum[...] = jnp.zeros(spread_sum.shape, F32)
    own_sum[...] = jnp.zeros(own_sum.shape, F32)
    left = ahead[...]
    right_back = back[...]
    bias = columns[:, 0:1]
    readout = columns[:, 1:2]

    def row(ref, n, lanes):
        return ref[pl.ds(n, 1), lanes]

    def scatter(g, joined):
        index = jnp.concatenate([nbr[pl.ds(GROUP * g + j, 1), :] for j in range(GROUP)], axis=1)
        spread_sum[...] += lax.dot_general(
            level_rows(joined, index >> 8), hot_rows(index & (HALF - 1), GROUP * OWN),
            (((1,), (1,)), ((), ())), preferred_element_type=F32,
        )

    def chunk(n, lanes, width):
        index = nbr[pl.ds(n, 1), lanes]
        weight = geo[3, pl.ds(n, 1), lanes]
        partner = jnp.concatenate(
            [
                take_lanes(tile_reader(table), EMB, GROUPS, index[:, LANES * c : LANES * (c + 1)])
                for c in range(width // LANES)
            ],
            axis=1,
        )
        embed_own = own[:, lanes]
        product_high, product_low = half_split(partner * embed_own)
        right = jnp.concatenate(
            [lat_high[n, :, lanes], product_high, lat_low[n, :, lanes], product_low], axis=0
        )
        sums = lax.dot_general(left, right, (((1,), (0,)), ((), ())), preferred_element_type=F32)
        value = sums[:H] + sums[H:] + bias
        gate = 0.5 * jnp.tanh(0.5 * value) + 0.5
        hidden = value * gate
        dvalue = (gate + hidden * (1.0 - gate)) * (readout * weight)
        dhigh, dlow = half_split(dvalue)
        sums = lax.dot_general(
            right_back, jnp.concatenate([dhigh, dlow], axis=0), (((1,), (0,)), ((), ())),
            preferred_element_type=F32,
        )
        total = sums[: H + EMB] + sums[H + EMB :]
        dlatent = total[:H]
        dproduct = total[H:]
        dsum = dlatent * slope[n, :, lanes] - (weight * weight) * (hidden * readout)
        rise[pl.ds(n, 1), lanes] = jnp.sum(dsum, axis=0, keepdims=True)
        high, low = half_split(dproduct * embed_own)
        return dproduct * partner, jnp.concatenate([high, low], axis=0)

    def turn(g, joined):
        scatter(jnp.maximum(g - 1, 0), joined)
        pieces = {}
        for part in range(OWN // CHUNK):
            lanes = slice(CHUNK * part, CHUNK * (part + 1))
            grown = own_sum[:, lanes]
            for j in range(GROUP):
                more, piece = chunk(GROUP * g + j, lanes, CHUNK)
                grown = grown + more
                pieces[j, part] = piece
            own_sum[:, lanes] = grown
        return jnp.concatenate([pieces[j, part] for j in range(GROUP) for part in range(OWN // CHUNK)], axis=1)

    joined = lax.fori_loop(0, NEI // GROUP, turn, jnp.zeros((2 * EMB, GROUP * OWN), BF16))
    scatter(NEI // GROUP - 1, joined)
    for k in range(LEVELS):
        base = 2 * EMB * k
        width = min(HALF, EXT - HALF * k)
        table[:, HALF * k : HALF * k + width] = (
            spread_sum[base : base + EMB, :width] + spread_sum[base + EMB : base + 2 * EMB, :width]
        )
    inner[:, 0:OWN] = table[:, 0:OWN] + own_sum[...]
    inner[:, OWN:INNER] = table[:, OWN:INNER]
    outer_messages(par, table, one, two)


def outer_messages(par, table, one, two):
    p = par[1]
    down = table[:, INNER : INNER + GY]
    up = table[:, INNER + GY : EXT]
    one[...] = by_parity(p, up, down)
    two[...] = by_parity(p, down, up)


def fold_narrow(par, inner, one, two, gy):
    p = par[1]
    from_upper = by_parity(p, one[...], two[...])
    from_lower = by_parity(p, two[...], one[...])
    return (
        inner[...]
        + spread(from_upper, gy[0:1, 0:GY], INNER)
        + spread(from_lower, gy[1:2, 0:GY], INNER)
    )


def fold_long(par, own, one, two, gx):
    p = par[0]
    from_upper = by_parity(p, one[...], two[...])
    from_lower = by_parity(p, two[...], one[...])
    return own[...] + spread(from_upper, gx[0:1, :], OWN) + spread(from_lower, gx[1:2, :], OWN)


def fold_kernel(par, inner, one_in, two_in, gy, own, one, two):
    total = fold_narrow(par, inner, one_in, two_in, gy)
    own[...] = total[:, 0:OWN]
    down = total[:, OWN : OWN + GX]
    up = total[:, OWN + GX : INNER]
    p = par[0]
    one[...] = by_parity(p, up, down)
    two[...] = by_parity(p, down, up)


def force_kernel(
    par, own_in, gx1, gx2, gx, w_back, slope, rise, geo, nbr, inner, one, two, table, spread_sum, pushes, grown,
):
    grad = fold_long(par, own_in, gx1, gx2, gx)
    grown[...] = jnp.dot(w_back[...], grad, precision=HIGHEST, preferred_element_type=F32) * (1.0 / math.sqrt(NEI))
    spread_sum[...] = jnp.zeros(spread_sum.shape, F32)

    def turn(n, carry):
        rate = jnp.sum(slope[n] * grown[...], axis=0, keepdims=True) + rise[pl.ds(n, 1), :]
        twice = 2.0 * rate
        push = [geo[c, pl.ds(n, 1), :] * twice for c in range(3)]
        highs = [v.astype(BF16).astype(F32) for v in push]
        rows = highs + [v - h for v, h in zip(push, highs)]
        empty = jnp.zeros((2, OWN), F32)
        value = jnp.concatenate(rows + [empty], axis=0)
        pushes[...] += value
        index = nbr[pl.ds(n, 1), :]
        high_row = index >> 8
        lifted = jnp.concatenate(
            [jnp.where(high_row == k, value, 0.0) for k in range(LEVELS)], axis=0
        ).astype(BF16)
        spread_sum[...] += lax.dot_general(
            lifted, hot_rows(index & (HALF - 1), OWN), (((1,), (1,)), ((), ())), preferred_element_type=F32
        )
        return carry

    pushes[...] = jnp.zeros(pushes.shape, F32)
    lax.fori_loop(0, NEI, turn, 0, unroll=UNROLL_FORCE)
    table[...] = jnp.zeros(table.shape, F32)
    for k in range(LEVELS):
        width = min(HALF, EXT - HALF * k)
        table[0:3, HALF * k : HALF * k + width] = (
            spread_sum[8 * k : 8 * k + 3, :width] + spread_sum[8 * k + 3 : 8 * k + 6, :width]
        )
    table[0:3, 0:OWN] = table[0:3, 0:OWN] - pushes[0:3, :] - pushes[3:6, :]
    inner[...] = table[:, 0:INNER]
    outer_messages(par, table, one, two)


def final_kernel(par, own, one, two, gx, bundle, pos_out, vel_out, frc_out):
    forces = -fold_long(par, own, one, two, gx)[0:3, :]
    pos_out[...] = bundle[0:3, :]
    vel_out[...] = bundle[3:6, :] + (0.5 * TIME_STEP) * forces
    frc_out[...] = forces


def call(kernel, name, shapes, scratch, par, *operands, far=(), limit=BIG):
    specs = [pl.BlockSpec(memory_space=pl.ANY if k in far else pltpu.VMEM) for k in range(len(operands))]
    return pl.pallas_call(
        kernel,
        name=name,
        out_shape=[jax.ShapeDtypeStruct(shape, kind) for shape, kind in shapes],
        in_specs=[pl.BlockSpec(memory_space=pltpu.SMEM)] + specs,
        out_specs=[pl.BlockSpec(memory_space=pltpu.VMEM)] * len(shapes),
        scratch_shapes=[
            pltpu.SemaphoreType.DMA(shape) if kind is None else pltpu.VMEM(shape, kind) for shape, kind in scratch
        ],
        compiler_params=pltpu.CompilerParams(vmem_limit_bytes=limit),
    )(par, *operands)


def holds(*arrays):
    return [(a.shape, a.dtype) for a in arrays] + [((len(arrays),), None)]


def swap(axis, first):
    count = lax.axis_size(axis)
    offset = 0 if first else 1
    route = []
    for i in range(count):
        route.append((i, (((i + offset) ^ 1) - offset) % count))
    return route


def exchange(axis, one, two):
    return (
        lax.ppermute(one, axis, swap(axis, True)),
        lax.ppermute(two, axis, swap(axis, False)),
    )


def on_device(
    positions, velocities, forces, neighbours, ghost_x, ghost_y, migrate_x, migrate_y,
    w_basis, b_basis, w_embed, w_pair, w_mix, b_pair, w_out,
):
    row = lax.axis_index("gx")
    column = lax.axis_index("gy")
    narrow_count = lax.axis_size("gy")
    par = jnp.stack([row % 2, column % 2, column]).astype(I32)

    tile = ((8, LANES), F32)
    wide = ((8, OWN), F32)
    given = (positions, velocities, forces, ghost_x, ghost_y, migrate_x, migrate_y)
    record, message, gx, gy = call(
        start_kernel, "start", [wide, tile, ((2, GX), I32), ((2, HALF), I32)], holds(*given), par, *given,
        far=range(len(given)),
    )
    given = (
        w_basis.T, w_pair, w_mix.T, w_embed, b_basis.reshape(1, H), b_pair.reshape(1, H), w_out.reshape(1, H),
    )
    basis, ahead, back, w_back, columns = call(
        prepare_kernel,
        "prepare",
        [
            ((H, 4 * NB), BF16), ((2 * H, 2 * (H + EMB)), BF16), ((2 * (H + EMB), 2 * H), BF16),
            ((H, EMB), F32), ((H, NB), F32),
        ],
        holds(*given), par, *given, far=range(len(given)),
    )
    message = lax.ppermute(message, "gx", swap("gx", True))
    joined = lax.ppermute(jnp.concatenate([record, message], axis=1), "gx", swap("gx", False))
    group = 2 * narrow_count
    (records,) = call(cross_kernel, "cross", [((group, 16, OWN), F32)], [], par, record, message, joined)
    members = [list(range(group * k, group * (k + 1))) for k in range(lax.axis_size("gx") // 2)]
    records = lax.all_to_all(records, ("gx", "gy"), 0, 0, axis_index_groups=members)

    bundle, embed, one, two, lat_high, lat_low, slope, geo, near = call(
        lambda *refs: env_kernel(narrow_count, *refs),
        "env",
        [
            wide, ((EMB, OWN), F32), ((EMB, GX), F32), ((EMB, GX), F32),
            ((NEI, H, OWN), BF16), ((NEI, H, OWN), BF16), ((NEI, H, OWN), F32), ((4, NEI, OWN), F32),
            ((NEI, OWN), I32),
        ],
        [((8, EXT), F32), ((NEI, OWN), F32), ((8, INNER), F32), ((1,), None)],
        par, records.reshape(2 * group, 8, OWN), neighbours, basis, w_embed, gx, far=(1,),
    )
    ex = exchange("gx", one, two)
    message = ((EMB, HALF), F32)
    one, two = call(
        ghost_kernel, "ghost_embed", [message, message], [((EMB, INNER), F32)],
        par, embed, *ex, gy,
    )
    ey = exchange("gy", one, two)
    message = ((EMB, GY), F32)
    rise, inner, one, two = call(
        pair_kernel,
        "pair",
        [((NEI, OWN), F32), ((EMB, INNER), F32), message, message],
        [
            ((EMB, EXT), F32), ((LEVELS * 2 * EMB, HALF), F32), ((EMB, OWN), F32),
        ],
        par, embed, *ex, *ey, near, lat_high, lat_low, slope, geo, ahead, back, columns,
    )
    one, two = exchange("gy", one, two)
    message = ((EMB, GX), F32)
    own, one, two = call(
        fold_kernel, "fold_embed", [((EMB, OWN), F32), message, message], [], par, inner, one, two, gy
    )
    one, two = exchange("gx", one, two)
    message = ((8, GY), F32)
    inner, one, two = call(
        force_kernel,
        "force",
        [((8, INNER), F32), message, message],
        [((8, EXT), F32), ((8 * LEVELS, HALF), F32), ((8, OWN), F32), ((H, OWN), F32)],
        par, own, one, two, gx, w_back, slope, rise, geo, near,
    )
    one, two = exchange("gy", one, two)
    own, one, two = call(fold_kernel, "fold_force", [wide, tile, tile], [], par, inner, one, two, gy)
    one, two = exchange("gx", one, two)
    flat = ((3, OWN), F32)
    return tuple(call(final_kernel, "final", [flat, flat, flat], [], par, own, one, two, gx, bundle))


def solution(mesh):
    both = ("gx", "gy")
    flat = P(None, both)
    stacked = P(None, None, both)
    return jax.shard_map(
        on_device,
        mesh=mesh,
        in_specs=(flat,) * 3 + (stacked,) * 5 + (P(),) * 7,
        out_specs=(flat,) * 3,
        check_vma=False,
    )
```

```python
import math

import jax
import jax.numpy as jnp
from jax import lax
from jax.experimental import pallas as pl
from jax.experimental.pallas import tpu as pltpu
from jax.sharding import PartitionSpec as P

F32 = jnp.float32
BF16 = jnp.bfloat16
I32 = jnp.int32

TIME_STEP = 0.05
CENTRE_SPAN = 3.0
HIGHEST = lax.Precision.HIGHEST

NB = 8
NEI = 32
H = 64
EMB = 32
OWN = 512
GX = 128
GY = 192
MIG = 8
LANES = 128
INNER = OWN + 2 * GX
EXT = INNER + 2 * GY
GROUPS = EXT // LANES
HALF = 256
LEVELS = -(-EXT // HALF)
BIG = 24 * 1024 * 1024
WHOLE = 60 * 1024 * 1024
GROUP = 4
CHUNK = 512
UNROLL_ENV = 8


def half_split(value):
    high = value.astype(BF16)
    low = (value - high.astype(F32)).astype(BF16)
    return high, low


def third_split(value):
    high = value.astype(BF16)
    rest = value - high.astype(F32)
    middle = rest.astype(BF16)
    low = (rest - middle.astype(F32)).astype(BF16)
    return high, middle, low


def lane_take(table, index):
    return jnp.take_along_axis(table, index, axis=1, mode="promise_in_bounds")


def take_lanes(read, rows, groups, index_row):
    low = jnp.broadcast_to(index_row & (LANES - 1), (8, LANES))
    high = jnp.broadcast_to(index_row >> 7, (8, LANES))
    pieces = []
    for r in range(rows // 8):
        taken = jnp.zeros((8, LANES), F32)
        for g in range(groups):
            taken = jnp.where(high == g, lane_take(read(r, g), low), taken)
        pieces.append(taken)
    return jnp.concatenate(pieces, axis=0) if len(pieces) > 1 else pieces[0]


def tile_reader(ref):
    return lambda r, g: ref[8 * r : 8 * r + 8, LANES * g : LANES * (g + 1)]


def spread(values, lists, width):
    count = values.shape[1]
    hot = jnp.where(lax.broadcasted_iota(I32, (width, count), 0) == lists, 1.0, 0.0).astype(BF16)
    total = None
    for part in third_split(values):
        piece = lax.dot_general(part, hot, (((1,), (1,)), ((), ())), preferred_element_type=F32)
        total = piece if total is None else total + piece
    return total


def by_parity(parity, even, odd):
    return jnp.where(parity == 0, even, odd)


def unit_row(rows, row, amount):
    return jnp.where(lax.broadcasted_iota(I32, (rows, 1), 0) == row, amount, 0.0)


def place(record, slots, message, base):
    lane = lax.broadcasted_iota(I32, record.shape, 1)
    moved = record
    for k in range(base, base + MIG):
        moved = jnp.where(lane == slots[:, k : k + 1], message[:, k : k + 1], moved)
    return jnp.where(lax.broadcasted_iota(I32, record.shape, 0) < 6, moved, record)


def value_reader(value):
    return lambda r, g: value[8 * r : 8 * r + 8, LANES * g : LANES * (g + 1)]


def side_list(record, side):
    return record[6:7, 2 * GX + LANES * side : 2 * GX + LANES * (side + 1)].astype(I32)


def ghost_list(record, side):
    return record[6:7, GX * side : GX * (side + 1)].astype(I32)


def narrow_list(record, side):
    return record[7:8, HALF * side : HALF * (side + 1)].astype(I32)


def leavers(record, side, row):
    shift = -1.0 if side == 0 else 1.0
    return take_lanes(value_reader(record), 8, OWN // LANES, side_list(record, side)) + unit_row(8, row, shift)


def fetch(sources, targets, sems):
    copies = [pltpu.make_async_copy(src, dst, sems.at[k]) for k, (src, dst) in enumerate(zip(sources, targets))]
    for copy in copies:
        copy.start()
    for copy in copies:
        copy.wait()


def prepare_kernel(
    par, neighbours, basis_t, pair, mix_t, w_embed, vectors, near, basis, pair_ahead, mix_ahead, pair_back, mix_back, w_ahead, w_back, columns, *scratch
):
    held = scratch[:-1]
    near[...] = neighbours[0]
    fetch((basis_t, pair, mix_t, w_embed, vectors), held, scratch[-1])
    basis_t, pair, mix_t, w_embed, vectors = held
    b_basis = vectors[0:1, :]
    high, low = half_split(basis_t[...])
    high, low = high.astype(F32), low.astype(F32)
    parts = [part.astype(F32) for part in third_split(b_basis)]
    parts = jnp.concatenate(parts + [jnp.zeros((NB - 3, H), F32)], axis=0)
    basis[...] = jnp.concatenate([high, high, low, parts], axis=0).T.astype(BF16)
    rows = jnp.concatenate([vectors[1:3, :], jnp.zeros((NB - 2, H), F32)], axis=0)
    columns[...] = rows.T
    w_ahead[...] = w_embed[...]
    w_back[...] = w_embed[...].T
    for layer_t, ahead, back in ((pair[...].T, pair_ahead, pair_back), (mix_t[...], mix_ahead, mix_back)):
        high, low = half_split(layer_t)
        high, low = high.astype(F32), low.astype(F32)
        nothing = jnp.zeros(high.shape, F32)
        back[...] = jnp.concatenate(
            [jnp.concatenate([high, high], axis=1), jnp.concatenate([low, nothing], axis=1)], axis=0
        ).astype(BF16)
        ahead[0:H, :] = jnp.concatenate([high, high], axis=0).T.astype(BF16)
        ahead[H : 2 * H, :] = jnp.concatenate([low, nothing], axis=0).T.astype(BF16)


def start_kernel(par, pos, vel, frc, gx, gy, mx, my, record, message, *scratch):
    held = scratch[:-1]
    fetch((pos, vel, frc, gx, gy, mx, my), held, scratch[-1])
    pos, vel, frc, gx, gy, mx, my = held
    speeds = vel[...] + (0.5 * TIME_STEP) * frc[...]
    record[0:3, :] = pos[...] + TIME_STEP * speeds
    record[3:6, :] = speeds
    record[6:8, :] = jnp.zeros((2, OWN), F32)
    for side in range(2):
        start = 2 * GX + LANES * side
        record[6:7, GX * side : GX * (side + 1)] = gx[0, side : side + 1, :].astype(F32)
        record[6:7, start : start + MIG] = mx[0, side : side + 1, :].astype(F32)
        record[6:7, start + MIG : start + 2 * MIG] = my[0, side : side + 1, :].astype(F32)
        record[7:8, HALF * side : HALF * side + GY] = gy[0, side : side + 1, :].astype(F32)
    whole = record[...]
    message[...] = by_parity(par[0], leavers(whole, 0, 0), leavers(whole, 1, 0))


def cross_kernel(par, kept, joined, out):
    p = par[0]
    own = kept[:, 0:OWN]
    other = joined[:, 0:OWN]
    mine = kept[:, OWN : OWN + LANES]
    theirs = joined[:, OWN : OWN + LANES]
    low = by_parity(p, other, own)
    high = by_parity(p, own, other)
    from_below = by_parity(p, theirs, mine)
    from_above = by_parity(p, mine, theirs)
    new_low = place(low, side_list(low, 1), from_below, 0)
    new_low = place(new_low, side_list(low, 0), leavers(high, 1, 0), 0)
    new_high = place(high, side_list(high, 1), leavers(low, 0, 0), 0)
    new_high = place(new_high, side_list(high, 0), from_above, 0)
    for b in range(out.shape[0]):
        out[b, 0:8, :] = new_low
        out[b, 8:16, :] = new_high


def settle(par, records, narrow_count, bundle, table, inner):
    p = par[0]

    def record_of(long_step, narrow_step):
        number = p + 1 + long_step
        column = lax.rem(par[2] + (narrow_step + narrow_count), narrow_count)
        return records[((number >> 1) * narrow_count + column) * 2 + (number & 1)]

    def settled(long_step, narrow_step):
        own = record_of(long_step, narrow_step)
        moved = place(own, side_list(own, 1), leavers(record_of(long_step, narrow_step - 1), 0, 1), MIG)
        return place(moved, side_list(own, 0), leavers(record_of(long_step, narrow_step + 1), 1, 1), MIG)

    for narrow_step in (-1, 1, 0):
        middle = settled(0, narrow_step)
        low = settled(-1, narrow_step)
        high = settled(1, narrow_step)
        inner[:, 0:OWN] = middle
        inner[:, OWN : OWN + GX] = (
            take_lanes(value_reader(low), 8, OWN // LANES, ghost_list(low, 0)) + unit_row(8, 0, -1.0)
        )
        inner[:, OWN + GX : INNER] = (
            take_lanes(value_reader(high), 8, OWN // LANES, ghost_list(high, 1)) + unit_row(8, 0, 1.0)
        )
        if narrow_step == 0:
            bundle[...] = middle
            table[:, 0:INNER] = inner[...]
            continue
        side = 0 if narrow_step < 0 else 1
        chosen = narrow_list(middle, side)
        taken = jnp.concatenate(
            [
                take_lanes(tile_reader(inner), 8, INNER // LANES, chosen[:, LANES * c : LANES * (c + 1)])
                for c in range(2)
            ],
            axis=1,
        )
        base = INNER + GY * side
        table[:, base : base + GY] = taken[:, 0:GY] + unit_row(8, 1, float(narrow_step))


def narrow_messages(par, table, rows, gy, one, two):
    p = par[1]
    for out, chosen in (
        (one, by_parity(p, gy[0:1, :], gy[1:2, :])),
        (two, by_parity(p, gy[1:2, :], gy[0:1, :])),
    ):
        for c in range(2):
            out[:, LANES * c : LANES * (c + 1)] = take_lanes(
                tile_reader(table), rows, INNER // LANES, chosen[:, LANES * c : LANES * (c + 1)]
            )


def inner_table(par, own, one, two, table):
    p = par[0]
    table[:, 0:OWN] = own
    table[:, OWN : OWN + GX] = by_parity(p, two[...], one[...])
    table[:, OWN + GX : INNER] = by_parity(p, one[...], two[...])


def outer_table(par, one, two, table):
    p = par[1]
    table[:, INNER : INNER + GY] = by_parity(p, two[:, 0:GY], one[:, 0:GY])
    table[:, INNER + GY : EXT] = by_parity(p, one[:, 0:GY], two[:, 0:GY])


def ghost_kernel(par, own, one_in, two_in, gy, one, two, table):
    inner_table(par, own[...], one_in, two_in, table)
    narrow_messages(par, table, own.shape[0], gy, one, two)


def product(left, right):
    return lax.dot_general(left, right, (((1,), (0,)), ((), ())), preferred_element_type=F32)


def centres():
    return lax.broadcasted_iota(I32, (NB, 1), 0).astype(F32) * (CENTRE_SPAN / (NB - 1))


def basis_rows(radial, last):
    high = radial.astype(BF16).astype(F32)
    return jnp.concatenate([high, radial - high, high, last], axis=0)


def slope_kernel(half, par, square, geo, basis, slope):
    lanes = slice(HALF * half, HALF * (half + 1))
    centre = centres()
    ones = jnp.ones((NB, HALF), F32)
    left = basis[...]

    def turn(n, carry):
        offset = square[pl.ds(n, 1), lanes] - centre
        weight = geo[3, pl.ds(n, 1), lanes]
        radial = jnp.exp(-(offset * offset))
        right = [basis_rows(radial, ones), basis_rows(-2.0 * offset * radial, 0.0 * ones)]
        both = product(left, jnp.concatenate(right, axis=1).astype(BF16))
        value = both[:, :HALF]
        gate = 0.5 * jnp.tanh(0.5 * value) + 0.5
        raw = value * gate
        slope[n] = weight * ((gate + raw * (1.0 - gate)) * both[:, HALF:] - raw * weight)
        return carry

    lax.fori_loop(0, NEI, turn, 0, unroll=UNROLL_ENV)


def grouped(ref, g):
    return jnp.concatenate([ref[GROUP * g + j] for j in range(GROUP)], axis=1)


def first_kernel(par, latent, pair_ahead, columns, first):
    left = pair_ahead[...]
    bias = columns[:, 0:1]

    def turn(g, carry):
        sums = product(left, grouped(latent, g))
        for j in range(GROUP):
            lanes = slice(OWN * j, OWN * (j + 1))
            first[GROUP * g + j] = sums[:H, lanes] + sums[H:, lanes] + bias
        return carry

    lax.fori_loop(0, NEI // GROUP, turn, 0)


def rise_kernel(par, dvalue, part, slope1, slope2, pair_back, rise):
    left = pair_back[...]

    def turn(g, carry):
        sums = product(left, grouped(dvalue, g))
        for j in range(GROUP):
            n = GROUP * g + j
            for half, slope in enumerate((slope1, slope2)):
                lanes = slice(HALF * half, HALF * (half + 1))
                wide = slice(OWN * j + HALF * half, OWN * j + HALF * (half + 1))
                dlatent = sums[:H, wide] + sums[H:, wide]
                total = jnp.sum(dlatent * slope[n], axis=0, keepdims=True)
                rise[pl.ds(n, 1), lanes] = total + part[pl.ds(n, 1), lanes]
        return carry

    lax.fori_loop(0, NEI // GROUP, turn, 0)


def env_kernel(
    narrow_count, par, records, nbr, basis, w_embed,
    own, gx, gy, embed, one, two, latent_out, geo, square, table, inner,
):
    settle(par, records, narrow_count, own, table, inner)
    for side in range(2):
        gx[side : side + 1, :] = ghost_list(own, side)
        gy[side : side + 1, :] = narrow_list(own, side)
    for b in range(OWN // LANES):
        lanes = slice(LANES * b, LANES * (b + 1))
        for q in range(NEI // 8):
            rows = slice(8 * q, 8 * q + 8)
            index = nbr[rows, lanes]
            low = index & (LANES - 1)
            high = index >> 7
            total = jnp.zeros((8, LANES), F32)
            for c in range(3):
                taken = jnp.zeros((8, LANES), F32)
                for g in range(GROUPS):
                    tile = jnp.broadcast_to(table[c : c + 1, LANES * g : LANES * (g + 1)], (8, LANES))
                    taken = jnp.where(high == g, lane_take(tile, low), taken)
                apart = taken - own[c : c + 1, lanes]
                geo[c, rows, lanes] = apart
                total = total + apart * apart
            square[rows, lanes] = total
            geo[3, rows, lanes] = jnp.where(index >= 0, 1.0 / (1.0 + total), 0.0)

    centre = centres()
    ones = jnp.ones((NB, HALF), F32)
    left = basis[...]
    for half in range(OWN // HALF):
        lanes = slice(HALF * half, HALF * (half + 1))

        def turn(n, gathered):
            offset = square[pl.ds(n, 1), lanes] - centre
            value = product(left, basis_rows(jnp.exp(-(offset * offset)), ones).astype(BF16))
            gate = 0.5 * jnp.tanh(0.5 * value) + 0.5
            latent = value * gate * geo[3, pl.ds(n, 1), lanes]
            high, low = half_split(latent)
            latent_out[n, 0:H, lanes] = high
            latent_out[n, H : 2 * H, lanes] = low
            return gathered + latent

        gathered = lax.fori_loop(0, NEI, turn, jnp.zeros((H, HALF), F32), unroll=UNROLL_ENV)
        environ = gathered * (1.0 / math.sqrt(NEI))
        embed[:, lanes] = jnp.dot(w_embed[...], environ, precision=HIGHEST, preferred_element_type=F32)
    p = par[0]
    reader = tile_reader(embed)
    one[...] = take_lanes(reader, EMB, OWN // LANES, by_parity(p, gx[0:1, :], gx[1:2, :]))
    two[...] = take_lanes(reader, EMB, OWN // LANES, by_parity(p, gx[1:2, :], gx[0:1, :]))


def hot_rows(low_row):
    level = lax.broadcasted_iota(I32, (HALF, low_row.shape[1]), 0)
    return jnp.where(level == low_row, 1.0, 0.0).astype(BF16)


def level_rows(value, high_row):
    pieces = []
    for k in range(LEVELS):
        mask = jnp.where(high_row == k, 1.0, 0.0).astype(BF16)
        pieces.append(value * mask)
    return jnp.concatenate(pieces, axis=0)


def pair_kernel(
    par, own, gx1, gx2, gy1, gy2, nbr, first, geo, ahead, back, columns,
    dvalue_out, part, inner, one, two, table, spread_sum, own_sum,
):
    inner_table(par, own[...], gx1, gx2, table)
    outer_table(par, gy1, gy2, table)
    spread_sum[...] = jnp.zeros(spread_sum.shape, F32)
    own_sum[...] = jnp.zeros(own_sum.shape, F32)
    left = ahead[...]
    right_back = back[...]
    readout = columns[:, 1:2]

    def scatter(g, joined):
        index = jnp.concatenate([nbr[pl.ds(GROUP * g + j, 1), :] for j in range(GROUP)], axis=1)
        spread_sum[...] += lax.dot_general(
            level_rows(joined, index >> 8), hot_rows(index & (HALF - 1)),
            (((1,), (1,)), ((), ())), preferred_element_type=F32,
        )

    def chunk(n, lanes, width):
        index = nbr[pl.ds(n, 1), lanes]
        weight = geo[3, pl.ds(n, 1), lanes]
        partner = jnp.concatenate(
            [
                take_lanes(tile_reader(table), EMB, GROUPS, index[:, LANES * c : LANES * (c + 1)])
                for c in range(width // LANES)
            ],
            axis=1,
        )
        embed_own = own[:, lanes]
        product_high, product_low = half_split(partner * embed_own)
        sums = product(left, jnp.concatenate([product_high, product_low], axis=0))
        value = first[n, :, lanes] + sums[:H] + sums[H:]
        gate = 0.5 * jnp.tanh(0.5 * value) + 0.5
        hidden = value * gate
        dvalue = (gate + hidden * (1.0 - gate)) * (readout * weight)
        dhigh, dlow = half_split(dvalue)
        dvalue = jnp.concatenate([dhigh, dlow], axis=0)
        dvalue_out[n, :, lanes] = dvalue
        sums = product(right_back, dvalue)
        dproduct = sums[:EMB] + sums[EMB:]
        part[pl.ds(n, 1), lanes] = -(weight * weight) * jnp.sum(hidden * readout, axis=0, keepdims=True)
        high, low = half_split(dproduct * embed_own)
        return dproduct * partner, jnp.concatenate([high, low], axis=0)

    def turn(g, joined):
        scatter(jnp.maximum(g - 1, 0), joined)
        pieces = {}
        for part in range(OWN // CHUNK):
            lanes = slice(CHUNK * part, CHUNK * (part + 1))
            grown = own_sum[:, lanes]
            for j in range(GROUP):
                more, piece = chunk(GROUP * g + j, lanes, CHUNK)
                grown = grown + more
                pieces[j, part] = piece
            own_sum[:, lanes] = grown
        return jnp.concatenate([pieces[j, part] for j in range(GROUP) for part in range(OWN // CHUNK)], axis=1)

    joined = lax.fori_loop(0, NEI // GROUP, turn, jnp.zeros((2 * EMB, GROUP * OWN), BF16))
    scatter(NEI // GROUP - 1, joined)
    for k in range(LEVELS):
        base = 2 * EMB * k
        width = min(HALF, EXT - HALF * k)
        table[:, HALF * k : HALF * k + width] = (
            spread_sum[base : base + EMB, :width] + spread_sum[base + EMB : base + 2 * EMB, :width]
        )
    inner[:, 0:OWN] = table[:, 0:OWN] + own_sum[...]
    inner[:, OWN:INNER] = table[:, OWN:INNER]
    outer_messages(par, table, one, two)


def outer_messages(par, table, one, two):
    p = par[1]
    down = table[:, INNER : INNER + GY]
    up = table[:, INNER + GY : EXT]
    one[...] = by_parity(p, up, down)
    two[...] = by_parity(p, down, up)


def fold_narrow(par, inner, one, two, gy):
    p = par[1]
    from_upper = by_parity(p, one[...], two[...])
    from_lower = by_parity(p, two[...], one[...])
    return (
        inner[...]
        + spread(from_upper, gy[0:1, 0:GY], INNER)
        + spread(from_lower, gy[1:2, 0:GY], INNER)
    )


def fold_long(par, own, one, two, gx):
    p = par[0]
    from_upper = by_parity(p, one[...], two[...])
    from_lower = by_parity(p, two[...], one[...])
    return own[...] + spread(from_upper, gx[0:1, :], OWN) + spread(from_lower, gx[1:2, :], OWN)


def fold_kernel(par, inner, one_in, two_in, gy, own, one, two):
    total = fold_narrow(par, inner, one_in, two_in, gy)
    own[...] = total[:, 0:OWN]
    down = total[:, OWN : OWN + GX]
    up = total[:, OWN + GX : INNER]
    p = par[0]
    one[...] = by_parity(p, up, down)
    two[...] = by_parity(p, down, up)


def force_kernel(
    par, own_in, gx1, gx2, gx, w_back, slope1, slope2, rise, geo, nbr,
    inner, one, two, table, spread_sum, pushes, grown,
):
    grad = fold_long(par, own_in, gx1, gx2, gx)
    grown[...] = jnp.dot(w_back[...], grad, precision=HIGHEST, preferred_element_type=F32) * (1.0 / math.sqrt(NEI))
    spread_sum[...] = jnp.zeros(spread_sum.shape, F32)
    pushes[...] = jnp.zeros(pushes.shape, F32)

    def turn(g, carry):
        lifted = []
        hot = []
        pushed = pushes[...]
        for j in range(GROUP):
            n = GROUP * g + j
            rate = jnp.concatenate(
                [
                    jnp.sum(slope[n] * grown[:, HALF * h : HALF * (h + 1)], axis=0, keepdims=True)
                    for h, slope in enumerate((slope1, slope2))
                ],
                axis=1,
            )
            twice = 2.0 * (rate + rise[pl.ds(n, 1), :])
            push = [geo[c, pl.ds(n, 1), :] * twice for c in range(3)]
            highs = [v.astype(BF16).astype(F32) for v in push]
            rows = highs + [v - h for v, h in zip(push, highs)]
            value = jnp.concatenate(rows + [jnp.zeros((2, OWN), F32)], axis=0)
            pushed = pushed + value
            index = nbr[pl.ds(n, 1), :]
            high_row = index >> 8
            hot.append(hot_rows(index & (HALF - 1)))
            lifted.append(
                jnp.concatenate([jnp.where(high_row == k, value, 0.0) for k in range(LEVELS)], axis=0).astype(BF16)
            )
        pushes[...] = pushed
        spread_sum[...] += lax.dot_general(
            jnp.concatenate(lifted, axis=1), jnp.concatenate(hot, axis=1), (((1,), (1,)), ((), ())), preferred_element_type=F32
        )
        return carry

    lax.fori_loop(0, NEI // GROUP, turn, 0)
    table[...] = jnp.zeros(table.shape, F32)
    for k in range(LEVELS):
        width = min(HALF, EXT - HALF * k)
        table[0:3, HALF * k : HALF * k + width] = (
            spread_sum[8 * k : 8 * k + 3, :width] + spread_sum[8 * k + 3 : 8 * k + 6, :width]
        )
    table[0:3, 0:OWN] = table[0:3, 0:OWN] - pushes[0:3, :] - pushes[3:6, :]
    inner[...] = table[:, 0:INNER]
    outer_messages(par, table, one, two)


def final_kernel(par, own, one, two, gx, bundle, pos_out, vel_out, frc_out):
    forces = -fold_long(par, own, one, two, gx)[0:3, :]
    pos_out[...] = bundle[0:3, :]
    vel_out[...] = bundle[3:6, :] + (0.5 * TIME_STEP) * forces
    frc_out[...] = forces


def call(kernel, name, shapes, scratch, *operands, far=(), limit=BIG):
    specs = [pl.BlockSpec(memory_space=pltpu.HBM if k in far else pltpu.VMEM) for k in range(len(operands))]

    def placed(*refs):
        column = lax.axis_index("gy")
        kernel((lax.rem(lax.axis_index("gx"), 2), lax.rem(column, 2), column), *refs)

    return pl.pallas_call(
        placed,
        name=name,
        out_shape=[jax.ShapeDtypeStruct(shape, kind) for shape, kind in shapes],
        in_specs=specs,
        out_specs=[pl.BlockSpec(memory_space=pltpu.VMEM)] * len(shapes),
        scratch_shapes=[
            pltpu.SemaphoreType.DMA(shape) if kind is None else pltpu.VMEM(shape, kind) for shape, kind in scratch
        ],
        compiler_params=pltpu.CompilerParams(vmem_limit_bytes=limit),
    )(*operands)


def holds(*arrays):
    return [(a.shape, a.dtype) for a in arrays] + [((len(arrays),), None)]


def swap(axis, first):
    count = lax.axis_size(axis)
    offset = 0 if first else 1
    route = []
    for i in range(count):
        route.append((i, (((i + offset) ^ 1) - offset) % count))
    return route


def exchange(axis, one, two):
    return (
        lax.ppermute(one, axis, swap(axis, True)),
        lax.ppermute(two, axis, swap(axis, False)),
    )


def on_device(
    positions, velocities, forces, neighbours, ghost_x, ghost_y, migrate_x, migrate_y,
    w_basis, b_basis, w_embed, w_pair, w_mix, b_pair, w_out,
):
    narrow_count = lax.axis_size("gy")
    tile = ((8, LANES), F32)
    wide = ((8, OWN), F32)
    given = (positions, velocities, forces, ghost_x, ghost_y, migrate_x, migrate_y)
    record, message = call(
        start_kernel, "start", [wide, tile], holds(*given), *given,
        far=range(len(given)), limit=WHOLE,
    )
    given = (
        w_basis.T, w_pair, w_mix.T, w_embed, jnp.stack([b_basis, b_pair, w_out]),
    )
    doubled = ((2 * H, 2 * H), BF16)
    near, basis, pair_ahead, mix_ahead, pair_back, mix_back, w_ahead, w_back, columns = call(
        prepare_kernel,
        "prepare",
        [
            ((NEI, OWN), I32), ((H, 4 * NB), BF16), doubled, ((2 * H, 2 * EMB), BF16), doubled, ((2 * EMB, 2 * H), BF16),
            ((EMB, H), F32), ((H, EMB), F32), ((H, NB), F32),
        ],
        holds(*given), neighbours, *given, far=range(1, len(given) + 1),
    )
    message = lax.ppermute(message, "gx", swap("gx", True))
    mine = jnp.concatenate([record, message], axis=1)
    joined = lax.ppermute(mine, "gx", swap("gx", False))
    group = 2 * narrow_count
    (records,) = call(cross_kernel, "cross", [((group, 16, OWN), F32)], [], mine, joined)
    members = [list(range(group * k, group * (k + 1))) for k in range(lax.axis_size("gx") // 2)]
    records = lax.all_to_all(records, ("gx", "gy"), 0, 0, axis_index_groups=members)

    bundle, gx, gy, embed, one, two, latent, geo, square = call(
        lambda *refs: env_kernel(narrow_count, *refs),
        "env",
        [
            wide, ((2, GX), I32), ((2, HALF), I32), ((EMB, OWN), F32), ((EMB, GX), F32), ((EMB, GX), F32),
            ((NEI, 2 * H, OWN), BF16), ((4, NEI, OWN), F32), ((NEI, OWN), F32),
        ],
        [((8, EXT), F32), ((8, INNER), F32)],
        records.reshape(2 * group, 8, OWN), near, basis, w_ahead,
    )
    (first,) = call(first_kernel, "first", [((NEI, H, OWN), F32)], [], latent, pair_ahead, columns)
    slopes = [
        call(
            lambda *refs, half=half: slope_kernel(half, *refs), f"slope{half}", [((NEI, H, HALF), F32)], [],
            square, geo, basis,
        )[0]
        for half in range(OWN // HALF)
    ]
    ex = exchange("gx", one, two)
    *ex, slopes[0] = lax.optimization_barrier((*ex, slopes[0]))
    message = ((EMB, HALF), F32)
    one, two = call(
        ghost_kernel, "ghost_embed", [message, message], [((EMB, INNER), F32)],
        embed, *ex, gy,
    )
    ey = exchange("gy", one, two)
    message = ((EMB, GY), F32)
    dvalue, part, inner, one, two = call(
        pair_kernel,
        "pair",
        [((NEI, 2 * H, OWN), BF16), ((NEI, OWN), F32), ((EMB, INNER), F32), message, message],
        [((EMB, EXT), F32), ((LEVELS * 2 * EMB, HALF), F32), ((EMB, OWN), F32)],
        embed, *ex, *ey, near, first, geo, mix_ahead, mix_back, columns,
    )
    one, two = exchange("gy", one, two)
    one, two, slopes[1] = lax.optimization_barrier((one, two, slopes[1]))
    (rise,) = call(rise_kernel, "rise", [((NEI, OWN), F32)], [], dvalue, part, *slopes, pair_back)
    message = ((EMB, GX), F32)
    own, one, two = call(
        fold_kernel, "fold_embed", [((EMB, OWN), F32), message, message], [], inner, one, two, gy
    )
    one, two = exchange("gx", one, two)
    message = ((8, GY), F32)
    inner, one, two = call(
        force_kernel,
        "force",
        [((8, INNER), F32), message, message],
        [((8, EXT), F32), ((8 * LEVELS, HALF), F32), ((8, OWN), F32), ((H, OWN), F32)],
        own, one, two, gx, w_back, *slopes, rise, geo, near,
    )
    one, two = exchange("gy", one, two)
    own, one, two = call(fold_kernel, "fold_force", [wide, tile, tile], [], inner, one, two, gy)
    one, two = exchange("gx", one, two)
    flat = ((3, OWN), F32)
    return tuple(call(final_kernel, "final", [flat, flat, flat], [], own, one, two, gx, bundle))


def solution(mesh):
    both = ("gx", "gy")
    flat = P(None, both)
    stacked = P(None, None, both)
    return jax.shard_map(
        on_device,
        mesh=mesh,
        in_specs=(flat,) * 3 + (stacked,) * 5 + (P(),) * 7,
        out_specs=(flat,) * 3,
        check_vma=False,
    )
```

```python
import math

import jax
import jax.numpy as jnp
from jax import lax
from jax.experimental import pallas as pl
from jax.experimental.pallas import tpu as pltpu
from jax.sharding import PartitionSpec as P

F32 = jnp.float32
BF16 = jnp.bfloat16
I32 = jnp.int32

TIME_STEP = 0.05
CENTRE_SPAN = 3.0
HIGHEST = lax.Precision.HIGHEST

NB = 8
NEI = 32
H = 64
EMB = 32
OWN = 512
GX = 128
GY = 192
MIG = 8
LANES = 128
INNER = OWN + 2 * GX
EXT = INNER + 2 * GY
GROUPS = EXT // LANES
HALF = 256
LEVELS = -(-EXT // HALF)
BIG = 24 * 1024 * 1024
WHOLE = 60 * 1024 * 1024
GROUP = 4
CHUNK = 512
UNROLL_ENV = 8


def half_split(value):
    high = value.astype(BF16)
    low = (value - high.astype(F32)).astype(BF16)
    return high, low


def third_split(value):
    high = value.astype(BF16)
    rest = value - high.astype(F32)
    middle = rest.astype(BF16)
    low = (rest - middle.astype(F32)).astype(BF16)
    return high, middle, low


def lane_take(table, index):
    return jnp.take_along_axis(table, index, axis=1, mode="promise_in_bounds")


def take_lanes(read, rows, groups, index_row):
    low = jnp.broadcast_to(index_row & (LANES - 1), (8, LANES))
    high = jnp.broadcast_to(index_row >> 7, (8, LANES))
    pieces = []
    for r in range(rows // 8):
        taken = jnp.zeros((8, LANES), F32)
        for g in range(groups):
            taken = jnp.where(high == g, lane_take(read(r, g), low), taken)
        pieces.append(taken)
    return jnp.concatenate(pieces, axis=0) if len(pieces) > 1 else pieces[0]


def tile_reader(ref):
    return lambda r, g: ref[8 * r : 8 * r + 8, LANES * g : LANES * (g + 1)]


def spread(values, lists, width):
    count = values.shape[1]
    hot = jnp.where(lax.broadcasted_iota(I32, (width, count), 0) == lists, 1.0, 0.0).astype(BF16)
    total = None
    for part in third_split(values):
        piece = lax.dot_general(part, hot, (((1,), (1,)), ((), ())), preferred_element_type=F32)
        total = piece if total is None else total + piece
    return total


def by_parity(parity, even, odd):
    return jnp.where(parity == 0, even, odd)


def unit_row(rows, row, amount):
    return jnp.where(lax.broadcasted_iota(I32, (rows, 1), 0) == row, amount, 0.0)


def place(spots, values, slots, from_lower, from_upper, base=0):
    for k in range(MIG):
        down = slice(MIG + k, MIG + k + 1)
        up = slice(k, k + 1)
        message_up = from_lower[:, base + k : base + k + 1]
        message_down = from_upper[:, base + MIG + k : base + MIG + k + 1]
        values = jnp.where(spots == slots[:, down], message_up, values)
        values = jnp.where(spots == slots[:, up], message_down, values)
    return values


def value_reader(value):
    return lambda r, g: value[8 * r : 8 * r + 8, LANES * g : LANES * (g + 1)]


LONG_SLOTS = slice(2 * GX, 2 * GX + LANES)
NARROW_SLOTS = slice(2 * GX + LANES, 2 * GX + 2 * LANES)


def ghost_list(record, side):
    return record[6:7, GX * side : GX * (side + 1)].astype(I32)


def narrow_list(record, side):
    return record[7:8, HALF * side : HALF * (side + 1)].astype(I32)


def leavers(record, lanes, row):
    lane = lax.broadcasted_iota(I32, (8, LANES), 1) & (2 * MIG - 1)
    shift = jnp.where(lane < MIG, -1.0, 1.0)
    rows = lax.broadcasted_iota(I32, (8, LANES), 0)
    taken = take_lanes(value_reader(record), 8, OWN // LANES, record[6:7, lanes].astype(I32))
    return taken + jnp.where(rows == row, shift, 0.0)


def fetch(sources, targets, sems):
    copies = [pltpu.make_async_copy(src, dst, sems.at[k]) for k, (src, dst) in enumerate(zip(sources, targets))]
    for copy in copies:
        copy.start()
    for copy in copies:
        copy.wait()


def prepare_kernel(
    par, neighbours, basis_t, pair, mix_t, w_embed, vectors, near, basis, pair_ahead, mix_ahead, pair_back, mix_back, w_ahead, w_back, columns, *scratch
):
    held = scratch[:-1]
    near[...] = neighbours[0]
    fetch((basis_t, pair, mix_t, w_embed, vectors), held, scratch[-1])
    basis_t, pair, mix_t, w_embed, vectors = held
    b_basis = vectors[0:1, :]
    high, low = half_split(basis_t[...])
    high, low = high.astype(F32), low.astype(F32)
    parts = [part.astype(F32) for part in third_split(b_basis)]
    parts = jnp.concatenate(parts + [jnp.zeros((NB - 3, H), F32)], axis=0)
    basis[...] = jnp.concatenate([high, high, low, parts], axis=0).T.astype(BF16)
    rows = jnp.concatenate([vectors[1:3, :], jnp.zeros((NB - 2, H), F32)], axis=0)
    columns[...] = rows.T
    w_ahead[...] = w_embed[...]
    w_back[...] = w_embed[...].T
    for layer_t, ahead, back in ((pair[...].T, pair_ahead, pair_back), (mix_t[...], mix_ahead, mix_back)):
        high, low = half_split(layer_t)
        high, low = high.astype(F32), low.astype(F32)
        nothing = jnp.zeros(high.shape, F32)
        back[...] = jnp.concatenate(
            [jnp.concatenate([high, high], axis=1), jnp.concatenate([low, nothing], axis=1)], axis=0
        ).astype(BF16)
        ahead[0:H, :] = jnp.concatenate([high, high], axis=0).T.astype(BF16)
        ahead[H : 2 * H, :] = jnp.concatenate([low, nothing], axis=0).T.astype(BF16)


def start_kernel(par, pos, vel, frc, gx, gy, mx, my, record, message, *scratch):
    held = scratch[:-1]
    fetch((pos, vel, frc, gx, gy, mx, my), held, scratch[-1])
    pos, vel, frc, gx, gy, mx, my = held
    speeds = vel[...] + (0.5 * TIME_STEP) * frc[...]
    record[0:3, :] = pos[...] + TIME_STEP * speeds
    record[3:6, :] = speeds
    record[6:8, :] = jnp.zeros((2, OWN), F32)
    for side in range(2):
        long_start = LONG_SLOTS.start + MIG * side
        record[6:7, GX * side : GX * (side + 1)] = gx[0, side : side + 1, :].astype(F32)
        record[6:7, long_start : long_start + MIG] = mx[0, side : side + 1, :].astype(F32)
        for again in range(2):
            start = NARROW_SLOTS.start + MIG * (side + 2 * again)
            record[6:7, start : start + MIG] = my[0, side : side + 1, :].astype(F32)
        record[7:8, HALF * side : HALF * side + GY] = gy[0, side : side + 1, :].astype(F32)
    message[...] = leavers(record[...], LONG_SLOTS, 0)


def crossed(record, from_lower, from_upper):
    lane = lax.broadcasted_iota(I32, record.shape, 1)
    moved = place(lane, record, record[6:7, LONG_SLOTS].astype(I32), from_lower, from_upper)
    return jnp.where(lax.broadcasted_iota(I32, record.shape, 0) < 6, moved, record)


AREAS = [slice(LANES * k, LANES * (k + 1)) for k in range(4)]


def cross_kernel(par, kept, joined, own_out, out, block):
    p = par[0]
    own = kept[:, 0:OWN]
    other = joined[:, 0:OWN]
    near_side = kept[:, OWN : OWN + LANES]
    far_side = joined[:, OWN : OWN + LANES]
    from_other = leavers(other, LONG_SLOTS, 0)
    from_own = leavers(own, LONG_SLOTS, 0)
    own = crossed(own, by_parity(p, from_other, near_side), by_parity(p, near_side, from_other))
    other = crossed(other, by_parity(p, far_side, from_own), by_parity(p, from_own, far_side))
    own_out[...] = own
    block[0:3, :] = own[0:3, :]
    block[3:4, :] = own[7:8, :]
    for area, record in ((AREAS[0], other), (AREAS[1], own)):
        chosen = by_parity(p, ghost_list(record, 0), ghost_list(record, 1))
        block[4:7, area] = take_lanes(value_reader(record), 8, OWN // LANES, chosen)[0:3, :]
        block[7:8, area] = chosen.astype(F32)
    lane = lax.broadcasted_iota(I32, (3, LANES), 1)
    for area, record in ((AREAS[2], own), (AREAS[3], other)):
        leave = leavers(record, NARROW_SLOTS, 1)
        block[4:7, area] = jnp.where(lane < 2 * MIG, leave[0:3, :], leave[3:6, :])
        block[7:8, area] = record[6:7, NARROW_SLOTS]
    for b in range(out.shape[0]):
        out[b] = block[...]


def settle(par, blocks, record, narrow_count, bundle, table, inner):
    p = par[0]

    def number(member, narrow_step):
        return member * narrow_count + lax.rem(par[2] + (narrow_step + narrow_count), narrow_count)

    def settled(member, narrow_step, spots, values, leave, base=0):
        slots = blocks[number(member, narrow_step), 7:8, leave].astype(I32)
        from_lower = blocks[number(member, narrow_step - 1), 4:7, leave]
        from_upper = blocks[number(member, narrow_step + 1), 4:7, leave]
        return place(spots, values, slots, from_lower, from_upper, base)

    lane = lax.broadcasted_iota(I32, (3, OWN), 1)
    inner[...] = jnp.zeros(inner.shape, F32)
    toward = by_parity(p, -1.0, 1.0)
    for narrow_step in (-1, 1, 0):
        here = number(p, narrow_step)
        there = number(1 - p, narrow_step)
        middle = settled(p, narrow_step, lane, blocks[here, 0:3, :], AREAS[2])
        second = settled(
            p, narrow_step, blocks[here, 7:8, AREAS[0]].astype(I32), blocks[here, 4:7, AREAS[0]], AREAS[3]
        ) + unit_row(3, 0, toward)
        first = settled(
            1 - p, narrow_step, blocks[there, 7:8, AREAS[1]].astype(I32), blocks[there, 4:7, AREAS[1]], AREAS[2]
        ) - unit_row(3, 0, toward)
        inner[0:3, 0:OWN] = middle
        inner[0:3, OWN : OWN + GX] = by_parity(p, second, first)
        inner[0:3, OWN + GX : INNER] = by_parity(p, first, second)
        if narrow_step == 0:
            bundle[0:3, :] = middle
            bundle[3:6, :] = settled(p, 0, lane, record[3:6, :], AREAS[2], 2 * MIG)
            bundle[6:8, :] = record[6:8, :]
            table[:, 0:INNER] = inner[...]
            continue
        side = 0 if narrow_step < 0 else 1
        chosen = blocks[here, 3:4, HALF * side : HALF * (side + 1)].astype(I32)
        taken = jnp.concatenate(
            [
                take_lanes(tile_reader(inner), 8, INNER // LANES, chosen[:, LANES * c : LANES * (c + 1)])
                for c in range(2)
            ],
            axis=1,
        )
        base = INNER + GY * side
        table[:, base : base + GY] = taken[:, 0:GY] + unit_row(8, 1, float(narrow_step))


def narrow_messages(par, table, rows, gy, one, two):
    p = par[1]
    for out, chosen in (
        (one, by_parity(p, gy[0:1, :], gy[1:2, :])),
        (two, by_parity(p, gy[1:2, :], gy[0:1, :])),
    ):
        for c in range(2):
            out[:, LANES * c : LANES * (c + 1)] = take_lanes(
                tile_reader(table), rows, INNER // LANES, chosen[:, LANES * c : LANES * (c + 1)]
            )


def inner_table(par, own, one, two, table):
    p = par[0]
    table[:, 0:OWN] = own
    table[:, OWN : OWN + GX] = by_parity(p, two[...], one[...])
    table[:, OWN + GX : INNER] = by_parity(p, one[...], two[...])


def outer_table(par, one, two, table):
    p = par[1]
    table[:, INNER : INNER + GY] = by_parity(p, two[:, 0:GY], one[:, 0:GY])
    table[:, INNER + GY : EXT] = by_parity(p, one[:, 0:GY], two[:, 0:GY])


def ghost_kernel(par, own, one_in, two_in, gy, one, two, table):
    inner_table(par, own[...], one_in, two_in, table)
    narrow_messages(par, table, own.shape[0], gy, one, two)


def product(left, right):
    return lax.dot_general(left, right, (((1,), (0,)), ((), ())), preferred_element_type=F32)


def centres():
    return lax.broadcasted_iota(I32, (NB, 1), 0).astype(F32) * (CENTRE_SPAN / (NB - 1))


def basis_rows(radial, last):
    high = radial.astype(BF16).astype(F32)
    return jnp.concatenate([high, radial - high, high, last], axis=0)


def slope_kernel(half, par, square, geo, basis, slope):
    lanes = slice(HALF * half, HALF * (half + 1))
    centre = centres()
    ones = jnp.ones((NB, HALF), F32)
    left = basis[...]

    def turn(n, carry):
        offset = square[pl.ds(n, 1), lanes] - centre
        weight = geo[3, pl.ds(n, 1), lanes]
        radial = jnp.exp(-(offset * offset))
        right = [basis_rows(radial, ones), basis_rows(-2.0 * offset * radial, 0.0 * ones)]
        both = product(left, jnp.concatenate(right, axis=1).astype(BF16))
        value = both[:, :HALF]
        gate = 0.5 * jnp.tanh(0.5 * value) + 0.5
        raw = value * gate
        slope[n] = weight * ((gate + raw * (1.0 - gate)) * both[:, HALF:] - raw * weight)
        return carry

    lax.fori_loop(0, NEI, turn, 0, unroll=UNROLL_ENV)


def grouped(ref, g):
    return jnp.concatenate([ref[GROUP * g + j] for j in range(GROUP)], axis=1)


def first_kernel(par, latent, pair_ahead, columns, first):
    left = pair_ahead[...]
    bias = columns[:, 0:1]

    def turn(g, carry):
        sums = product(left, grouped(latent, g))
        for j in range(GROUP):
            lanes = slice(OWN * j, OWN * (j + 1))
            first[GROUP * g + j] = sums[:H, lanes] + sums[H:, lanes] + bias
        return carry

    lax.fori_loop(0, NEI // GROUP, turn, 0)


def rise_kernel(par, dvalue, part, slope1, slope2, pair_back, rise):
    left = pair_back[...]

    def turn(g, carry):
        sums = product(left, grouped(dvalue, g))
        for j in range(GROUP):
            n = GROUP * g + j
            for half, slope in enumerate((slope1, slope2)):
                lanes = slice(HALF * half, HALF * (half + 1))
                wide = slice(OWN * j + HALF * half, OWN * j + HALF * (half + 1))
                dlatent = sums[:H, wide] + sums[H:, wide]
                total = jnp.sum(dlatent * slope[n], axis=0, keepdims=True)
                rise[pl.ds(n, 1), lanes] = total + part[pl.ds(n, 1), lanes]
        return carry

    lax.fori_loop(0, NEI // GROUP, turn, 0)


def env_kernel(
    narrow_count, par, blocks, record, nbr, basis, w_embed,
    own, gx, gy, embed, one, two, latent_out, geo, square, table, inner,
):
    settle(par, blocks, record, narrow_count, own, table, inner)
    for side in range(2):
        gx[side : side + 1, :] = ghost_list(own, side)
        gy[side : side + 1, :] = narrow_list(own, side)
    for b in range(OWN // LANES):
        lanes = slice(LANES * b, LANES * (b + 1))
        for q in range(NEI // 8):
            rows = slice(8 * q, 8 * q + 8)
            index = nbr[rows, lanes]
            low = index & (LANES - 1)
            high = index >> 7
            total = jnp.zeros((8, LANES), F32)
            for c in range(3):
                taken = jnp.zeros((8, LANES), F32)
                for g in range(GROUPS):
                    tile = jnp.broadcast_to(table[c : c + 1, LANES * g : LANES * (g + 1)], (8, LANES))
                    taken = jnp.where(high == g, lane_take(tile, low), taken)
                apart = taken - own[c : c + 1, lanes]
                geo[c, rows, lanes] = apart
                total = total + apart * apart
            square[rows, lanes] = total
            geo[3, rows, lanes] = jnp.where(index >= 0, 1.0 / (1.0 + total), 0.0)

    centre = centres()
    ones = jnp.ones((NB, HALF), F32)
    left = basis[...]
    for half in range(OWN // HALF):
        lanes = slice(HALF * half, HALF * (half + 1))

        def turn(n, gathered):
            offset = square[pl.ds(n, 1), lanes] - centre
            value = product(left, basis_rows(jnp.exp(-(offset * offset)), ones).astype(BF16))
            gate = 0.5 * jnp.tanh(0.5 * value) + 0.5
            latent = value * gate * geo[3, pl.ds(n, 1), lanes]
            high, low = half_split(latent)
            latent_out[n, 0:H, lanes] = high
            latent_out[n, H : 2 * H, lanes] = low
            return gathered + latent

        gathered = lax.fori_loop(0, NEI, turn, jnp.zeros((H, HALF), F32), unroll=UNROLL_ENV)
        environ = gathered * (1.0 / math.sqrt(NEI))
        embed[:, lanes] = jnp.dot(w_embed[...], environ, precision=HIGHEST, preferred_element_type=F32)
    p = par[0]
    reader = tile_reader(embed)
    one[...] = take_lanes(reader, EMB, OWN // LANES, by_parity(p, gx[0:1, :], gx[1:2, :]))
    two[...] = take_lanes(reader, EMB, OWN // LANES, by_parity(p, gx[1:2, :], gx[0:1, :]))


def hot_rows(low_row):
    level = lax.broadcasted_iota(I32, (HALF, low_row.shape[1]), 0)
    return jnp.where(level == low_row, 1.0, 0.0).astype(BF16)


def level_rows(value, high_row):
    pieces = []
    for k in range(LEVELS):
        mask = jnp.where(high_row == k, 1.0, 0.0).astype(BF16)
        pieces.append(value * mask)
    return jnp.concatenate(pieces, axis=0)


def pair_kernel(
    par, own, gx1, gx2, gy1, gy2, nbr, first, geo, ahead, back, columns,
    dvalue_out, part, inner, one, two, table, spread_sum, own_sum,
):
    inner_table(par, own[...], gx1, gx2, table)
    outer_table(par, gy1, gy2, table)
    spread_sum[...] = jnp.zeros(spread_sum.shape, F32)
    own_sum[...] = jnp.zeros(own_sum.shape, F32)
    left = ahead[...]
    right_back = back[...]
    readout = columns[:, 1:2]

    def scatter(g, joined):
        index = jnp.concatenate([nbr[pl.ds(GROUP * g + j, 1), :] for j in range(GROUP)], axis=1)
        spread_sum[...] += lax.dot_general(
            level_rows(joined, index >> 8), hot_rows(index & (HALF - 1)),
            (((1,), (1,)), ((), ())), preferred_element_type=F32,
        )

    def chunk(n, lanes, width):
        index = nbr[pl.ds(n, 1), lanes]
        weight = geo[3, pl.ds(n, 1), lanes]
        partner = jnp.concatenate(
            [
                take_lanes(tile_reader(table), EMB, GROUPS, index[:, LANES * c : LANES * (c + 1)])
                for c in range(width // LANES)
            ],
            axis=1,
        )
        embed_own = own[:, lanes]
        product_high, product_low = half_split(partner * embed_own)
        sums = product(left, jnp.concatenate([product_high, product_low], axis=0))
        value = first[n, :, lanes] + sums[:H] + sums[H:]
        gate = 0.5 * jnp.tanh(0.5 * value) + 0.5
        hidden = value * gate
        dvalue = (gate + hidden * (1.0 - gate)) * (readout * weight)
        dhigh, dlow = half_split(dvalue)
        dvalue = jnp.concatenate([dhigh, dlow], axis=0)
        dvalue_out[n, :, lanes] = dvalue
        sums = product(right_back, dvalue)
        dproduct = sums[:EMB] + sums[EMB:]
        part[pl.ds(n, 1), lanes] = -(weight * weight) * jnp.sum(hidden * readout, axis=0, keepdims=True)
        high, low = half_split(dproduct * embed_own)
        return dproduct * partner, jnp.concatenate([high, low], axis=0)

    def turn(g, joined):
        scatter(jnp.maximum(g - 1, 0), joined)
        pieces = {}
        for part in range(OWN // CHUNK):
            lanes = slice(CHUNK * part, CHUNK * (part + 1))
            grown = own_sum[:, lanes]
            for j in range(GROUP):
                more, piece = chunk(GROUP * g + j, lanes, CHUNK)
                grown = grown + more
                pieces[j, part] = piece
            own_sum[:, lanes] = grown
        return jnp.concatenate([pieces[j, part] for j in range(GROUP) for part in range(OWN // CHUNK)], axis=1)

    joined = lax.fori_loop(0, NEI // GROUP, turn, jnp.zeros((2 * EMB, GROUP * OWN), BF16))
    scatter(NEI // GROUP - 1, joined)
    for k in range(LEVELS):
        base = 2 * EMB * k
        width = min(HALF, EXT - HALF * k)
        table[:, HALF * k : HALF * k + width] = (
            spread_sum[base : base + EMB, :width] + spread_sum[base + EMB : base + 2 * EMB, :width]
        )
    inner[:, 0:OWN] = table[:, 0:OWN] + own_sum[...]
    inner[:, OWN:INNER] = table[:, OWN:INNER]
    outer_messages(par, table, one, two)


def outer_messages(par, table, one, two):
    p = par[1]
    down = table[:, INNER : INNER + GY]
    up = table[:, INNER + GY : EXT]
    one[...] = by_parity(p, up, down)
    two[...] = by_parity(p, down, up)


def fold_narrow(par, inner, one, two, gy):
    p = par[1]
    from_upper = by_parity(p, one[...], two[...])
    from_lower = by_parity(p, two[...], one[...])
    return (
        inner[...]
        + spread(from_upper, gy[0:1, 0:GY], INNER)
        + spread(from_lower, gy[1:2, 0:GY], INNER)
    )


def fold_long(par, own, one, two, gx):
    p = par[0]
    from_upper = by_parity(p, one[...], two[...])
    from_lower = by_parity(p, two[...], one[...])
    return own[...] + spread(from_upper, gx[0:1, :], OWN) + spread(from_lower, gx[1:2, :], OWN)


def fold_kernel(par, inner, one_in, two_in, gy, own, one, two):
    total = fold_narrow(par, inner, one_in, two_in, gy)
    own[...] = total[:, 0:OWN]
    down = total[:, OWN : OWN + GX]
    up = total[:, OWN + GX : INNER]
    p = par[0]
    one[...] = by_parity(p, up, down)
    two[...] = by_parity(p, down, up)


def force_kernel(
    par, own_in, gx1, gx2, gx, w_back, slope1, slope2, rise, geo, nbr,
    inner, one, two, table, spread_sum, pushes, grown,
):
    grad = fold_long(par, own_in, gx1, gx2, gx)
    grown[...] = jnp.dot(w_back[...], grad, precision=HIGHEST, preferred_element_type=F32) * (1.0 / math.sqrt(NEI))
    spread_sum[...] = jnp.zeros(spread_sum.shape, F32)
    pushes[...] = jnp.zeros(pushes.shape, F32)

    def turn(g, carry):
        lifted = []
        hot = []
        pushed = pushes[...]
        for j in range(GROUP):
            n = GROUP * g + j
            rate = jnp.concatenate(
                [
                    jnp.sum(slope[n] * grown[:, HALF * h : HALF * (h + 1)], axis=0, keepdims=True)
                    for h, slope in enumerate((slope1, slope2))
                ],
                axis=1,
            )
            twice = 2.0 * (rate + rise[pl.ds(n, 1), :])
            push = [geo[c, pl.ds(n, 1), :] * twice for c in range(3)]
            highs = [v.astype(BF16).astype(F32) for v in push]
            rows = highs + [v - h for v, h in zip(push, highs)]
            value = jnp.concatenate(rows + [jnp.zeros((2, OWN), F32)], axis=0)
            pushed = pushed + value
            index = nbr[pl.ds(n, 1), :]
            high_row = index >> 8
            hot.append(hot_rows(index & (HALF - 1)))
            lifted.append(
                jnp.concatenate([jnp.where(high_row == k, value, 0.0) for k in range(LEVELS)], axis=0).astype(BF16)
            )
        pushes[...] = pushed
        spread_sum[...] += lax.dot_general(
            jnp.concatenate(lifted, axis=1), jnp.concatenate(hot, axis=1), (((1,), (1,)), ((), ())), preferred_element_type=F32
        )
        return carry

    lax.fori_loop(0, NEI // GROUP, turn, 0)
    table[...] = jnp.zeros(table.shape, F32)
    for k in range(LEVELS):
        width = min(HALF, EXT - HALF * k)
        table[0:3, HALF * k : HALF * k + width] = (
            spread_sum[8 * k : 8 * k + 3, :width] + spread_sum[8 * k + 3 : 8 * k + 6, :width]
        )
    table[0:3, 0:OWN] = table[0:3, 0:OWN] - pushes[0:3, :] - pushes[3:6, :]
    inner[...] = table[:, 0:INNER]
    outer_messages(par, table, one, two)


def final_kernel(par, own, one, two, gx, bundle, pos_out, vel_out, frc_out):
    forces = -fold_long(par, own, one, two, gx)[0:3, :]
    pos_out[...] = bundle[0:3, :]
    vel_out[...] = bundle[3:6, :] + (0.5 * TIME_STEP) * forces
    frc_out[...] = forces


def call(kernel, name, shapes, scratch, *operands, far=(), limit=BIG):
    specs = [pl.BlockSpec(memory_space=pltpu.HBM if k in far else pltpu.VMEM) for k in range(len(operands))]

    def placed(*refs):
        column = lax.axis_index("gy")
        kernel((lax.rem(lax.axis_index("gx"), 2), lax.rem(column, 2), column), *refs)

    return pl.pallas_call(
        placed,
        name=name,
        out_shape=[jax.ShapeDtypeStruct(shape, kind) for shape, kind in shapes],
        in_specs=specs,
        out_specs=[pl.BlockSpec(memory_space=pltpu.VMEM)] * len(shapes),
        scratch_shapes=[
            pltpu.SemaphoreType.DMA(shape) if kind is None else pltpu.VMEM(shape, kind) for shape, kind in scratch
        ],
        compiler_params=pltpu.CompilerParams(vmem_limit_bytes=limit),
    )(*operands)


def holds(*arrays):
    return [(a.shape, a.dtype) for a in arrays] + [((len(arrays),), None)]


def swap(axis, first):
    count = lax.axis_size(axis)
    offset = 0 if first else 1
    route = []
    for i in range(count):
        route.append((i, (((i + offset) ^ 1) - offset) % count))
    return route


def exchange(axis, one, two):
    return (
        lax.ppermute(one, axis, swap(axis, True)),
        lax.ppermute(two, axis, swap(axis, False)),
    )


def on_device(
    positions, velocities, forces, neighbours, ghost_x, ghost_y, migrate_x, migrate_y,
    w_basis, b_basis, w_embed, w_pair, w_mix, b_pair, w_out,
):
    narrow_count = lax.axis_size("gy")
    tile = ((8, LANES), F32)
    wide = ((8, OWN), F32)
    given = (positions, velocities, forces, ghost_x, ghost_y, migrate_x, migrate_y)
    record, message = call(
        start_kernel, "start", [wide, tile], holds(*given), *given,
        far=range(len(given)), limit=WHOLE,
    )
    given = (
        w_basis.T, w_pair, w_mix.T, w_embed, jnp.stack([b_basis, b_pair, w_out]),
    )
    doubled = ((2 * H, 2 * H), BF16)
    near, basis, pair_ahead, mix_ahead, pair_back, mix_back, w_ahead, w_back, columns = call(
        prepare_kernel,
        "prepare",
        [
            ((NEI, OWN), I32), ((H, 4 * NB), BF16), doubled, ((2 * H, 2 * EMB), BF16), doubled, ((2 * EMB, 2 * H), BF16),
            ((EMB, H), F32), ((H, EMB), F32), ((H, NB), F32),
        ],
        holds(*given), neighbours, *given, far=range(1, len(given) + 1),
    )
    message = lax.ppermute(message, "gx", swap("gx", True))
    mine = jnp.concatenate([record, message], axis=1)
    joined = lax.ppermute(mine, "gx", swap("gx", False))
    group = 2 * narrow_count
    own, blocks = call(cross_kernel, "cross", [wide, ((group, 8, OWN), F32)], [wide], mine, joined)
    members = [list(range(group * k, group * (k + 1))) for k in range(lax.axis_size("gx") // 2)]
    blocks = lax.all_to_all(blocks, ("gx", "gy"), 0, 0, axis_index_groups=members)

    bundle, gx, gy, embed, one, two, latent, geo, square = call(
        lambda *refs: env_kernel(narrow_count, *refs),
        "env",
        [
            wide, ((2, GX), I32), ((2, HALF), I32), ((EMB, OWN), F32), ((EMB, GX), F32), ((EMB, GX), F32),
            ((NEI, 2 * H, OWN), BF16), ((4, NEI, OWN), F32), ((NEI, OWN), F32),
        ],
        [((8, EXT), F32), ((8, INNER), F32)],
        blocks, own, near, basis, w_ahead,
    )
    (first,) = call(first_kernel, "first", [((NEI, H, OWN), F32)], [], latent, pair_ahead, columns)
    slopes = [
        call(
            lambda *refs, half=half: slope_kernel(half, *refs), f"slope{half}", [((NEI, H, HALF), F32)], [],
            square, geo, basis,
        )[0]
        for half in range(OWN // HALF)
    ]
    ex = exchange("gx", one, two)
    *ex, slopes[0] = lax.optimization_barrier((*ex, slopes[0]))
    message = ((EMB, HALF), F32)
    one, two = call(
        ghost_kernel, "ghost_embed", [message, message], [((EMB, INNER), F32)],
        embed, *ex, gy,
    )
    ey = exchange("gy", one, two)
    message = ((EMB, GY), F32)
    dvalue, part, inner, one, two = call(
        pair_kernel,
        "pair",
        [((NEI, 2 * H, OWN), BF16), ((NEI, OWN), F32), ((EMB, INNER), F32), message, message],
        [((EMB, EXT), F32), ((LEVELS * 2 * EMB, HALF), F32), ((EMB, OWN), F32)],
        embed, *ex, *ey, near, first, geo, mix_ahead, mix_back, columns,
    )
    one, two = exchange("gy", one, two)
    one, two, slopes[1] = lax.optimization_barrier((one, two, slopes[1]))
    (rise,) = call(rise_kernel, "rise", [((NEI, OWN), F32)], [], dvalue, part, *slopes, pair_back)
    message = ((EMB, GX), F32)
    own, one, two = call(
        fold_kernel, "fold_embed", [((EMB, OWN), F32), message, message], [], inner, one, two, gy
    )
    one, two = exchange("gx", one, two)
    message = ((8, GY), F32)
    inner, one, two = call(
        force_kernel,
        "force",
        [((8, INNER), F32), message, message],
        [((8, EXT), F32), ((8 * LEVELS, HALF), F32), ((8, OWN), F32), ((H, OWN), F32)],
        own, one, two, gx, w_back, *slopes, rise, geo, near,
    )
    one, two = exchange("gy", one, two)
    own, one, two = call(fold_kernel, "fold_force", [wide, tile, tile], [], inner, one, two, gy)
    one, two = exchange("gx", one, two)
    flat = ((3, OWN), F32)
    return tuple(call(final_kernel, "final", [flat, flat, flat], [], own, one, two, gx, bundle))


def solution(mesh):
    both = ("gx", "gy")
    flat = P(None, both)
    stacked = P(None, None, both)
    return jax.shard_map(
        on_device,
        mesh=mesh,
        in_specs=(flat,) * 3 + (stacked,) * 5 + (P(),) * 7,
        out_specs=(flat,) * 3,
        check_vma=False,
    )
```

```python
import math

import jax
import jax.numpy as jnp
from jax import lax
from jax.experimental import pallas as pl
from jax.experimental.pallas import tpu as pltpu
from jax.sharding import PartitionSpec as P

F32 = jnp.float32
BF16 = jnp.bfloat16
I32 = jnp.int32

TIME_STEP = 0.05
CENTRE_SPAN = 3.0
HIGHEST = lax.Precision.HIGHEST

NB = 8
NEI = 32
H = 64
EMB = 32
OWN = 512
GX = 128
GY = 192
MIG = 8
LANES = 128
INNER = OWN + 2 * GX
EXT = INNER + 2 * GY
GROUPS = EXT // LANES
HALF = 256
LEVELS = -(-EXT // HALF)
BIG = 24 * 1024 * 1024
WHOLE = 60 * 1024 * 1024
GROUP = 4
PAIR_GROUP = 16
SPAN = 2
FORCE_GROUP = 8
UNROLL_ENV = 8
ENV_WIDTH = 256
ENV_TURNS = 16


def half_split(value):
    high = value.astype(BF16)
    low = (value - high.astype(F32)).astype(BF16)
    return high, low


def third_split(value):
    high = value.astype(BF16)
    rest = value - high.astype(F32)
    middle = rest.astype(BF16)
    low = (rest - middle.astype(F32)).astype(BF16)
    return high, middle, low


def lane_take(table, index):
    return jnp.take_along_axis(table, index, axis=1, mode="promise_in_bounds")


def take_lanes(read, rows, groups, index_row):
    low = jnp.broadcast_to(index_row & (LANES - 1), (8, LANES))
    high = jnp.broadcast_to(index_row >> 7, (8, LANES))
    pieces = []
    for r in range(rows // 8):
        taken = jnp.zeros((8, LANES), F32)
        for g in range(groups):
            taken = jnp.where(high == g, lane_take(read(r, g), low), taken)
        pieces.append(taken)
    return jnp.concatenate(pieces, axis=0) if len(pieces) > 1 else pieces[0]


def tile_reader(ref):
    return lambda r, g: ref[8 * r : 8 * r + 8, LANES * g : LANES * (g + 1)]


def spread(values, lists, width):
    count = values.shape[1]
    hot = jnp.where(lax.broadcasted_iota(I32, (width, count), 0) == lists, 1.0, 0.0).astype(BF16)
    total = None
    for part in third_split(values):
        piece = lax.dot_general(part, hot, (((1,), (1,)), ((), ())), preferred_element_type=F32)
        total = piece if total is None else total + piece
    return total


def by_parity(parity, even, odd):
    return jnp.where(parity == 0, even, odd)


def unit_row(rows, row, amount):
    return jnp.where(lax.broadcasted_iota(I32, (rows, 1), 0) == row, amount, 0.0)


def place(spots, values, slots, from_lower, from_upper, base=0):
    for k in range(MIG):
        down = slice(MIG + k, MIG + k + 1)
        up = slice(k, k + 1)
        message_up = from_lower[:, base + k : base + k + 1]
        message_down = from_upper[:, base + MIG + k : base + MIG + k + 1]
        values = jnp.where(spots == slots[:, down], message_up, values)
        values = jnp.where(spots == slots[:, up], message_down, values)
    return values


def value_reader(value):
    return lambda r, g: value[8 * r : 8 * r + 8, LANES * g : LANES * (g + 1)]


LONG_SLOTS = slice(2 * GX, 2 * GX + LANES)
NARROW_SLOTS = slice(2 * GX + LANES, 2 * GX + 2 * LANES)


def ghost_list(record, side):
    return record[6:7, GX * side : GX * (side + 1)].astype(I32)


def narrow_list(record, side):
    return record[7:8, HALF * side : HALF * (side + 1)].astype(I32)


def leavers(record, lanes, row):
    lane = lax.broadcasted_iota(I32, (8, LANES), 1) & (2 * MIG - 1)
    shift = jnp.where(lane < MIG, -1.0, 1.0)
    rows = lax.broadcasted_iota(I32, (8, LANES), 0)
    taken = take_lanes(value_reader(record), 8, OWN // LANES, record[6:7, lanes].astype(I32))
    return taken + jnp.where(rows == row, shift, 0.0)


def fetch(sources, targets, sems):
    copies = [pltpu.make_async_copy(src, dst, sems.at[k]) for k, (src, dst) in enumerate(zip(sources, targets))]
    for copy in copies:
        copy.start()
    for copy in copies:
        copy.wait()


def prepare_kernel(
    par, neighbours, basis_t, pair, mix_t, w_embed, vectors, near, basis, pair_ahead, mix_ahead, pair_back, mix_back, w_ahead, w_back, columns, *scratch
):
    held = scratch[:-1]
    near[...] = neighbours[0]
    fetch((basis_t, pair, mix_t, w_embed, vectors), held, scratch[-1])
    basis_t, pair, mix_t, w_embed, vectors = held
    b_basis = vectors[0:1, :]
    high, low = half_split(basis_t[...])
    high, low = high.astype(F32), low.astype(F32)
    parts = [part.astype(F32) for part in third_split(b_basis)]
    parts = jnp.concatenate(parts + [jnp.zeros((NB - 3, H), F32)], axis=0)
    basis[...] = jnp.concatenate([high, high, low, parts], axis=0).T.astype(BF16)
    rows = jnp.concatenate([vectors[1:3, :], jnp.zeros((NB - 2, H), F32)], axis=0)
    columns[...] = rows.T
    w_ahead[...] = w_embed[...]
    w_back[...] = w_embed[...].T
    for layer_t, ahead, back in ((pair[...].T, pair_ahead, pair_back), (mix_t[...], mix_ahead, mix_back)):
        high, low = half_split(layer_t)
        high, low = high.astype(F32), low.astype(F32)
        nothing = jnp.zeros(high.shape, F32)
        back[...] = jnp.concatenate(
            [jnp.concatenate([high, high], axis=1), jnp.concatenate([low, nothing], axis=1)], axis=0
        ).astype(BF16)
        ahead[0:H, :] = jnp.concatenate([high, high], axis=0).T.astype(BF16)
        ahead[H : 2 * H, :] = jnp.concatenate([low, nothing], axis=0).T.astype(BF16)


def start_kernel(par, pos, vel, frc, gx, gy, mx, my, record, message, *scratch):
    held = scratch[:-1]
    fetch((pos, vel, frc, gx, gy, mx, my), held, scratch[-1])
    pos, vel, frc, gx, gy, mx, my = held
    speeds = vel[...] + (0.5 * TIME_STEP) * frc[...]
    record[0:3, :] = pos[...] + TIME_STEP * speeds
    record[3:6, :] = speeds
    record[6:8, :] = jnp.zeros((2, OWN), F32)
    for side in range(2):
        long_start = LONG_SLOTS.start + MIG * side
        record[6:7, GX * side : GX * (side + 1)] = gx[0, side : side + 1, :].astype(F32)
        record[6:7, long_start : long_start + MIG] = mx[0, side : side + 1, :].astype(F32)
        for again in range(2):
            start = NARROW_SLOTS.start + MIG * (side + 2 * again)
            record[6:7, start : start + MIG] = my[0, side : side + 1, :].astype(F32)
        record[7:8, HALF * side : HALF * side + GY] = gy[0, side : side + 1, :].astype(F32)
    message[...] = leavers(record[...], LONG_SLOTS, 0)


def crossed(record, from_lower, from_upper):
    lane = lax.broadcasted_iota(I32, record.shape, 1)
    moved = place(lane, record, record[6:7, LONG_SLOTS].astype(I32), from_lower, from_upper)
    return jnp.where(lax.broadcasted_iota(I32, record.shape, 0) < 6, moved, record)


AREAS = [slice(LANES * k, LANES * (k + 1)) for k in range(4)]


def cross_kernel(par, kept, joined, own_out, out, block):
    p = par[0]
    own = kept[:, 0:OWN]
    other = joined[:, 0:OWN]
    near_side = kept[:, OWN : OWN + LANES]
    far_side = joined[:, OWN : OWN + LANES]
    from_other = leavers(other, LONG_SLOTS, 0)
    from_own = leavers(own, LONG_SLOTS, 0)
    own = crossed(own, by_parity(p, from_other, near_side), by_parity(p, near_side, from_other))
    other = crossed(other, by_parity(p, far_side, from_own), by_parity(p, from_own, far_side))
    own_out[...] = own
    block[0:3, :] = own[0:3, :]
    block[3:4, :] = own[7:8, :]
    for area, record in ((AREAS[0], other), (AREAS[1], own)):
        chosen = by_parity(p, ghost_list(record, 0), ghost_list(record, 1))
        block[4:7, area] = take_lanes(value_reader(record), 8, OWN // LANES, chosen)[0:3, :]
        block[7:8, area] = chosen.astype(F32)
    lane = lax.broadcasted_iota(I32, (3, LANES), 1)
    for area, record in ((AREAS[2], own), (AREAS[3], other)):
        leave = leavers(record, NARROW_SLOTS, 1)
        block[4:7, area] = jnp.where(lane < 2 * MIG, leave[0:3, :], leave[3:6, :])
        block[7:8, area] = record[6:7, NARROW_SLOTS]
    for b in range(out.shape[0]):
        out[b] = block[...]


def settle(par, blocks, record, narrow_count, bundle, table, inner):
    p = par[0]

    def number(member, narrow_step):
        return member * narrow_count + lax.rem(par[2] + (narrow_step + narrow_count), narrow_count)

    def settled(member, narrow_step, spots, values, leave, base=0):
        slots = blocks[number(member, narrow_step), 7:8, leave].astype(I32)
        from_lower = blocks[number(member, narrow_step - 1), 4:7, leave]
        from_upper = blocks[number(member, narrow_step + 1), 4:7, leave]
        return place(spots, values, slots, from_lower, from_upper, base)

    lane = lax.broadcasted_iota(I32, (3, OWN), 1)
    inner[...] = jnp.zeros(inner.shape, F32)
    toward = by_parity(p, -1.0, 1.0)
    for narrow_step in (-1, 1, 0):
        here = number(p, narrow_step)
        there = number(1 - p, narrow_step)
        middle = settled(p, narrow_step, lane, blocks[here, 0:3, :], AREAS[2])
        second = settled(
            p, narrow_step, blocks[here, 7:8, AREAS[0]].astype(I32), blocks[here, 4:7, AREAS[0]], AREAS[3]
        ) + unit_row(3, 0, toward)
        first = settled(
            1 - p, narrow_step, blocks[there, 7:8, AREAS[1]].astype(I32), blocks[there, 4:7, AREAS[1]], AREAS[2]
        ) - unit_row(3, 0, toward)
        inner[0:3, 0:OWN] = middle
        inner[0:3, OWN : OWN + GX] = by_parity(p, second, first)
        inner[0:3, OWN + GX : INNER] = by_parity(p, first, second)
        if narrow_step == 0:
            bundle[0:3, :] = middle
            bundle[3:6, :] = settled(p, 0, lane, record[3:6, :], AREAS[2], 2 * MIG)
            bundle[6:8, :] = record[6:8, :]
            table[:, 0:INNER] = inner[...]
            continue
        side = 0 if narrow_step < 0 else 1
        chosen = blocks[here, 3:4, HALF * side : HALF * (side + 1)].astype(I32)
        taken = jnp.concatenate(
            [
                take_lanes(tile_reader(inner), 8, INNER // LANES, chosen[:, LANES * c : LANES * (c + 1)])
                for c in range(2)
            ],
            axis=1,
        )
        base = INNER + GY * side
        table[:, base : base + GY] = taken[:, 0:GY] + unit_row(8, 1, float(narrow_step))


def narrow_messages(par, table, rows, gy, one, two):
    p = par[1]
    for out, chosen in (
        (one, by_parity(p, gy[0:1, :], gy[1:2, :])),
        (two, by_parity(p, gy[1:2, :], gy[0:1, :])),
    ):
        for c in range(2):
            out[:, LANES * c : LANES * (c + 1)] = take_lanes(
                tile_reader(table), rows, INNER // LANES, chosen[:, LANES * c : LANES * (c + 1)]
            )


def inner_table(par, own, one, two, table):
    p = par[0]
    table[:, 0:OWN] = own
    table[:, OWN : OWN + GX] = by_parity(p, two[...], one[...])
    table[:, OWN + GX : INNER] = by_parity(p, one[...], two[...])


def outer_table(par, one, two, table):
    p = par[1]
    table[:, INNER : INNER + GY] = by_parity(p, two[:, 0:GY], one[:, 0:GY])
    table[:, INNER + GY : EXT] = by_parity(p, one[:, 0:GY], two[:, 0:GY])


def ghost_kernel(par, own, one_in, two_in, gy, one, two, table):
    inner_table(par, own[...], one_in, two_in, table)
    narrow_messages(par, table, own.shape[0], gy, one, two)


def product(left, right):
    return lax.dot_general(left, right, (((1,), (0,)), ((), ())), preferred_element_type=F32)


def centres():
    return lax.broadcasted_iota(I32, (NB, 1), 0).astype(F32) * (CENTRE_SPAN / (NB - 1))


def basis_rows(radial, last):
    high = radial.astype(BF16).astype(F32)
    return jnp.concatenate([high, radial - high, high, last], axis=0)


def slope_kernel(half, par, square, geo, basis, slope):
    lanes = slice(HALF * half, HALF * (half + 1))
    centre = centres()
    ones = jnp.ones((NB, HALF), F32)
    left = basis[...]

    def turn(n, carry):
        offset = square[pl.ds(n, 1), lanes] - centre
        weight = geo[3, pl.ds(n, 1), lanes]
        radial = jnp.exp(-(offset * offset))
        right = [basis_rows(radial, ones), basis_rows(-2.0 * offset * radial, 0.0 * ones)]
        both = product(left, jnp.concatenate(right, axis=1).astype(BF16))
        value = both[:, :HALF]
        gate = 0.5 * jnp.tanh(0.5 * value) + 0.5
        raw = value * gate
        slope[n] = weight * ((gate + raw * (1.0 - gate)) * both[:, HALF:] - raw * weight)
        return carry

    lax.fori_loop(0, NEI, turn, 0, unroll=UNROLL_ENV)


def grouped(ref, g):
    return jnp.concatenate([ref[GROUP * g + j] for j in range(GROUP)], axis=1)


def first_kernel(par, latent, pair_ahead, columns, first):
    left = pair_ahead[...]
    bias = columns[:, 0:1]

    def turn(g, carry):
        sums = product(left, grouped(latent, g))
        for j in range(GROUP):
            lanes = slice(OWN * j, OWN * (j + 1))
            first[GROUP * g + j] = sums[:H, lanes] + sums[H:, lanes] + bias
        return carry

    lax.fori_loop(0, NEI // GROUP, turn, 0)


def rise_kernel(par, dvalue, part, slope1, slope2, pair_back, rise):
    left = pair_back[...]

    def turn(g, carry):
        sums = product(left, grouped(dvalue, g))
        for j in range(GROUP):
            n = GROUP * g + j
            for half, slope in enumerate((slope1, slope2)):
                lanes = slice(HALF * half, HALF * (half + 1))
                wide = slice(OWN * j + HALF * half, OWN * j + HALF * (half + 1))
                dlatent = sums[:H, wide] + sums[H:, wide]
                total = jnp.sum(dlatent * slope[n], axis=0, keepdims=True)
                rise[pl.ds(n, 1), lanes] = total + part[pl.ds(n, 1), lanes]
        return carry

    lax.fori_loop(0, NEI // GROUP, turn, 0)


def env_kernel(
    narrow_count, par, blocks, record, nbr, basis, w_embed,
    own, gx, gy, embed, one, two, latent_out, geo, square, table, inner,
):
    settle(par, blocks, record, narrow_count, own, table, inner)
    for side in range(2):
        gx[side : side + 1, :] = ghost_list(own, side)
        gy[side : side + 1, :] = narrow_list(own, side)
    for b in range(OWN // LANES):
        lanes = slice(LANES * b, LANES * (b + 1))
        for q in range(NEI // 8):
            rows = slice(8 * q, 8 * q + 8)
            index = nbr[rows, lanes]
            low = index & (LANES - 1)
            high = index >> 7
            total = jnp.zeros((8, LANES), F32)
            for c in range(3):
                taken = jnp.zeros((8, LANES), F32)
                for g in range(GROUPS):
                    tile = jnp.broadcast_to(table[c : c + 1, LANES * g : LANES * (g + 1)], (8, LANES))
                    taken = jnp.where(high == g, lane_take(tile, low), taken)
                apart = taken - own[c : c + 1, lanes]
                geo[c, rows, lanes] = apart
                total = total + apart * apart
            square[rows, lanes] = total
            geo[3, rows, lanes] = jnp.where(index >= 0, 1.0 / (1.0 + total), 0.0)

    centre = centres()
    ones = jnp.ones((NB, ENV_WIDTH), F32)
    left = basis[...]
    for half in range(OWN // ENV_WIDTH):
        lanes = slice(ENV_WIDTH * half, ENV_WIDTH * (half + 1))

        def turn(n, gathered):
            offset = square[pl.ds(n, 1), lanes] - centre
            value = product(left, basis_rows(jnp.exp(-(offset * offset)), ones).astype(BF16))
            gate = 0.5 * jnp.tanh(0.5 * value) + 0.5
            latent = value * gate * geo[3, pl.ds(n, 1), lanes]
            high, low = half_split(latent)
            latent_out[n, 0:H, lanes] = high
            latent_out[n, H : 2 * H, lanes] = low
            return gathered + latent

        gathered = lax.fori_loop(0, NEI, turn, jnp.zeros((H, ENV_WIDTH), F32), unroll=ENV_TURNS)
        environ = gathered * (1.0 / math.sqrt(NEI))
        embed[:, lanes] = jnp.dot(w_embed[...], environ, precision=HIGHEST, preferred_element_type=F32)
    p = par[0]
    reader = tile_reader(embed)
    one[...] = take_lanes(reader, EMB, OWN // LANES, by_parity(p, gx[0:1, :], gx[1:2, :]))
    two[...] = take_lanes(reader, EMB, OWN // LANES, by_parity(p, gx[1:2, :], gx[0:1, :]))


def hot_rows(low_row):
    level = lax.broadcasted_iota(I32, (HALF, low_row.shape[1]), 0)
    return jnp.where(level == low_row, 1.0, 0.0).astype(BF16)


def level_rows(value, high_row):
    pieces = []
    for k in range(LEVELS):
        mask = jnp.where(high_row == k, 1.0, 0.0).astype(BF16)
        pieces.append(value * mask)
    return jnp.concatenate(pieces, axis=0)


def pair_kernel(
    par, own, gx1, gx2, gy1, gy2, nbr, first, geo, ahead, back, columns,
    dvalue_out, part, inner, one, two, table, spread_sum, own_sum,
):
    inner_table(par, own[...], gx1, gx2, table)
    outer_table(par, gy1, gy2, table)
    spread_sum[...] = jnp.zeros(spread_sum.shape, F32)
    own_sum[...] = jnp.zeros(own_sum.shape, F32)
    left = ahead[...]
    right_back = back[...]
    readout = columns[:, 1:2]

    def rows_of(read, start, count):
        return jnp.concatenate([read(start + j) for j in range(count)], axis=1)

    def scatter(g, joined):
        index = rows_of(lambda n: nbr[pl.ds(n, 1), :], PAIR_GROUP * g, PAIR_GROUP)
        spread_sum[...] += lax.dot_general(
            level_rows(joined, index >> 8), hot_rows(index & (HALF - 1)),
            (((1,), (1,)), ((), ())), preferred_element_type=F32,
        )

    def chunk(n):
        index = rows_of(lambda m: nbr[pl.ds(m, 1), :], n, SPAN)
        weight = rows_of(lambda m: geo[3, pl.ds(m, 1), :], n, SPAN)
        partner = jnp.concatenate(
            [
                take_lanes(tile_reader(table), EMB, GROUPS, index[:, LANES * c : LANES * (c + 1)])
                for c in range(SPAN * OWN // LANES)
            ],
            axis=1,
        )
        embed_own = jnp.concatenate([own[...]] * SPAN, axis=1)
        product_high, product_low = half_split(partner * embed_own)
        sums = product(left, jnp.concatenate([product_high, product_low], axis=0))
        value = rows_of(lambda m: first[m], n, SPAN) + sums[:H] + sums[H:]
        gate = 0.5 * jnp.tanh(0.5 * value) + 0.5
        hidden = value * gate
        dvalue = (gate + hidden * (1.0 - gate)) * (readout * weight)
        dhigh, dlow = half_split(dvalue)
        dvalue = jnp.concatenate([dhigh, dlow], axis=0)
        sums = product(right_back, dvalue)
        dproduct = sums[:EMB] + sums[EMB:]
        partial = -(weight * weight) * jnp.sum(hidden * readout, axis=0, keepdims=True)
        more = dproduct * partner
        for j in range(SPAN):
            lanes = slice(OWN * j, OWN * (j + 1))
            dvalue_out[n + j] = dvalue[:, lanes]
            part[pl.ds(n + j, 1), :] = partial[:, lanes]
            own_sum[...] += more[:, lanes]
        high, low = half_split(dproduct * embed_own)
        return jnp.concatenate([high, low], axis=0)

    def turn(g, joined):
        scatter(jnp.maximum(g - 1, 0), joined)
        return jnp.concatenate([chunk(PAIR_GROUP * g + SPAN * j) for j in range(PAIR_GROUP // SPAN)], axis=1)

    joined = lax.fori_loop(0, NEI // PAIR_GROUP, turn, jnp.zeros((2 * EMB, PAIR_GROUP * OWN), BF16))
    scatter(NEI // PAIR_GROUP - 1, joined)
    for k in range(LEVELS):
        base = 2 * EMB * k
        width = min(HALF, EXT - HALF * k)
        table[:, HALF * k : HALF * k + width] = (
            spread_sum[base : base + EMB, :width] + spread_sum[base + EMB : base + 2 * EMB, :width]
        )
    inner[:, 0:OWN] = table[:, 0:OWN] + own_sum[...]
    inner[:, OWN:INNER] = table[:, OWN:INNER]
    outer_messages(par, table, one, two)


def outer_messages(par, table, one, two):
    p = par[1]
    down = table[:, INNER : INNER + GY]
    up = table[:, INNER + GY : EXT]
    one[...] = by_parity(p, up, down)
    two[...] = by_parity(p, down, up)


def fold_narrow(par, inner, one, two, gy):
    p = par[1]
    from_upper = by_parity(p, one[...], two[...])
    from_lower = by_parity(p, two[...], one[...])
    return (
        inner[...]
        + spread(from_upper, gy[0:1, 0:GY], INNER)
        + spread(from_lower, gy[1:2, 0:GY], INNER)
    )


def fold_long(par, own, one, two, gx):
    p = par[0]
    from_upper = by_parity(p, one[...], two[...])
    from_lower = by_parity(p, two[...], one[...])
    return own[...] + spread(from_upper, gx[0:1, :], OWN) + spread(from_lower, gx[1:2, :], OWN)


def fold_kernel(par, inner, one_in, two_in, gy, own, one, two):
    total = fold_narrow(par, inner, one_in, two_in, gy)
    own[...] = total[:, 0:OWN]
    down = total[:, OWN : OWN + GX]
    up = total[:, OWN + GX : INNER]
    p = par[0]
    one[...] = by_parity(p, up, down)
    two[...] = by_parity(p, down, up)


def force_kernel(
    par, own_in, gx1, gx2, gx, w_back, slope1, slope2, rise, geo, nbr,
    inner, one, two, table, spread_sum, pushes, grown,
):
    grad = fold_long(par, own_in, gx1, gx2, gx)
    grown[...] = jnp.dot(w_back[...], grad, precision=HIGHEST, preferred_element_type=F32) * (1.0 / math.sqrt(NEI))
    spread_sum[...] = jnp.zeros(spread_sum.shape, F32)
    pushes[...] = jnp.zeros(pushes.shape, F32)

    def turn(g, carry):
        lifted = []
        hot = []
        pushed = pushes[...]
        for j in range(FORCE_GROUP):
            n = FORCE_GROUP * g + j
            rate = jnp.concatenate(
                [
                    jnp.sum(slope[n] * grown[:, HALF * h : HALF * (h + 1)], axis=0, keepdims=True)
                    for h, slope in enumerate((slope1, slope2))
                ],
                axis=1,
            )
            twice = 2.0 * (rate + rise[pl.ds(n, 1), :])
            push = [geo[c, pl.ds(n, 1), :] * twice for c in range(3)]
            highs = [v.astype(BF16).astype(F32) for v in push]
            rows = highs + [v - h for v, h in zip(push, highs)]
            value = jnp.concatenate(rows + [jnp.zeros((2, OWN), F32)], axis=0)
            pushed = pushed + value
            index = nbr[pl.ds(n, 1), :]
            high_row = index >> 8
            hot.append(hot_rows(index & (HALF - 1)))
            lifted.append(
                jnp.concatenate([jnp.where(high_row == k, value, 0.0) for k in range(LEVELS)], axis=0).astype(BF16)
            )
        pushes[...] = pushed
        spread_sum[...] += lax.dot_general(
            jnp.concatenate(lifted, axis=1), jnp.concatenate(hot, axis=1), (((1,), (1,)), ((), ())), preferred_element_type=F32
        )
        return carry

    lax.fori_loop(0, NEI // FORCE_GROUP, turn, 0)
    table[...] = jnp.zeros(table.shape, F32)
    for k in range(LEVELS):
        width = min(HALF, EXT - HALF * k)
        table[0:3, HALF * k : HALF * k + width] = (
            spread_sum[8 * k : 8 * k + 3, :width] + spread_sum[8 * k + 3 : 8 * k + 6, :width]
        )
    table[0:3, 0:OWN] = table[0:3, 0:OWN] - pushes[0:3, :] - pushes[3:6, :]
    inner[...] = table[:, 0:INNER]
    outer_messages(par, table, one, two)


def final_kernel(par, own, one, two, gx, bundle, pos_out, vel_out, frc_out):
    forces = -fold_long(par, own, one, two, gx)[0:3, :]
    pos_out[...] = bundle[0:3, :]
    vel_out[...] = bundle[3:6, :] + (0.5 * TIME_STEP) * forces
    frc_out[...] = forces


def call(kernel, name, shapes, scratch, *operands, far=(), limit=BIG):
    specs = [pl.BlockSpec(memory_space=pltpu.HBM if k in far else pltpu.VMEM) for k in range(len(operands))]

    def placed(*refs):
        column = lax.axis_index("gy")
        kernel((lax.rem(lax.axis_index("gx"), 2), lax.rem(column, 2), column), *refs)

    return pl.pallas_call(
        placed,
        name=name,
        out_shape=[jax.ShapeDtypeStruct(shape, kind) for shape, kind in shapes],
        in_specs=specs,
        out_specs=[pl.BlockSpec(memory_space=pltpu.VMEM)] * len(shapes),
        scratch_shapes=[
            pltpu.SemaphoreType.DMA(shape) if kind is None else pltpu.VMEM(shape, kind) for shape, kind in scratch
        ],
        compiler_params=pltpu.CompilerParams(vmem_limit_bytes=limit),
    )(*operands)


def holds(*arrays):
    return [(a.shape, a.dtype) for a in arrays] + [((len(arrays),), None)]


def swap(axis, first):
    count = lax.axis_size(axis)
    offset = 0 if first else 1
    route = []
    for i in range(count):
        route.append((i, (((i + offset) ^ 1) - offset) % count))
    return route


def exchange(axis, one, two):
    return (
        lax.ppermute(one, axis, swap(axis, True)),
        lax.ppermute(two, axis, swap(axis, False)),
    )


def on_device(
    positions, velocities, forces, neighbours, ghost_x, ghost_y, migrate_x, migrate_y,
    w_basis, b_basis, w_embed, w_pair, w_mix, b_pair, w_out,
):
    narrow_count = lax.axis_size("gy")
    tile = ((8, LANES), F32)
    wide = ((8, OWN), F32)
    given = (positions, velocities, forces, ghost_x, ghost_y, migrate_x, migrate_y)
    record, message = call(
        start_kernel, "start", [wide, tile], holds(*given), *given,
        far=range(len(given)), limit=WHOLE,
    )
    given = (
        w_basis.T, w_pair, w_mix.T, w_embed, jnp.stack([b_basis, b_pair, w_out]),
    )
    doubled = ((2 * H, 2 * H), BF16)
    near, basis, pair_ahead, mix_ahead, pair_back, mix_back, w_ahead, w_back, columns = call(
        prepare_kernel,
        "prepare",
        [
            ((NEI, OWN), I32), ((H, 4 * NB), BF16), doubled, ((2 * H, 2 * EMB), BF16), doubled, ((2 * EMB, 2 * H), BF16),
            ((EMB, H), F32), ((H, EMB), F32), ((H, NB), F32),
        ],
        holds(*given), neighbours, *given, far=range(1, len(given) + 1),
    )
    message = lax.ppermute(message, "gx", swap("gx", True))
    mine = jnp.concatenate([record, message], axis=1)
    joined = lax.ppermute(mine, "gx", swap("gx", False))
    group = 2 * narrow_count
    own, blocks = call(cross_kernel, "cross", [wide, ((group, 8, OWN), F32)], [wide], mine, joined)
    members = [list(range(group * k, group * (k + 1))) for k in range(lax.axis_size("gx") // 2)]
    blocks = lax.all_to_all(blocks, ("gx", "gy"), 0, 0, axis_index_groups=members)

    bundle, gx, gy, embed, one, two, latent, geo, square = call(
        lambda *refs: env_kernel(narrow_count, *refs),
        "env",
        [
            wide, ((2, GX), I32), ((2, HALF), I32), ((EMB, OWN), F32), ((EMB, GX), F32), ((EMB, GX), F32),
            ((NEI, 2 * H, OWN), BF16), ((4, NEI, OWN), F32), ((NEI, OWN), F32),
        ],
        [((8, EXT), F32), ((8, INNER), F32)],
        blocks, own, near, basis, w_ahead,
    )
    (first,) = call(first_kernel, "first", [((NEI, H, OWN), F32)], [], latent, pair_ahead, columns)
    slopes = [
        call(
            lambda *refs, half=half: slope_kernel(half, *refs), f"slope{half}", [((NEI, H, HALF), F32)], [],
            square, geo, basis,
        )[0]
        for half in range(OWN // HALF)
    ]
    ex = exchange("gx", one, two)
    *ex, slopes[0] = lax.optimization_barrier((*ex, slopes[0]))
    message = ((EMB, HALF), F32)
    one, two = call(
        ghost_kernel, "ghost_embed", [message, message], [((EMB, INNER), F32)],
        embed, *ex, gy,
    )
    ey = exchange("gy", one, two)
    message = ((EMB, GY), F32)
    dvalue, part, inner, one, two = call(
        pair_kernel,
        "pair",
        [((NEI, 2 * H, OWN), BF16), ((NEI, OWN), F32), ((EMB, INNER), F32), message, message],
        [((EMB, EXT), F32), ((LEVELS * 2 * EMB, HALF), F32), ((EMB, OWN), F32)],
        embed, *ex, *ey, near, first, geo, mix_ahead, mix_back, columns,
    )
    one, two = exchange("gy", one, two)
    one, two, slopes[1] = lax.optimization_barrier((one, two, slopes[1]))
    (rise,) = call(rise_kernel, "rise", [((NEI, OWN), F32)], [], dvalue, part, *slopes, pair_back)
    message = ((EMB, GX), F32)
    own, one, two = call(
        fold_kernel, "fold_embed", [((EMB, OWN), F32), message, message], [], inner, one, two, gy
    )
    one, two = exchange("gx", one, two)
    message = ((8, GY), F32)
    inner, one, two = call(
        force_kernel,
        "force",
        [((8, INNER), F32), message, message],
        [((8, EXT), F32), ((8 * LEVELS, HALF), F32), ((8, OWN), F32), ((H, OWN), F32)],
        own, one, two, gx, w_back, *slopes, rise, geo, near,
    )
    one, two = exchange("gy", one, two)
    own, one, two = call(fold_kernel, "fold_force", [wide, tile, tile], [], inner, one, two, gy)
    one, two = exchange("gx", one, two)
    flat = ((3, OWN), F32)
    return tuple(call(final_kernel, "final", [flat, flat, flat], [], own, one, two, gx, bundle))


def solution(mesh):
    both = ("gx", "gy")
    flat = P(None, both)
    stacked = P(None, None, both)
    return jax.shard_map(
        on_device,
        mesh=mesh,
        in_specs=(flat,) * 3 + (stacked,) * 5 + (P(),) * 7,
        out_specs=(flat,) * 3,
        check_vma=False,
    )
```

```python
import math

import jax
import jax.numpy as jnp
from jax import lax
from jax.experimental import pallas as pl
from jax.experimental.pallas import tpu as pltpu
from jax.sharding import PartitionSpec as P

F32 = jnp.float32
BF16 = jnp.bfloat16
I32 = jnp.int32

TIME_STEP = 0.05
CENTRE_SPAN = 3.0
HIGHEST = lax.Precision.HIGHEST

NB = 8
NEI = 32
H = 64
EMB = 32
OWN = 512
GX = 128
GY = 192
MIG = 8
LANES = 128
INNER = OWN + 2 * GX
EXT = INNER + 2 * GY
GROUPS = EXT // LANES
HALF = 256
LEVELS = -(-EXT // HALF)
BIG = 24 * 1024 * 1024
WHOLE = 60 * 1024 * 1024
GROUP = 4
PAIR_GROUP = 16
SPAN = 2
FORCE_GROUP = 16
UNROLL_ENV = 8
ENV_WIDTH = 256
ENV_TURNS = 16


def half_split(value):
    high = value.astype(BF16)
    low = (value - high.astype(F32)).astype(BF16)
    return high, low


def third_split(value):
    high = value.astype(BF16)
    rest = value - high.astype(F32)
    middle = rest.astype(BF16)
    low = (rest - middle.astype(F32)).astype(BF16)
    return high, middle, low


def lane_take(table, index):
    return jnp.take_along_axis(table, index, axis=1, mode="promise_in_bounds")


def take_lanes(read, rows, groups, index_row):
    low = jnp.broadcast_to(index_row & (LANES - 1), (8, LANES))
    high = jnp.broadcast_to(index_row >> 7, (8, LANES))
    pieces = []
    for r in range(rows // 8):
        taken = jnp.zeros((8, LANES), F32)
        for g in range(groups):
            taken = jnp.where(high == g, lane_take(read(r, g), low), taken)
        pieces.append(taken)
    return jnp.concatenate(pieces, axis=0) if len(pieces) > 1 else pieces[0]


def tile_reader(ref):
    return lambda r, g: ref[8 * r : 8 * r + 8, LANES * g : LANES * (g + 1)]


def spread(values, lists, width):
    count = values.shape[1]
    hot = jnp.where(lax.broadcasted_iota(I32, (width, count), 0) == lists, 1.0, 0.0).astype(BF16)
    total = None
    for part in third_split(values):
        piece = lax.dot_general(part, hot, (((1,), (1,)), ((), ())), preferred_element_type=F32)
        total = piece if total is None else total + piece
    return total


def by_parity(parity, even, odd):
    return jnp.where(parity == 0, even, odd)


def unit_row(rows, row, amount):
    return jnp.where(lax.broadcasted_iota(I32, (rows, 1), 0) == row, amount, 0.0)


def place(spots, values, slots, from_lower, from_upper, base=0):
    for k in range(MIG):
        down = slice(MIG + k, MIG + k + 1)
        up = slice(k, k + 1)
        message_up = from_lower[:, base + k : base + k + 1]
        message_down = from_upper[:, base + MIG + k : base + MIG + k + 1]
        values = jnp.where(spots == slots[:, down], message_up, values)
        values = jnp.where(spots == slots[:, up], message_down, values)
    return values


def value_reader(value):
    return lambda r, g: value[8 * r : 8 * r + 8, LANES * g : LANES * (g + 1)]


LONG_SLOTS = slice(2 * GX, 2 * GX + LANES)
NARROW_SLOTS = slice(2 * GX + LANES, 2 * GX + 2 * LANES)


def ghost_list(record, side):
    return record[6:7, GX * side : GX * (side + 1)].astype(I32)


def narrow_list(record, side):
    return record[7:8, HALF * side : HALF * (side + 1)].astype(I32)


def leavers(record, lanes, row):
    lane = lax.broadcasted_iota(I32, (8, LANES), 1) & (2 * MIG - 1)
    shift = jnp.where(lane < MIG, -1.0, 1.0)
    rows = lax.broadcasted_iota(I32, (8, LANES), 0)
    taken = take_lanes(value_reader(record), 8, OWN // LANES, record[6:7, lanes].astype(I32))
    return taken + jnp.where(rows == row, shift, 0.0)


def fetch(sources, targets, sems):
    copies = [pltpu.make_async_copy(src, dst, sems.at[k]) for k, (src, dst) in enumerate(zip(sources, targets))]
    for copy in copies:
        copy.start()
    for copy in copies:
        copy.wait()


def prepare_kernel(
    par, neighbours, basis_t, pair, mix_t, w_embed, vectors, near, basis, pair_ahead, mix_ahead, pair_back, mix_back, w_ahead, w_back, columns, *scratch
):
    held = scratch[:-1]
    near[...] = neighbours[0]
    fetch((basis_t, pair, mix_t, w_embed, vectors), held, scratch[-1])
    basis_t, pair, mix_t, w_embed, vectors = held
    b_basis = vectors[0:1, :]
    high, low = half_split(basis_t[...])
    high, low = high.astype(F32), low.astype(F32)
    parts = [part.astype(F32) for part in third_split(b_basis)]
    parts = jnp.concatenate(parts + [jnp.zeros((NB - 3, H), F32)], axis=0)
    basis[...] = jnp.concatenate([high, high, low, parts], axis=0).T.astype(BF16)
    rows = jnp.concatenate([vectors[1:3, :], jnp.zeros((NB - 2, H), F32)], axis=0)
    columns[...] = rows.T
    w_ahead[...] = w_embed[...]
    w_back[...] = w_embed[...].T
    for layer_t, ahead, back in ((pair[...].T, pair_ahead, pair_back), (mix_t[...], mix_ahead, mix_back)):
        high, low = half_split(layer_t)
        high, low = high.astype(F32), low.astype(F32)
        nothing = jnp.zeros(high.shape, F32)
        back[...] = jnp.concatenate(
            [jnp.concatenate([high, high], axis=1), jnp.concatenate([low, nothing], axis=1)], axis=0
        ).astype(BF16)
        ahead[0:H, :] = jnp.concatenate([high, high], axis=0).T.astype(BF16)
        ahead[H : 2 * H, :] = jnp.concatenate([low, nothing], axis=0).T.astype(BF16)


def start_kernel(par, pos, vel, frc, gx, gy, mx, my, record, message, *scratch):
    held = scratch[:-1]
    fetch((pos, vel, frc, gx, gy, mx, my), held, scratch[-1])
    pos, vel, frc, gx, gy, mx, my = held
    speeds = vel[...] + (0.5 * TIME_STEP) * frc[...]
    record[0:3, :] = pos[...] + TIME_STEP * speeds
    record[3:6, :] = speeds
    record[6:8, :] = jnp.zeros((2, OWN), F32)
    for side in range(2):
        long_start = LONG_SLOTS.start + MIG * side
        record[6:7, GX * side : GX * (side + 1)] = gx[0, side : side + 1, :].astype(F32)
        record[6:7, long_start : long_start + MIG] = mx[0, side : side + 1, :].astype(F32)
        for again in range(2):
            start = NARROW_SLOTS.start + MIG * (side + 2 * again)
            record[6:7, start : start + MIG] = my[0, side : side + 1, :].astype(F32)
        record[7:8, HALF * side : HALF * side + GY] = gy[0, side : side + 1, :].astype(F32)
    message[...] = leavers(record[...], LONG_SLOTS, 0)


def crossed(record, from_lower, from_upper):
    lane = lax.broadcasted_iota(I32, record.shape, 1)
    moved = place(lane, record, record[6:7, LONG_SLOTS].astype(I32), from_lower, from_upper)
    return jnp.where(lax.broadcasted_iota(I32, record.shape, 0) < 6, moved, record)


AREAS = [slice(LANES * k, LANES * (k + 1)) for k in range(4)]


def cross_kernel(par, kept, joined, own_out, out, block):
    p = par[0]
    own = kept[:, 0:OWN]
    other = joined[:, 0:OWN]
    near_side = kept[:, OWN : OWN + LANES]
    far_side = joined[:, OWN : OWN + LANES]
    from_other = leavers(other, LONG_SLOTS, 0)
    from_own = leavers(own, LONG_SLOTS, 0)
    own = crossed(own, by_parity(p, from_other, near_side), by_parity(p, near_side, from_other))
    other = crossed(other, by_parity(p, far_side, from_own), by_parity(p, from_own, far_side))
    own_out[...] = own
    block[0:3, :] = own[0:3, :]
    block[3:4, :] = own[7:8, :]
    for area, record in ((AREAS[0], other), (AREAS[1], own)):
        chosen = by_parity(p, ghost_list(record, 0), ghost_list(record, 1))
        block[4:7, area] = take_lanes(value_reader(record), 8, OWN // LANES, chosen)[0:3, :]
        block[7:8, area] = chosen.astype(F32)
    lane = lax.broadcasted_iota(I32, (3, LANES), 1)
    for area, record in ((AREAS[2], own), (AREAS[3], other)):
        leave = leavers(record, NARROW_SLOTS, 1)
        block[4:7, area] = jnp.where(lane < 2 * MIG, leave[0:3, :], leave[3:6, :])
        block[7:8, area] = record[6:7, NARROW_SLOTS]
    for b in range(out.shape[0]):
        out[b] = block[...]


def settle(par, blocks, record, narrow_count, bundle, table, inner):
    p = par[0]

    def number(member, narrow_step):
        return member * narrow_count + lax.rem(par[2] + (narrow_step + narrow_count), narrow_count)

    def settled(member, narrow_step, spots, values, leave, base=0):
        slots = blocks[number(member, narrow_step), 7:8, leave].astype(I32)
        from_lower = blocks[number(member, narrow_step - 1), 4:7, leave]
        from_upper = blocks[number(member, narrow_step + 1), 4:7, leave]
        return place(spots, values, slots, from_lower, from_upper, base)

    lane = lax.broadcasted_iota(I32, (3, OWN), 1)
    inner[...] = jnp.zeros(inner.shape, F32)
    toward = by_parity(p, -1.0, 1.0)
    for narrow_step in (-1, 1, 0):
        here = number(p, narrow_step)
        there = number(1 - p, narrow_step)
        middle = settled(p, narrow_step, lane, blocks[here, 0:3, :], AREAS[2])
        second = settled(
            p, narrow_step, blocks[here, 7:8, AREAS[0]].astype(I32), blocks[here, 4:7, AREAS[0]], AREAS[3]
        ) + unit_row(3, 0, toward)
        first = settled(
            1 - p, narrow_step, blocks[there, 7:8, AREAS[1]].astype(I32), blocks[there, 4:7, AREAS[1]], AREAS[2]
        ) - unit_row(3, 0, toward)
        inner[0:3, 0:OWN] = middle
        inner[0:3, OWN : OWN + GX] = by_parity(p, second, first)
        inner[0:3, OWN + GX : INNER] = by_parity(p, first, second)
        if narrow_step == 0:
            bundle[0:3, :] = middle
            bundle[3:6, :] = settled(p, 0, lane, record[3:6, :], AREAS[2], 2 * MIG)
            bundle[6:8, :] = record[6:8, :]
            table[:, 0:INNER] = inner[...]
            continue
        side = 0 if narrow_step < 0 else 1
        chosen = blocks[here, 3:4, HALF * side : HALF * (side + 1)].astype(I32)
        taken = jnp.concatenate(
            [
                take_lanes(tile_reader(inner), 8, INNER // LANES, chosen[:, LANES * c : LANES * (c + 1)])
                for c in range(2)
            ],
            axis=1,
        )
        base = INNER + GY * side
        table[:, base : base + GY] = taken[:, 0:GY] + unit_row(8, 1, float(narrow_step))


def narrow_messages(par, table, rows, gy, one, two):
    p = par[1]
    for out, chosen in (
        (one, by_parity(p, gy[0:1, :], gy[1:2, :])),
        (two, by_parity(p, gy[1:2, :], gy[0:1, :])),
    ):
        for c in range(2):
            out[:, LANES * c : LANES * (c + 1)] = take_lanes(
                tile_reader(table), rows, INNER // LANES, chosen[:, LANES * c : LANES * (c + 1)]
            )


def inner_table(par, own, one, two, table):
    p = par[0]
    table[:, 0:OWN] = own
    table[:, OWN : OWN + GX] = by_parity(p, two[...], one[...])
    table[:, OWN + GX : INNER] = by_parity(p, one[...], two[...])


def outer_table(par, one, two, table):
    p = par[1]
    table[:, INNER : INNER + GY] = by_parity(p, two[:, 0:GY], one[:, 0:GY])
    table[:, INNER + GY : EXT] = by_parity(p, one[:, 0:GY], two[:, 0:GY])


def ghost_kernel(par, own, one_in, two_in, gy, one, two, table):
    inner_table(par, own[...], one_in, two_in, table)
    narrow_messages(par, table, own.shape[0], gy, one, two)


def product(left, right):
    return lax.dot_general(left, right, (((1,), (0,)), ((), ())), preferred_element_type=F32)


def centres():
    return lax.broadcasted_iota(I32, (NB, 1), 0).astype(F32) * (CENTRE_SPAN / (NB - 1))


def basis_rows(radial, last):
    high = radial.astype(BF16).astype(F32)
    return jnp.concatenate([high, radial - high, high, last], axis=0)


def slope_kernel(half, par, square, geo, basis, slope):
    lanes = slice(HALF * half, HALF * (half + 1))
    centre = centres()
    ones = jnp.ones((NB, HALF), F32)
    left = basis[...]

    def turn(n, carry):
        offset = square[pl.ds(n, 1), lanes] - centre
        weight = geo[3, pl.ds(n, 1), lanes]
        radial = jnp.exp(-(offset * offset))
        right = [basis_rows(radial, ones), basis_rows(-2.0 * offset * radial, 0.0 * ones)]
        both = product(left, jnp.concatenate(right, axis=1).astype(BF16))
        value = both[:, :HALF]
        gate = 0.5 * jnp.tanh(0.5 * value) + 0.5
        raw = value * gate
        slope[n] = weight * ((gate + raw * (1.0 - gate)) * both[:, HALF:] - raw * weight)
        return carry

    lax.fori_loop(0, NEI, turn, 0, unroll=UNROLL_ENV)


def grouped(ref, g):
    return jnp.concatenate([ref[GROUP * g + j] for j in range(GROUP)], axis=1)


def first_kernel(par, latent, pair_ahead, columns, first):
    left = pair_ahead[...]
    bias = columns[:, 0:1]

    def turn(g, carry):
        sums = product(left, grouped(latent, g))
        for j in range(GROUP):
            lanes = slice(OWN * j, OWN * (j + 1))
            first[GROUP * g + j] = sums[:H, lanes] + sums[H:, lanes] + bias
        return carry

    lax.fori_loop(0, NEI // GROUP, turn, 0)


def rise_kernel(par, dvalue, part, slope1, slope2, pair_back, rise):
    left = pair_back[...]

    def turn(g, carry):
        sums = product(left, grouped(dvalue, g))
        for j in range(GROUP):
            n = GROUP * g + j
            for half, slope in enumerate((slope1, slope2)):
                lanes = slice(HALF * half, HALF * (half + 1))
                wide = slice(OWN * j + HALF * half, OWN * j + HALF * (half + 1))
                dlatent = sums[:H, wide] + sums[H:, wide]
                total = jnp.sum(dlatent * slope[n], axis=0, keepdims=True)
                rise[pl.ds(n, 1), lanes] = total + part[pl.ds(n, 1), lanes]
        return carry

    lax.fori_loop(0, NEI // GROUP, turn, 0)


def env_kernel(
    narrow_count, par, blocks, record, nbr, basis, w_embed,
    own, gx, gy, embed, one, two, latent_out, geo, square, table, inner,
):
    settle(par, blocks, record, narrow_count, own, table, inner)
    for side in range(2):
        gx[side : side + 1, :] = ghost_list(own, side)
        gy[side : side + 1, :] = narrow_list(own, side)
    for b in range(OWN // LANES):
        lanes = slice(LANES * b, LANES * (b + 1))
        for q in range(NEI // 8):
            rows = slice(8 * q, 8 * q + 8)
            index = nbr[rows, lanes]
            low = index & (LANES - 1)
            high = index >> 7
            total = jnp.zeros((8, LANES), F32)
            for c in range(3):
                taken = jnp.zeros((8, LANES), F32)
                for g in range(GROUPS):
                    tile = jnp.broadcast_to(table[c : c + 1, LANES * g : LANES * (g + 1)], (8, LANES))
                    taken = jnp.where(high == g, lane_take(tile, low), taken)
                apart = taken - own[c : c + 1, lanes]
                geo[c, rows, lanes] = apart
                total = total + apart * apart
            square[rows, lanes] = total
            geo[3, rows, lanes] = jnp.where(index >= 0, 1.0 / (1.0 + total), 0.0)

    centre = centres()
    ones = jnp.ones((NB, ENV_WIDTH), F32)
    left = basis[...]
    for half in range(OWN // ENV_WIDTH):
        lanes = slice(ENV_WIDTH * half, ENV_WIDTH * (half + 1))

        def turn(n, gathered):
            offset = square[pl.ds(n, 1), lanes] - centre
            value = product(left, basis_rows(jnp.exp(-(offset * offset)), ones).astype(BF16))
            gate = 0.5 * jnp.tanh(0.5 * value) + 0.5
            latent = value * gate * geo[3, pl.ds(n, 1), lanes]
            high, low = half_split(latent)
            latent_out[n, 0:H, lanes] = high
            latent_out[n, H : 2 * H, lanes] = low
            return gathered + latent

        gathered = lax.fori_loop(0, NEI, turn, jnp.zeros((H, ENV_WIDTH), F32), unroll=ENV_TURNS)
        environ = gathered * (1.0 / math.sqrt(NEI))
        embed[:, lanes] = jnp.dot(w_embed[...], environ, precision=HIGHEST, preferred_element_type=F32)
    p = par[0]
    reader = tile_reader(embed)
    one[...] = take_lanes(reader, EMB, OWN // LANES, by_parity(p, gx[0:1, :], gx[1:2, :]))
    two[...] = take_lanes(reader, EMB, OWN // LANES, by_parity(p, gx[1:2, :], gx[0:1, :]))


def hot_rows(low_row):
    level = lax.broadcasted_iota(I32, (HALF, low_row.shape[1]), 0)
    return jnp.where(level == low_row, 1.0, 0.0).astype(BF16)


def level_rows(value, high_row):
    pieces = []
    for k in range(LEVELS):
        mask = jnp.where(high_row == k, 1.0, 0.0).astype(BF16)
        pieces.append(value * mask)
    return jnp.concatenate(pieces, axis=0)


def pair_kernel(
    par, own, gx1, gx2, gy1, gy2, nbr, first, geo, ahead, back, columns,
    dvalue_out, part, inner, one, two, table, spread_sum, own_sum,
):
    inner_table(par, own[...], gx1, gx2, table)
    outer_table(par, gy1, gy2, table)
    spread_sum[...] = jnp.zeros(spread_sum.shape, F32)
    own_sum[...] = jnp.zeros(own_sum.shape, F32)
    left = ahead[...]
    right_back = back[...]
    readout = columns[:, 1:2]

    def rows_of(read, start, count):
        return jnp.concatenate([read(start + j) for j in range(count)], axis=1)

    def scatter(g, joined):
        index = rows_of(lambda n: nbr[pl.ds(n, 1), :], PAIR_GROUP * g, PAIR_GROUP)
        spread_sum[...] += lax.dot_general(
            level_rows(joined, index >> 8), hot_rows(index & (HALF - 1)),
            (((1,), (1,)), ((), ())), preferred_element_type=F32,
        )

    def chunk(n):
        index = rows_of(lambda m: nbr[pl.ds(m, 1), :], n, SPAN)
        weight = rows_of(lambda m: geo[3, pl.ds(m, 1), :], n, SPAN)
        partner = jnp.concatenate(
            [
                take_lanes(tile_reader(table), EMB, GROUPS, index[:, LANES * c : LANES * (c + 1)])
                for c in range(SPAN * OWN // LANES)
            ],
            axis=1,
        )
        embed_own = jnp.concatenate([own[...]] * SPAN, axis=1)
        product_high, product_low = half_split(partner * embed_own)
        sums = product(left, jnp.concatenate([product_high, product_low], axis=0))
        value = rows_of(lambda m: first[m], n, SPAN) + sums[:H] + sums[H:]
        gate = 0.5 * jnp.tanh(0.5 * value) + 0.5
        hidden = value * gate
        dvalue = (gate + hidden * (1.0 - gate)) * (readout * weight)
        dhigh, dlow = half_split(dvalue)
        dvalue = jnp.concatenate([dhigh, dlow], axis=0)
        sums = product(right_back, dvalue)
        dproduct = sums[:EMB] + sums[EMB:]
        partial = -(weight * weight) * jnp.sum(hidden * readout, axis=0, keepdims=True)
        more = dproduct * partner
        for j in range(SPAN):
            lanes = slice(OWN * j, OWN * (j + 1))
            dvalue_out[n + j] = dvalue[:, lanes]
            part[pl.ds(n + j, 1), :] = partial[:, lanes]
            own_sum[...] += more[:, lanes]
        high, low = half_split(dproduct * embed_own)
        return jnp.concatenate([high, low], axis=0)

    def turn(g, joined):
        scatter(jnp.maximum(g - 1, 0), joined)
        return jnp.concatenate([chunk(PAIR_GROUP * g + SPAN * j) for j in range(PAIR_GROUP // SPAN)], axis=1)

    joined = lax.fori_loop(0, NEI // PAIR_GROUP, turn, jnp.zeros((2 * EMB, PAIR_GROUP * OWN), BF16))
    scatter(NEI // PAIR_GROUP - 1, joined)
    for k in range(LEVELS):
        base = 2 * EMB * k
        width = min(HALF, EXT - HALF * k)
        table[:, HALF * k : HALF * k + width] = (
            spread_sum[base : base + EMB, :width] + spread_sum[base + EMB : base + 2 * EMB, :width]
        )
    inner[:, 0:OWN] = table[:, 0:OWN] + own_sum[...]
    inner[:, OWN:INNER] = table[:, OWN:INNER]
    outer_messages(par, table, one, two)


def outer_messages(par, table, one, two):
    p = par[1]
    down = table[:, INNER : INNER + GY]
    up = table[:, INNER + GY : EXT]
    one[...] = by_parity(p, up, down)
    two[...] = by_parity(p, down, up)


def fold_narrow(par, inner, one, two, gy):
    p = par[1]
    from_upper = by_parity(p, one[...], two[...])
    from_lower = by_parity(p, two[...], one[...])
    return (
        inner[...]
        + spread(from_upper, gy[0:1, 0:GY], INNER)
        + spread(from_lower, gy[1:2, 0:GY], INNER)
    )


def fold_long(par, own, one, two, gx):
    p = par[0]
    from_upper = by_parity(p, one[...], two[...])
    from_lower = by_parity(p, two[...], one[...])
    return own[...] + spread(from_upper, gx[0:1, :], OWN) + spread(from_lower, gx[1:2, :], OWN)


def fold_kernel(par, inner, one_in, two_in, gy, own, one, two):
    total = fold_narrow(par, inner, one_in, two_in, gy)
    own[...] = total[:, 0:OWN]
    down = total[:, OWN : OWN + GX]
    up = total[:, OWN + GX : INNER]
    p = par[0]
    one[...] = by_parity(p, up, down)
    two[...] = by_parity(p, down, up)


def force_kernel(
    par, own_in, gx1, gx2, gx, w_back, slope1, slope2, rise, geo, nbr,
    inner, one, two, table, spread_sum, pushes, grown,
):
    grad = fold_long(par, own_in, gx1, gx2, gx)
    grown[...] = jnp.dot(w_back[...], grad, precision=HIGHEST, preferred_element_type=F32) * (1.0 / math.sqrt(NEI))
    spread_sum[...] = jnp.zeros(spread_sum.shape, F32)
    pushes[...] = jnp.zeros(pushes.shape, F32)

    def turn(g, carry):
        lifted = []
        hot = []
        pushed = pushes[...]
        for j in range(FORCE_GROUP):
            n = FORCE_GROUP * g + j
            rate = jnp.concatenate(
                [
                    jnp.sum(slope[n] * grown[:, HALF * h : HALF * (h + 1)], axis=0, keepdims=True)
                    for h, slope in enumerate((slope1, slope2))
                ],
                axis=1,
            )
            twice = 2.0 * (rate + rise[pl.ds(n, 1), :])
            push = [geo[c, pl.ds(n, 1), :] * twice for c in range(3)]
            highs = [v.astype(BF16).astype(F32) for v in push]
            rows = highs + [v - h for v, h in zip(push, highs)]
            value = jnp.concatenate(rows + [jnp.zeros((2, OWN), F32)], axis=0)
            pushed = pushed + value
            index = nbr[pl.ds(n, 1), :]
            high_row = index >> 8
            hot.append(hot_rows(index & (HALF - 1)))
            lifted.append(
                jnp.concatenate([jnp.where(high_row == k, value, 0.0) for k in range(LEVELS)], axis=0).astype(BF16)
            )
        pushes[...] = pushed
        spread_sum[...] += lax.dot_general(
            jnp.concatenate(lifted, axis=1), jnp.concatenate(hot, axis=1), (((1,), (1,)), ((), ())), preferred_element_type=F32
        )
        return carry

    lax.fori_loop(0, NEI // FORCE_GROUP, turn, 0)
    table[...] = jnp.zeros(table.shape, F32)
    for k in range(LEVELS):
        width = min(HALF, EXT - HALF * k)
        table[0:3, HALF * k : HALF * k + width] = (
            spread_sum[8 * k : 8 * k + 3, :width] + spread_sum[8 * k + 3 : 8 * k + 6, :width]
        )
    table[0:3, 0:OWN] = table[0:3, 0:OWN] - pushes[0:3, :] - pushes[3:6, :]
    inner[...] = table[:, 0:INNER]
    outer_messages(par, table, one, two)


def final_kernel(par, own, one, two, gx, bundle, pos_out, vel_out, frc_out):
    forces = -fold_long(par, own, one, two, gx)[0:3, :]
    pos_out[...] = bundle[0:3, :]
    vel_out[...] = bundle[3:6, :] + (0.5 * TIME_STEP) * forces
    frc_out[...] = forces


def call(kernel, name, shapes, scratch, *operands, far=(), limit=BIG):
    specs = [pl.BlockSpec(memory_space=pltpu.HBM if k in far else pltpu.VMEM) for k in range(len(operands))]

    def placed(*refs):
        column = lax.axis_index("gy")
        kernel((lax.rem(lax.axis_index("gx"), 2), lax.rem(column, 2), column), *refs)

    return pl.pallas_call(
        placed,
        name=name,
        out_shape=[jax.ShapeDtypeStruct(shape, kind) for shape, kind in shapes],
        in_specs=specs,
        out_specs=[pl.BlockSpec(memory_space=pltpu.VMEM)] * len(shapes),
        scratch_shapes=[
            pltpu.SemaphoreType.DMA(shape) if kind is None else pltpu.VMEM(shape, kind) for shape, kind in scratch
        ],
        compiler_params=pltpu.CompilerParams(vmem_limit_bytes=limit),
    )(*operands)


def holds(*arrays):
    return [(a.shape, a.dtype) for a in arrays] + [((len(arrays),), None)]


def swap(axis, first):
    count = lax.axis_size(axis)
    offset = 0 if first else 1
    route = []
    for i in range(count):
        route.append((i, (((i + offset) ^ 1) - offset) % count))
    return route


def exchange(axis, one, two):
    two = lax.ppermute(two, axis, swap(axis, False))
    one = lax.ppermute(one, axis, swap(axis, True))
    two, one = lax.optimization_barrier((two, one))
    return one, two


def on_device(
    positions, velocities, forces, neighbours, ghost_x, ghost_y, migrate_x, migrate_y,
    w_basis, b_basis, w_embed, w_pair, w_mix, b_pair, w_out,
):
    narrow_count = lax.axis_size("gy")
    tile = ((8, LANES), F32)
    wide = ((8, OWN), F32)
    given = (positions, velocities, forces, ghost_x, ghost_y, migrate_x, migrate_y)
    record, message = call(
        start_kernel, "start", [wide, tile], holds(*given), *given,
        far=range(len(given)), limit=WHOLE,
    )
    given = (
        w_basis.T, w_pair, w_mix.T, w_embed, jnp.stack([b_basis, b_pair, w_out]),
    )
    doubled = ((2 * H, 2 * H), BF16)
    near, basis, pair_ahead, mix_ahead, pair_back, mix_back, w_ahead, w_back, columns = call(
        prepare_kernel,
        "prepare",
        [
            ((NEI, OWN), I32), ((H, 4 * NB), BF16), doubled, ((2 * H, 2 * EMB), BF16), doubled, ((2 * EMB, 2 * H), BF16),
            ((EMB, H), F32), ((H, EMB), F32), ((H, NB), F32),
        ],
        holds(*given), neighbours, *given, far=range(1, len(given) + 1),
    )
    message = lax.ppermute(message, "gx", swap("gx", True))
    mine = jnp.concatenate([record, message], axis=1)
    joined = lax.ppermute(mine, "gx", swap("gx", False))
    group = 2 * narrow_count
    own, blocks = call(cross_kernel, "cross", [wide, ((group, 8, OWN), F32)], [wide], mine, joined)
    members = [list(range(group * k, group * (k + 1))) for k in range(lax.axis_size("gx") // 2)]
    blocks = lax.all_to_all(blocks, ("gx", "gy"), 0, 0, axis_index_groups=members)

    bundle, gx, gy, embed, one, two, latent, geo, square = call(
        lambda *refs: env_kernel(narrow_count, *refs),
        "env",
        [
            wide, ((2, GX), I32), ((2, HALF), I32), ((EMB, OWN), F32), ((EMB, GX), F32), ((EMB, GX), F32),
            ((NEI, 2 * H, OWN), BF16), ((4, NEI, OWN), F32), ((NEI, OWN), F32),
        ],
        [((8, EXT), F32), ((8, INNER), F32)],
        blocks, own, near, basis, w_ahead,
    )
    (first,) = call(first_kernel, "first", [((NEI, H, OWN), F32)], [], latent, pair_ahead, columns)
    slopes = [
        call(
            lambda *refs, half=half: slope_kernel(half, *refs), f"slope{half}", [((NEI, H, HALF), F32)], [],
            square, geo, basis,
        )[0]
        for half in range(OWN // HALF)
    ]
    ex = exchange("gx", one, two)
    *ex, slopes[0] = lax.optimization_barrier((*ex, slopes[0]))
    message = ((EMB, HALF), F32)
    one, two = call(
        ghost_kernel, "ghost_embed", [message, message], [((EMB, INNER), F32)],
        embed, *ex, gy,
    )
    ey = exchange("gy", one, two)
    message = ((EMB, GY), F32)
    dvalue, part, inner, one, two = call(
        pair_kernel,
        "pair",
        [((NEI, 2 * H, OWN), BF16), ((NEI, OWN), F32), ((EMB, INNER), F32), message, message],
        [((EMB, EXT), F32), ((LEVELS * 2 * EMB, HALF), F32), ((EMB, OWN), F32)],
        embed, *ex, *ey, near, first, geo, mix_ahead, mix_back, columns,
    )
    one, two = exchange("gy", one, two)
    one, two, slopes[1] = lax.optimization_barrier((one, two, slopes[1]))
    (rise,) = call(rise_kernel, "rise", [((NEI, OWN), F32)], [], dvalue, part, *slopes, pair_back)
    message = ((EMB, GX), F32)
    own, one, two = call(
        fold_kernel, "fold_embed", [((EMB, OWN), F32), message, message], [], inner, one, two, gy
    )
    one, two = exchange("gx", one, two)
    message = ((8, GY), F32)
    inner, one, two = call(
        force_kernel,
        "force",
        [((8, INNER), F32), message, message],
        [((8, EXT), F32), ((8 * LEVELS, HALF), F32), ((8, OWN), F32), ((H, OWN), F32)],
        own, one, two, gx, w_back, *slopes, rise, geo, near,
    )
    one, two = exchange("gy", one, two)
    own, one, two = call(fold_kernel, "fold_force", [wide, tile, tile], [], inner, one, two, gy)
    one, two = exchange("gx", one, two)
    flat = ((3, OWN), F32)
    return tuple(call(final_kernel, "final", [flat, flat, flat], [], own, one, two, gx, bundle))


def solution(mesh):
    both = ("gx", "gy")
    flat = P(None, both)
    stacked = P(None, None, both)
    return jax.shard_map(
        on_device,
        mesh=mesh,
        in_specs=(flat,) * 3 + (stacked,) * 5 + (P(),) * 7,
        out_specs=(flat,) * 3,
        check_vma=False,
    )
```

```python
import math

import jax
import jax.numpy as jnp
from jax import lax
from jax.experimental import pallas as pl
from jax.experimental.pallas import tpu as pltpu
from jax.sharding import PartitionSpec as P

F32 = jnp.float32
BF16 = jnp.bfloat16
I32 = jnp.int32

TIME_STEP = 0.05
CENTRE_SPAN = 3.0
HIGHEST = lax.Precision.HIGHEST

NB = 8
NEI = 32
H = 64
EMB = 32
OWN = 512
GX = 128
GY = 192
MIG = 8
LANES = 128
INNER = OWN + 2 * GX
EXT = INNER + 2 * GY
GROUPS = EXT // LANES
HALF = 256
LEVELS = -(-EXT // HALF)
BIG = 24 * 1024 * 1024
WHOLE = 60 * 1024 * 1024
GROUP = 8
PAIR_GROUP = 16
SPAN = 2
FORCE_GROUP = 16
UNROLL_ENV = 8
ENV_WIDTH = 256
ENV_TURNS = 16


def half_split(value):
    high = value.astype(BF16)
    low = (value - high.astype(F32)).astype(BF16)
    return high, low


def third_split(value):
    high = value.astype(BF16)
    rest = value - high.astype(F32)
    middle = rest.astype(BF16)
    low = (rest - middle.astype(F32)).astype(BF16)
    return high, middle, low


def lane_take(table, index):
    return jnp.take_along_axis(table, index, axis=1, mode="promise_in_bounds")


def take_lanes(read, rows, groups, index_row):
    low = jnp.broadcast_to(index_row & (LANES - 1), (8, LANES))
    high = jnp.broadcast_to(index_row >> 7, (8, LANES))
    pieces = []
    for r in range(rows // 8):
        taken = jnp.zeros((8, LANES), F32)
        for g in range(groups):
            taken = jnp.where(high == g, lane_take(read(r, g), low), taken)
        pieces.append(taken)
    return jnp.concatenate(pieces, axis=0) if len(pieces) > 1 else pieces[0]


def tile_reader(ref):
    return lambda r, g: ref[8 * r : 8 * r + 8, LANES * g : LANES * (g + 1)]


def spread(values, lists, width):
    count = values.shape[1]
    hot = jnp.where(lax.broadcasted_iota(I32, (width, count), 0) == lists, 1.0, 0.0).astype(BF16)
    total = None
    for part in third_split(values):
        piece = lax.dot_general(part, hot, (((1,), (1,)), ((), ())), preferred_element_type=F32)
        total = piece if total is None else total + piece
    return total


def by_parity(parity, even, odd):
    return jnp.where(parity == 0, even, odd)


def unit_row(rows, row, amount):
    return jnp.where(lax.broadcasted_iota(I32, (rows, 1), 0) == row, amount, 0.0)


def place(spots, values, slots, from_lower, from_upper, base=0):
    for k in range(MIG):
        down = slice(MIG + k, MIG + k + 1)
        up = slice(k, k + 1)
        message_up = from_lower[:, base + k : base + k + 1]
        message_down = from_upper[:, base + MIG + k : base + MIG + k + 1]
        values = jnp.where(spots == slots[:, down], message_up, values)
        values = jnp.where(spots == slots[:, up], message_down, values)
    return values


def value_reader(value):
    return lambda r, g: value[8 * r : 8 * r + 8, LANES * g : LANES * (g + 1)]


LONG_SLOTS = slice(2 * GX, 2 * GX + LANES)
NARROW_SLOTS = slice(2 * GX + LANES, 2 * GX + 2 * LANES)


def ghost_list(record, side):
    return record[6:7, GX * side : GX * (side + 1)].astype(I32)


def narrow_list(record, side):
    return record[7:8, HALF * side : HALF * (side + 1)].astype(I32)


def leavers(record, lanes, row):
    lane = lax.broadcasted_iota(I32, (8, LANES), 1) & (2 * MIG - 1)
    shift = jnp.where(lane < MIG, -1.0, 1.0)
    rows = lax.broadcasted_iota(I32, (8, LANES), 0)
    taken = take_lanes(value_reader(record), 8, OWN // LANES, record[6:7, lanes].astype(I32))
    return taken + jnp.where(rows == row, shift, 0.0)


def fetch(sources, targets, sems):
    copies = [pltpu.make_async_copy(src, dst, sems.at[k]) for k, (src, dst) in enumerate(zip(sources, targets))]
    for copy in copies:
        copy.start()
    for copy in copies:
        copy.wait()


def prepare_kernel(
    par, neighbours, basis_t, pair, mix_t, w_embed, vectors, near, basis, pair_ahead, mix_ahead, pair_back, mix_back, w_ahead, w_back, columns, *scratch
):
    held = scratch[:-1]
    near[...] = neighbours[0]
    fetch((basis_t, pair, mix_t, w_embed, vectors), held, scratch[-1])
    basis_t, pair, mix_t, w_embed, vectors = held
    b_basis = vectors[0:1, :]
    high, low = half_split(basis_t[...])
    high, low = high.astype(F32), low.astype(F32)
    parts = [part.astype(F32) for part in third_split(b_basis)]
    parts = jnp.concatenate(parts + [jnp.zeros((NB - 3, H), F32)], axis=0)
    basis[...] = jnp.concatenate([high, high, low, parts], axis=0).T.astype(BF16)
    rows = jnp.concatenate([vectors[1:3, :], jnp.zeros((NB - 2, H), F32)], axis=0)
    columns[...] = rows.T
    w_ahead[...] = w_embed[...]
    w_back[...] = w_embed[...].T
    for layer_t, ahead, back in ((pair[...].T, pair_ahead, pair_back), (mix_t[...], mix_ahead, mix_back)):
        high, low = half_split(layer_t)
        high, low = high.astype(F32), low.astype(F32)
        nothing = jnp.zeros(high.shape, F32)
        back[...] = jnp.concatenate(
            [jnp.concatenate([high, high], axis=1), jnp.concatenate([low, nothing], axis=1)], axis=0
        ).astype(BF16)
        ahead[0:H, :] = jnp.concatenate([high, high], axis=0).T.astype(BF16)
        ahead[H : 2 * H, :] = jnp.concatenate([low, nothing], axis=0).T.astype(BF16)


def start_kernel(par, pos, vel, frc, gx, gy, mx, my, record, message, *scratch):
    held = scratch[:-1]
    fetch((pos, vel, frc, gx, gy, mx, my), held, scratch[-1])
    pos, vel, frc, gx, gy, mx, my = held
    speeds = vel[...] + (0.5 * TIME_STEP) * frc[...]
    record[0:3, :] = pos[...] + TIME_STEP * speeds
    record[3:6, :] = speeds
    record[6:8, :] = jnp.zeros((2, OWN), F32)
    for side in range(2):
        long_start = LONG_SLOTS.start + MIG * side
        record[6:7, GX * side : GX * (side + 1)] = gx[0, side : side + 1, :].astype(F32)
        record[6:7, long_start : long_start + MIG] = mx[0, side : side + 1, :].astype(F32)
        for again in range(2):
            start = NARROW_SLOTS.start + MIG * (side + 2 * again)
            record[6:7, start : start + MIG] = my[0, side : side + 1, :].astype(F32)
        record[7:8, HALF * side : HALF * side + GY] = gy[0, side : side + 1, :].astype(F32)
    message[...] = leavers(record[...], LONG_SLOTS, 0)


def crossed(record, from_lower, from_upper):
    lane = lax.broadcasted_iota(I32, record.shape, 1)
    moved = place(lane, record, record[6:7, LONG_SLOTS].astype(I32), from_lower, from_upper)
    return jnp.where(lax.broadcasted_iota(I32, record.shape, 0) < 6, moved, record)


AREAS = [slice(LANES * k, LANES * (k + 1)) for k in range(4)]


def cross_kernel(par, kept, joined, own_out, out, block):
    p = par[0]
    own = kept[:, 0:OWN]
    other = joined[:, 0:OWN]
    near_side = kept[:, OWN : OWN + LANES]
    far_side = joined[:, OWN : OWN + LANES]
    from_other = leavers(other, LONG_SLOTS, 0)
    from_own = leavers(own, LONG_SLOTS, 0)
    own = crossed(own, by_parity(p, from_other, near_side), by_parity(p, near_side, from_other))
    other = crossed(other, by_parity(p, far_side, from_own), by_parity(p, from_own, far_side))
    own_out[...] = own
    block[0:3, :] = own[0:3, :]
    block[3:4, :] = own[7:8, :]
    for area, record in ((AREAS[0], other), (AREAS[1], own)):
        chosen = by_parity(p, ghost_list(record, 0), ghost_list(record, 1))
        block[4:7, area] = take_lanes(value_reader(record), 8, OWN // LANES, chosen)[0:3, :]
        block[7:8, area] = chosen.astype(F32)
    lane = lax.broadcasted_iota(I32, (3, LANES), 1)
    for area, record in ((AREAS[2], own), (AREAS[3], other)):
        leave = leavers(record, NARROW_SLOTS, 1)
        block[4:7, area] = jnp.where(lane < 2 * MIG, leave[0:3, :], leave[3:6, :])
        block[7:8, area] = record[6:7, NARROW_SLOTS]
    for b in range(out.shape[0]):
        out[b] = block[...]


def settle(par, blocks, record, narrow_count, bundle, table, inner):
    p = par[0]

    def number(member, narrow_step):
        return member * narrow_count + lax.rem(par[2] + (narrow_step + narrow_count), narrow_count)

    def settled(member, narrow_step, spots, values, leave, base=0):
        slots = blocks[number(member, narrow_step), 7:8, leave].astype(I32)
        from_lower = blocks[number(member, narrow_step - 1), 4:7, leave]
        from_upper = blocks[number(member, narrow_step + 1), 4:7, leave]
        return place(spots, values, slots, from_lower, from_upper, base)

    lane = lax.broadcasted_iota(I32, (3, OWN), 1)
    inner[...] = jnp.zeros(inner.shape, F32)
    toward = by_parity(p, -1.0, 1.0)
    for narrow_step in (-1, 1, 0):
        here = number(p, narrow_step)
        there = number(1 - p, narrow_step)
        middle = settled(p, narrow_step, lane, blocks[here, 0:3, :], AREAS[2])
        second = settled(
            p, narrow_step, blocks[here, 7:8, AREAS[0]].astype(I32), blocks[here, 4:7, AREAS[0]], AREAS[3]
        ) + unit_row(3, 0, toward)
        first = settled(
            1 - p, narrow_step, blocks[there, 7:8, AREAS[1]].astype(I32), blocks[there, 4:7, AREAS[1]], AREAS[2]
        ) - unit_row(3, 0, toward)
        inner[0:3, 0:OWN] = middle
        inner[0:3, OWN : OWN + GX] = by_parity(p, second, first)
        inner[0:3, OWN + GX : INNER] = by_parity(p, first, second)
        if narrow_step == 0:
            bundle[0:3, :] = middle
            bundle[3:6, :] = settled(p, 0, lane, record[3:6, :], AREAS[2], 2 * MIG)
            bundle[6:8, :] = record[6:8, :]
            table[:, 0:INNER] = inner[...]
            continue
        side = 0 if narrow_step < 0 else 1
        chosen = blocks[here, 3:4, HALF * side : HALF * (side + 1)].astype(I32)
        taken = jnp.concatenate(
            [
                take_lanes(tile_reader(inner), 8, INNER // LANES, chosen[:, LANES * c : LANES * (c + 1)])
                for c in range(2)
            ],
            axis=1,
        )
        base = INNER + GY * side
        table[:, base : base + GY] = taken[:, 0:GY] + unit_row(8, 1, float(narrow_step))


def narrow_messages(par, table, rows, gy, one, two):
    p = par[1]
    for out, chosen in (
        (one, by_parity(p, gy[0:1, :], gy[1:2, :])),
        (two, by_parity(p, gy[1:2, :], gy[0:1, :])),
    ):
        for c in range(2):
            out[:, LANES * c : LANES * (c + 1)] = take_lanes(
                tile_reader(table), rows, INNER // LANES, chosen[:, LANES * c : LANES * (c + 1)]
            )


def inner_table(par, own, one, two, table):
    p = par[0]
    table[:, 0:OWN] = own
    table[:, OWN : OWN + GX] = by_parity(p, two[...], one[...])
    table[:, OWN + GX : INNER] = by_parity(p, one[...], two[...])


def outer_table(par, one, two, table):
    p = par[1]
    table[:, INNER : INNER + GY] = by_parity(p, two[:, 0:GY], one[:, 0:GY])
    table[:, INNER + GY : EXT] = by_parity(p, one[:, 0:GY], two[:, 0:GY])


def ghost_kernel(par, own, one_in, two_in, gy, one, two, table):
    inner_table(par, own[...], one_in, two_in, table)
    narrow_messages(par, table, own.shape[0], gy, one, two)


def product(left, right):
    return lax.dot_general(left, right, (((1,), (0,)), ((), ())), preferred_element_type=F32)


def centres():
    return lax.broadcasted_iota(I32, (NB, 1), 0).astype(F32) * (CENTRE_SPAN / (NB - 1))


def basis_rows(radial, last):
    high = radial.astype(BF16).astype(F32)
    return jnp.concatenate([high, radial - high, high, last], axis=0)


def slope_kernel(half, par, square, geo, basis, slope):
    lanes = slice(HALF * half, HALF * (half + 1))
    centre = centres()
    ones = jnp.ones((NB, HALF), F32)
    left = basis[...]

    def turn(n, carry):
        offset = square[pl.ds(n, 1), lanes] - centre
        weight = geo[3, pl.ds(n, 1), lanes]
        radial = jnp.exp(-(offset * offset))
        right = [basis_rows(radial, ones), basis_rows(-2.0 * offset * radial, 0.0 * ones)]
        both = product(left, jnp.concatenate(right, axis=1).astype(BF16))
        value = both[:, :HALF]
        gate = 0.5 * jnp.tanh(0.5 * value) + 0.5
        raw = value * gate
        slope[n] = weight * ((gate + raw * (1.0 - gate)) * both[:, HALF:] - raw * weight)
        return carry

    lax.fori_loop(0, NEI, turn, 0, unroll=UNROLL_ENV)


def grouped(ref, g):
    return jnp.concatenate([ref[GROUP * g + j] for j in range(GROUP)], axis=1)


def first_kernel(par, latent, pair_ahead, columns, first):
    left = pair_ahead[...]
    bias = columns[:, 0:1]

    def turn(g, carry):
        sums = product(left, grouped(latent, g))
        for j in range(GROUP):
            lanes = slice(OWN * j, OWN * (j + 1))
            first[GROUP * g + j] = sums[:H, lanes] + sums[H:, lanes] + bias
        return carry

    lax.fori_loop(0, NEI // GROUP, turn, 0)


def rise_kernel(par, dvalue, part, slope1, slope2, pair_back, rise):
    left = pair_back[...]

    def turn(g, carry):
        sums = product(left, grouped(dvalue, g))
        for j in range(GROUP):
            n = GROUP * g + j
            for half, slope in enumerate((slope1, slope2)):
                lanes = slice(HALF * half, HALF * (half + 1))
                wide = slice(OWN * j + HALF * half, OWN * j + HALF * (half + 1))
                dlatent = sums[:H, wide] + sums[H:, wide]
                total = jnp.sum(dlatent * slope[n], axis=0, keepdims=True)
                rise[pl.ds(n, 1), lanes] = total + part[pl.ds(n, 1), lanes]
        return carry

    lax.fori_loop(0, NEI // GROUP, turn, 0)


def env_kernel(
    narrow_count, par, blocks, record, nbr, basis, w_embed,
    own, gx, gy, embed, one, two, latent_out, geo, square, table, inner,
):
    settle(par, blocks, record, narrow_count, own, table, inner)
    for side in range(2):
        gx[side : side + 1, :] = ghost_list(own, side)
        gy[side : side + 1, :] = narrow_list(own, side)
    for b in range(OWN // LANES):
        lanes = slice(LANES * b, LANES * (b + 1))
        for q in range(NEI // 8):
            rows = slice(8 * q, 8 * q + 8)
            index = nbr[rows, lanes]
            low = index & (LANES - 1)
            high = index >> 7
            total = jnp.zeros((8, LANES), F32)
            for c in range(3):
                taken = jnp.zeros((8, LANES), F32)
                for g in range(GROUPS):
                    tile = jnp.broadcast_to(table[c : c + 1, LANES * g : LANES * (g + 1)], (8, LANES))
                    taken = jnp.where(high == g, lane_take(tile, low), taken)
                apart = taken - own[c : c + 1, lanes]
                geo[c, rows, lanes] = apart
                total = total + apart * apart
            square[rows, lanes] = total
            geo[3, rows, lanes] = jnp.where(index >= 0, 1.0 / (1.0 + total), 0.0)

    centre = centres()
    ones = jnp.ones((NB, ENV_WIDTH), F32)
    left = basis[...]
    for half in range(OWN // ENV_WIDTH):
        lanes = slice(ENV_WIDTH * half, ENV_WIDTH * (half + 1))

        def turn(n, gathered):
            offset = square[pl.ds(n, 1), lanes] - centre
            value = product(left, basis_rows(jnp.exp(-(offset * offset)), ones).astype(BF16))
            gate = 0.5 * jnp.tanh(0.5 * value) + 0.5
            latent = value * gate * geo[3, pl.ds(n, 1), lanes]
            high, low = half_split(latent)
            latent_out[n, 0:H, lanes] = high
            latent_out[n, H : 2 * H, lanes] = low
            return gathered + latent

        gathered = lax.fori_loop(0, NEI, turn, jnp.zeros((H, ENV_WIDTH), F32), unroll=ENV_TURNS)
        environ = gathered * (1.0 / math.sqrt(NEI))
        embed[:, lanes] = jnp.dot(w_embed[...], environ, precision=HIGHEST, preferred_element_type=F32)
    p = par[0]
    reader = tile_reader(embed)
    one[...] = take_lanes(reader, EMB, OWN // LANES, by_parity(p, gx[0:1, :], gx[1:2, :]))
    two[...] = take_lanes(reader, EMB, OWN // LANES, by_parity(p, gx[1:2, :], gx[0:1, :]))


def hot_rows(low_row):
    level = lax.broadcasted_iota(I32, (HALF, low_row.shape[1]), 0)
    return jnp.where(level == low_row, 1.0, 0.0).astype(BF16)


def level_rows(value, high_row):
    pieces = []
    for k in range(LEVELS):
        mask = jnp.where(high_row == k, 1.0, 0.0).astype(BF16)
        pieces.append(value * mask)
    return jnp.concatenate(pieces, axis=0)


def pair_kernel(
    par, own, gx1, gx2, gy1, gy2, nbr, first, geo, ahead, back, columns,
    dvalue_out, part, inner, one, two, table, spread_sum, own_sum,
):
    inner_table(par, own[...], gx1, gx2, table)
    outer_table(par, gy1, gy2, table)
    spread_sum[...] = jnp.zeros(spread_sum.shape, F32)
    own_sum[...] = jnp.zeros(own_sum.shape, F32)
    left = ahead[...]
    right_back = back[...]
    readout = columns[:, 1:2]

    def rows_of(read, start, count):
        return jnp.concatenate([read(start + j) for j in range(count)], axis=1)

    def scatter(g, joined):
        index = rows_of(lambda n: nbr[pl.ds(n, 1), :], PAIR_GROUP * g, PAIR_GROUP)
        spread_sum[...] += lax.dot_general(
            level_rows(joined, index >> 8), hot_rows(index & (HALF - 1)),
            (((1,), (1,)), ((), ())), preferred_element_type=F32,
        )

    def chunk(n):
        index = rows_of(lambda m: nbr[pl.ds(m, 1), :], n, SPAN)
        weight = rows_of(lambda m: geo[3, pl.ds(m, 1), :], n, SPAN)
        partner = jnp.concatenate(
            [
                take_lanes(tile_reader(table), EMB, GROUPS, index[:, LANES * c : LANES * (c + 1)])
                for c in range(SPAN * OWN // LANES)
            ],
            axis=1,
        )
        embed_own = jnp.concatenate([own[...]] * SPAN, axis=1)
        product_high, product_low = half_split(partner * embed_own)
        sums = product(left, jnp.concatenate([product_high, product_low], axis=0))
        value = rows_of(lambda m: first[m], n, SPAN) + sums[:H] + sums[H:]
        gate = 0.5 * jnp.tanh(0.5 * value) + 0.5
        hidden = value * gate
        dvalue = (gate + hidden * (1.0 - gate)) * (readout * weight)
        dhigh, dlow = half_split(dvalue)
        dvalue = jnp.concatenate([dhigh, dlow], axis=0)
        sums = product(right_back, dvalue)
        dproduct = sums[:EMB] + sums[EMB:]
        partial = -(weight * weight) * jnp.sum(hidden * readout, axis=0, keepdims=True)
        more = dproduct * partner
        for j in range(SPAN):
            lanes = slice(OWN * j, OWN * (j + 1))
            dvalue_out[n + j] = dvalue[:, lanes]
            part[pl.ds(n + j, 1), :] = partial[:, lanes]
            own_sum[...] += more[:, lanes]
        high, low = half_split(dproduct * embed_own)
        return jnp.concatenate([high, low], axis=0)

    def turn(g, joined):
        scatter(jnp.maximum(g - 1, 0), joined)
        return jnp.concatenate([chunk(PAIR_GROUP * g + SPAN * j) for j in range(PAIR_GROUP // SPAN)], axis=1)

    joined = lax.fori_loop(0, NEI // PAIR_GROUP, turn, jnp.zeros((2 * EMB, PAIR_GROUP * OWN), BF16))
    scatter(NEI // PAIR_GROUP - 1, joined)
    for k in range(LEVELS):
        base = 2 * EMB * k
        width = min(HALF, EXT - HALF * k)
        table[:, HALF * k : HALF * k + width] = (
            spread_sum[base : base + EMB, :width] + spread_sum[base + EMB : base + 2 * EMB, :width]
        )
    inner[:, 0:OWN] = table[:, 0:OWN] + own_sum[...]
    inner[:, OWN:INNER] = table[:, OWN:INNER]
    outer_messages(par, table, one, two)


def outer_messages(par, table, one, two):
    p = par[1]
    down = table[:, INNER : INNER + GY]
    up = table[:, INNER + GY : EXT]
    one[...] = by_parity(p, up, down)
    two[...] = by_parity(p, down, up)


def fold_narrow(par, inner, one, two, gy):
    p = par[1]
    from_upper = by_parity(p, one[...], two[...])
    from_lower = by_parity(p, two[...], one[...])
    return (
        inner[...]
        + spread(from_upper, gy[0:1, 0:GY], INNER)
        + spread(from_lower, gy[1:2, 0:GY], INNER)
    )


def fold_long(par, own, one, two, gx):
    p = par[0]
    from_upper = by_parity(p, one[...], two[...])
    from_lower = by_parity(p, two[...], one[...])
    return own[...] + spread(from_upper, gx[0:1, :], OWN) + spread(from_lower, gx[1:2, :], OWN)


def fold_kernel(par, inner, one_in, two_in, gy, own, one, two):
    total = fold_narrow(par, inner, one_in, two_in, gy)
    own[...] = total[:, 0:OWN]
    down = total[:, OWN : OWN + GX]
    up = total[:, OWN + GX : INNER]
    p = par[0]
    one[...] = by_parity(p, up, down)
    two[...] = by_parity(p, down, up)


def force_kernel(
    par, own_in, gx1, gx2, gx, w_back, slope1, slope2, rise, geo, nbr,
    inner, one, two, table, spread_sum, pushes, grown,
):
    grad = fold_long(par, own_in, gx1, gx2, gx)
    grown[...] = jnp.dot(w_back[...], grad, precision=HIGHEST, preferred_element_type=F32) * (1.0 / math.sqrt(NEI))
    spread_sum[...] = jnp.zeros(spread_sum.shape, F32)
    pushes[...] = jnp.zeros(pushes.shape, F32)

    def turn(g, carry):
        lifted = []
        hot = []
        pushed = pushes[...]
        for j in range(FORCE_GROUP):
            n = FORCE_GROUP * g + j
            rate = jnp.concatenate(
                [
                    jnp.sum(slope[n] * grown[:, HALF * h : HALF * (h + 1)], axis=0, keepdims=True)
                    for h, slope in enumerate((slope1, slope2))
                ],
                axis=1,
            )
            twice = 2.0 * (rate + rise[pl.ds(n, 1), :])
            push = [geo[c, pl.ds(n, 1), :] * twice for c in range(3)]
            highs = [v.astype(BF16).astype(F32) for v in push]
            rows = highs + [v - h for v, h in zip(push, highs)]
            value = jnp.concatenate(rows + [jnp.zeros((2, OWN), F32)], axis=0)
            pushed = pushed + value
            index = nbr[pl.ds(n, 1), :]
            high_row = index >> 8
            hot.append(hot_rows(index & (HALF - 1)))
            lifted.append(
                jnp.concatenate([jnp.where(high_row == k, value, 0.0) for k in range(LEVELS)], axis=0).astype(BF16)
            )
        pushes[...] = pushed
        spread_sum[...] += lax.dot_general(
            jnp.concatenate(lifted, axis=1), jnp.concatenate(hot, axis=1), (((1,), (1,)), ((), ())), preferred_element_type=F32
        )
        return carry

    lax.fori_loop(0, NEI // FORCE_GROUP, turn, 0)
    table[...] = jnp.zeros(table.shape, F32)
    for k in range(LEVELS):
        width = min(HALF, EXT - HALF * k)
        table[0:3, HALF * k : HALF * k + width] = (
            spread_sum[8 * k : 8 * k + 3, :width] + spread_sum[8 * k + 3 : 8 * k + 6, :width]
        )
    table[0:3, 0:OWN] = table[0:3, 0:OWN] - pushes[0:3, :] - pushes[3:6, :]
    inner[...] = table[:, 0:INNER]
    outer_messages(par, table, one, two)


def final_kernel(par, own, one, two, gx, bundle, pos_out, vel_out, frc_out):
    forces = -fold_long(par, own, one, two, gx)[0:3, :]
    pos_out[...] = bundle[0:3, :]
    vel_out[...] = bundle[3:6, :] + (0.5 * TIME_STEP) * forces
    frc_out[...] = forces


def call(kernel, name, shapes, scratch, *operands, far=(), limit=BIG):
    specs = [pl.BlockSpec(memory_space=pltpu.HBM if k in far else pltpu.VMEM) for k in range(len(operands))]

    def placed(*refs):
        column = lax.axis_index("gy")
        kernel((lax.rem(lax.axis_index("gx"), 2), lax.rem(column, 2), column), *refs)

    return pl.pallas_call(
        placed,
        name=name,
        out_shape=[jax.ShapeDtypeStruct(shape, kind) for shape, kind in shapes],
        in_specs=specs,
        out_specs=[pl.BlockSpec(memory_space=pltpu.VMEM)] * len(shapes),
        scratch_shapes=[
            pltpu.SemaphoreType.DMA(shape) if kind is None else pltpu.VMEM(shape, kind) for shape, kind in scratch
        ],
        compiler_params=pltpu.CompilerParams(vmem_limit_bytes=limit),
    )(*operands)


def holds(*arrays):
    return [(a.shape, a.dtype) for a in arrays] + [((len(arrays),), None)]


def swap(axis, first):
    count = lax.axis_size(axis)
    offset = 0 if first else 1
    route = []
    for i in range(count):
        route.append((i, (((i + offset) ^ 1) - offset) % count))
    return route


def exchange(axis, one, two):
    two = lax.ppermute(two, axis, swap(axis, False))
    one = lax.ppermute(one, axis, swap(axis, True))
    two, one = lax.optimization_barrier((two, one))
    return one, two


def on_device(
    positions, velocities, forces, neighbours, ghost_x, ghost_y, migrate_x, migrate_y,
    w_basis, b_basis, w_embed, w_pair, w_mix, b_pair, w_out,
):
    narrow_count = lax.axis_size("gy")
    tile = ((8, LANES), F32)
    wide = ((8, OWN), F32)
    given = (positions, velocities, forces, ghost_x, ghost_y, migrate_x, migrate_y)
    record, message = call(
        start_kernel, "start", [wide, tile], holds(*given), *given,
        far=range(len(given)), limit=WHOLE,
    )
    given = (
        w_basis.T, w_pair, w_mix.T, w_embed, jnp.stack([b_basis, b_pair, w_out]),
    )
    doubled = ((2 * H, 2 * H), BF16)
    near, basis, pair_ahead, mix_ahead, pair_back, mix_back, w_ahead, w_back, columns = call(
        prepare_kernel,
        "prepare",
        [
            ((NEI, OWN), I32), ((H, 4 * NB), BF16), doubled, ((2 * H, 2 * EMB), BF16), doubled, ((2 * EMB, 2 * H), BF16),
            ((EMB, H), F32), ((H, EMB), F32), ((H, NB), F32),
        ],
        holds(*given), neighbours, *given, far=range(1, len(given) + 1),
    )
    message = lax.ppermute(message, "gx", swap("gx", True))
    mine = jnp.concatenate([record, message], axis=1)
    joined = lax.ppermute(mine, "gx", swap("gx", False))
    group = 2 * narrow_count
    own, blocks = call(cross_kernel, "cross", [wide, ((group, 8, OWN), F32)], [wide], mine, joined)
    members = [list(range(group * k, group * (k + 1))) for k in range(lax.axis_size("gx") // 2)]
    blocks = lax.all_to_all(blocks, ("gx", "gy"), 0, 0, axis_index_groups=members)

    bundle, gx, gy, embed, one, two, latent, geo, square = call(
        lambda *refs: env_kernel(narrow_count, *refs),
        "env",
        [
            wide, ((2, GX), I32), ((2, HALF), I32), ((EMB, OWN), F32), ((EMB, GX), F32), ((EMB, GX), F32),
            ((NEI, 2 * H, OWN), BF16), ((4, NEI, OWN), F32), ((NEI, OWN), F32),
        ],
        [((8, EXT), F32), ((8, INNER), F32)],
        blocks, own, near, basis, w_ahead,
    )
    (first,) = call(first_kernel, "first", [((NEI, H, OWN), F32)], [], latent, pair_ahead, columns)
    slopes = [
        call(
            lambda *refs, half=half: slope_kernel(half, *refs), f"slope{half}", [((NEI, H, HALF), F32)], [],
            square, geo, basis,
        )[0]
        for half in range(OWN // HALF)
    ]
    ex = exchange("gx", one, two)
    *ex, slopes[0] = lax.optimization_barrier((*ex, slopes[0]))
    message = ((EMB, HALF), F32)
    one, two = call(
        ghost_kernel, "ghost_embed", [message, message], [((EMB, INNER), F32)],
        embed, *ex, gy,
    )
    ey = exchange("gy", one, two)
    message = ((EMB, GY), F32)
    dvalue, part, inner, one, two = call(
        pair_kernel,
        "pair",
        [((NEI, 2 * H, OWN), BF16), ((NEI, OWN), F32), ((EMB, INNER), F32), message, message],
        [((EMB, EXT), F32), ((LEVELS * 2 * EMB, HALF), F32), ((EMB, OWN), F32)],
        embed, *ex, *ey, near, first, geo, mix_ahead, mix_back, columns,
    )
    one, two = exchange("gy", one, two)
    one, two, slopes[1] = lax.optimization_barrier((one, two, slopes[1]))
    (rise,) = call(rise_kernel, "rise", [((NEI, OWN), F32)], [], dvalue, part, *slopes, pair_back)
    message = ((EMB, GX), F32)
    own, one, two = call(
        fold_kernel, "fold_embed", [((EMB, OWN), F32), message, message], [], inner, one, two, gy
    )
    one, two = exchange("gx", one, two)
    message = ((8, GY), F32)
    inner, one, two = call(
        force_kernel,
        "force",
        [((8, INNER), F32), message, message],
        [((8, EXT), F32), ((8 * LEVELS, HALF), F32), ((8, OWN), F32), ((H, OWN), F32)],
        own, one, two, gx, w_back, *slopes, rise, geo, near,
    )
    one, two = exchange("gy", one, two)
    own, one, two = call(fold_kernel, "fold_force", [wide, tile, tile], [], inner, one, two, gy)
    one, two = exchange("gx", one, two)
    flat = ((3, OWN), F32)
    return tuple(call(final_kernel, "final", [flat, flat, flat], [], own, one, two, gx, bundle))


def solution(mesh):
    both = ("gx", "gy")
    flat = P(None, both)
    stacked = P(None, None, both)
    return jax.shard_map(
        on_device,
        mesh=mesh,
        in_specs=(flat,) * 3 + (stacked,) * 5 + (P(),) * 7,
        out_specs=(flat,) * 3,
        check_vma=False,
    )
```
